32 devices in a mesh: gx: 2 (over x), gy: 4 (over z), gz: 4 (over y, core).
Axes of the slice: x: 2, y: 2, z: 4, core: 2. Of those that a mesh axis runs over, the one named last changes fastest.
Arguments:
- features: bfloat16 [2, 4, 4, 768, 256], P('gx', 'gy', 'gz'), may hold values from -6 to 6
- weight: bfloat16 [27, 256, 256], replicated, may hold values from -0.078125 to 0.078125
- upstream: bfloat16 [2, 4, 4, 768, 256], P('gx', 'gy', 'gz'), may hold values from -6 to 6
- send_rows: int32 [2, 4, 4, 6, 96], P('gx', 'gy', 'gz'), may hold values from 0 to 767
- in_rows: int32 [2, 4, 4, 27, 768], P('gx', 'gy', 'gz'), may hold values from 0 to 1343, as said below
- out_rows: int32 [2, 4, 4, 27, 768], P('gx', 'gy', 'gz'), may hold values from 0 to 767, each once within a row
- tap_pair_exists: int32 [2, 4, 4, 27, 768], P('gx', 'gy', 'gz'), may hold values from 0 to 1, as said below
Outputs:
- activated: bfloat16 [2, 4, 4, 768, 256], P('gx', 'gy', 'gz')
- grad_features: bfloat16 [2, 4, 4, 768, 256], P('gx', 'gy', 'gz')
- grad_weight: bfloat16 [27, 256, 256], replicated
The draws below stay inside these ranges and needn't reach their ends.
Inputs may be any that keep to these rules, and one draw needn't show every extreme that they name: `in_rows`: rows below 768 are a device's own; row 768 + d * 96 + f is row f of face d of the extended rows. For each device and tap the 768 rows are distinct. `out_rows`: for each device and tap, every row appears exactly once. `tap_pair_exists`: the share of existing pairs differs from device to device and from tap to tap.
All inputs are finite; a program needn't handle non-finite values.
Results may differ from the reference program's by a relative error of at most 0.0053.
Values may be sent and summed in bfloat16 or wider, within the bound.
No kernel may reach another device: no remote copies, remote signals or barrier semaphores. Data moves between devices by JAX's collectives and lax.ppermute only.
A program may use at most 128 MiB of HBM per device.

```python
import jax
import jax.numpy as jnp
from jax import lax

C = 256
TAPS = 27
VOX = 768
FACE = 96
ROWS_EXT = 1344
N_GX = 2
N_GY = 4
N_GZ = 4


def draw_in_rows(key, part):
    devices_all = N_GX * N_GY * N_GZ
    base = jax.random.fold_in(key, 21)
    tap_keys = jax.random.split(base, devices_all * TAPS)
    picked = jax.vmap(lambda one_key: jax.random.permutation(one_key, ROWS_EXT)[:VOX])(tap_keys)
    return picked.astype(jnp.int32).reshape(N_GX, N_GY, N_GZ, TAPS, VOX)


def draw_tap_pair_exists(key, part):
    key_count = jax.random.fold_in(key, 11)
    key_order = jax.random.fold_in(key, 12)
    key_pairs = jax.random.fold_in(key, 13)
    devices_all = N_GX * N_GY * N_GZ
    live_taps = jax.random.randint(key_count, (devices_all, 1), 9, TAPS + 1)
    scores = jax.random.randint(key_order, (devices_all, TAPS), 0, 1 << 20) * TAPS + jnp.arange(TAPS, dtype=jnp.int32)[None, :]
    ranking = jnp.argsort(jnp.argsort(scores, axis=1), axis=1).astype(jnp.int32)
    tap_open = ranking < live_taps
    coins = jax.random.randint(key_pairs, (devices_all, TAPS, VOX), 0, 8)
    live = jnp.logical_and(tap_open[:, :, None], coins < 7)
    return live.astype(jnp.int32).reshape(N_GX, N_GY, N_GZ, TAPS, VOX)


def place_ends(values, stream_key, smallest, largest):
    longest = values.shape.index(max(values.shape))
    spots = []
    for shift in (0, 1):
        where = [jax.random.randint(jax.random.fold_in(stream_key, axis), (), 0, length) for axis, length in enumerate(values.shape)]
        where[longest] = (where[longest] + shift) % values.shape[longest]
        spots.append(tuple(where))
    return values.at[spots[0]].set(smallest).at[spots[1]].set(largest)


def shard_levels(stream_key, dims, cuts, smallest, top_value):
    loudness = 1.0
    for axis_at, blocks in cuts:
        heights = jax.random.uniform(jax.random.fold_in(jax.random.fold_in(stream_key, 6), axis_at), (blocks,), jnp.float32, smallest / len(cuts), top_value / len(cuts))
        loudness = loudness * jnp.repeat(jnp.exp(heights), dims[axis_at] // blocks).reshape((-1,) + (1,) * (len(dims) - 1 - axis_at))
    return loudness


def centred(rng, shape, spread, bound, cuts=(), kind=jnp.bfloat16):
    entries = jax.random.normal(rng, shape, jnp.float32) * spread
    if len(cuts) > 0:
        entries = shard_levels(rng, shape, cuts, -0.22, 0.18) * entries
    return jnp.clip(entries, min=-bound, max=bound).astype(kind)


def setup_inputs(seed: int = 0) -> dict:
    seeds = jax.random.split(jax.random.key(seed), 8)
    features = centred(seeds[0], (N_GX, N_GY, N_GZ, VOX, C), 1.0, 6.0, ((0, 2), (1, 4), (2, 4)))
    weight = centred(seeds[1], (TAPS, C, C), (TAPS * C) ** -0.5, 0.078125)
    upstream = centred(seeds[2], (N_GX, N_GY, N_GZ, VOX, C), 1.0, 6.0, ((0, 2), (1, 4), (2, 4)))
    send_rows = place_ends(jax.random.randint(seeds[3], (N_GX, N_GY, N_GZ, 6, FACE), 0, VOX), jax.random.fold_in(seeds[3], 1), 0, VOX - 1).astype(jnp.int32)
    in_rows = draw_in_rows(jax.random.fold_in(seeds[7], 71), 0)
    out_rows = jax.vmap(lambda own: jax.random.permutation(own, VOX))(jax.random.split(seeds[5], N_GX * N_GY * N_GZ * TAPS)).reshape((N_GX, N_GY, N_GZ, TAPS, VOX)).astype(jnp.int32)
    tap_pair_exists = draw_tap_pair_exists(jax.random.fold_in(seeds[7], 71), 0)
    return {"features": features, "weight": weight, "upstream": upstream, "send_rows": send_rows, "in_rows": in_rows, "out_rows": out_rows, "tap_pair_exists": tap_pair_exists}


def trade_all(stacked):
    pieces = []
    for axis_number in range(3):
        lower = stacked[..., 2 * axis_number + 1, :, :]
        upper = stacked[..., 2 * axis_number, :, :]
        lower = jnp.moveaxis(lower, axis_number, 0)
        upper = jnp.moveaxis(upper, axis_number, 0)
        blank = jnp.zeros_like(lower[:1])
        from_lower = jnp.concatenate([blank, lower[:-1]], axis=0)
        from_upper = jnp.concatenate([upper[1:], blank], axis=0)
        pieces.append(jnp.moveaxis(from_lower, 0, axis_number))
        pieces.append(jnp.moveaxis(from_upper, 0, axis_number))
    return jnp.stack(pieces, axis=3)


def shard_forward(padded_features, source_voxels, target_voxels, occupancy_flags, weight):
    own_rows = target_voxels.shape[1]
    channels = weight.shape[2]

    def advance(kernel_tap, running):
        gathered = padded_features[source_voxels[kernel_tap]]
        kernel_product = jnp.dot(gathered, weight[kernel_tap], preferred_element_type=jnp.float32)
        kernel_product = kernel_product * occupancy_flags[kernel_tap].astype(jnp.float32)[:, None]
        return running.at[target_voxels[kernel_tap]].add(kernel_product)

    return lax.fori_loop(0, TAPS, advance, jnp.zeros((own_rows, channels), jnp.float32))


def shard_backward(padded_features, source_voxels, target_voxels, occupancy_flags, weight, preactivation_gradient):
    channels = weight.shape[2]

    def advance(kernel_tap, carried):
        grad_rows, grad_kernel = carried
        gathered = padded_features[source_voxels[kernel_tap]]
        selected_entries = jnp.where(occupancy_flags[kernel_tap][:, None] > 0, preactivation_gradient[target_voxels[kernel_tap]], jnp.zeros((), jnp.bfloat16))
        back = jnp.dot(selected_entries, weight[kernel_tap].T, preferred_element_type=jnp.float32)
        grad_rows = grad_rows.at[source_voxels[kernel_tap]].add(back)
        kernel_term = jnp.dot(gathered.T, selected_entries, preferred_element_type=jnp.float32)
        grad_kernel = grad_kernel.at[kernel_tap].add(kernel_term)
        return grad_rows, grad_kernel

    start = (jnp.zeros((padded_features.shape[0], channels), jnp.float32), jnp.zeros((TAPS, channels, channels), jnp.float32))
    return lax.fori_loop(0, TAPS, advance, start)


def reference(features, weight, upstream, send_rows, in_rows, out_rows, tap_pair_exists):
    count = N_GX * N_GY * N_GZ
    channels = features.shape[-1]
    flat_features = features.reshape(count, VOX, channels)
    flat_sends = send_rows.reshape(count, 6, FACE)
    sent = jax.vmap(lambda rows, picks: rows[picks])(flat_features, flat_sends)
    incoming = trade_all(sent.reshape(N_GX, N_GY, N_GZ, 6, FACE, channels)).reshape(count, 6 * FACE, channels)
    padded_features = jnp.concatenate([flat_features, incoming], axis=1)
    flat_in = in_rows.reshape(count, TAPS, VOX)
    flat_out = out_rows.reshape(count, TAPS, VOX)
    flat_live = tap_pair_exists.reshape(count, TAPS, VOX)

    linear_response = lax.map(lambda group: shard_forward(group[0], group[1], group[2], group[3], weight), (padded_features, flat_in, flat_out, flat_live))
    sigmoid = jax.nn.sigmoid(linear_response)
    activated = (linear_response * sigmoid).astype(jnp.bfloat16)
    derivative = sigmoid * (1.0 + linear_response * (1.0 - sigmoid))
    preactivation_gradient = (upstream.reshape(count, VOX, channels).astype(jnp.float32) * derivative).astype(jnp.bfloat16)

    def scan_device(kernel_sum, group):
        grad_rows, grad_kernel = shard_backward(group[0], group[1], group[2], group[3], weight, group[4])
        return kernel_sum + grad_kernel, grad_rows

    kernel_sum, grad_extended = lax.scan(scan_device, jnp.zeros((TAPS, channels, channels), jnp.float32), (padded_features, flat_in, flat_out, flat_live, preactivation_gradient))
    grad_weight = (kernel_sum * (float(count * VOX) ** -0.5)).astype(jnp.bfloat16)

    returned_faces = grad_extended[:, VOX:].astype(jnp.bfloat16).reshape(N_GX, N_GY, N_GZ, 6, FACE, channels)
    returned = trade_all(returned_faces).reshape(count, 6 * FACE, channels)
    grad_features = jax.vmap(lambda own, picks, back: own.at[picks].add(back.astype(jnp.float32)))(grad_extended[:, :VOX], flat_sends.reshape(count, 6 * FACE), returned)
    shape = (N_GX, N_GY, N_GZ, VOX, channels)
    return activated.reshape(shape), grad_features.astype(jnp.bfloat16).reshape(shape), grad_weight
```

```python
import jax
import jax.numpy as jnp
from jax import lax
from jax.experimental import pallas as pl
from jax.experimental.pallas import tpu as pltpu
from jax.sharding import PartitionSpec as P

BF = jnp.bfloat16
F32 = jnp.float32
NT = (((1,), (1,)), ((), ()))
NN = (((1,), (0,)), ((), ()))
TN = (((0,), (0,)), ((), ()))
LIMIT = 56 << 20
AXES = ("gx", "gy", "gz")


def dot(a, b, dims=NN):
    return lax.dot_general(a, b, dims, preferred_element_type=F32)


def one_hot(mask):
    return jnp.where(mask, jnp.ones((), F32), jnp.zeros((), F32)).astype(BF)


def whole(shape):
    return pl.BlockSpec(shape, lambda k: (0,) * len(shape))


def send_kernel(rows_ref, own_ref, sent_ref):
    directions, face = rows_ref.shape
    own = own_ref.shape[0]
    places = lax.broadcasted_iota(jnp.int32, (own, face), 0)
    for d in range(directions):
        hot = one_hot(places == rows_ref[d : d + 1, :])
        sent_ref[d] = dot(hot, own_ref[...], TN).astype(BF)


def send(rows, own_features):
    directions, face = rows.shape
    return pl.pallas_call(
        send_kernel,
        out_shape=jax.ShapeDtypeStruct((directions, face, own_features.shape[1]), BF),
        compiler_params=pltpu.CompilerParams(vmem_limit_bytes=LIMIT),
        name="send",
    )(rows, own_features)


def invert_kernel(block, missing, in_ref, out_ref, live_ref, col_ref, row_ref):
    taps, own = in_ref.shape
    lows = lax.broadcasted_iota(jnp.int32, (block, own), 0)
    ranks = lax.broadcasted_iota(jnp.int32, (8, own), 0)
    for k in range(taps):
        target = out_ref[pl.ds(k, 1), :]
        source = jnp.where(live_ref[pl.ds(k, 1), :] > 0, in_ref[pl.ds(k, 1), :], missing)
        high = target // block
        hot = one_hot(lows == target - high * block)
        big = (source // 16) * 16
        spread = jnp.where(ranks == high, big, jnp.where(ranks - 4 == high, source - big, 0))
        spread = spread.astype(F32).astype(BF)
        col_ref[k] = dot(hot, spread, NT)
        row_ref[k] = dot(spread, hot, NT)


def invert(in_rows, out_rows, live, missing, block):
    taps, own = in_rows.shape
    return pl.pallas_call(
        lambda *refs: invert_kernel(block, missing, *refs),
        out_shape=(
            jax.ShapeDtypeStruct((taps, block, 8), F32),
            jax.ShapeDtypeStruct((taps, 8, block), F32),
        ),
        compiler_params=pltpu.CompilerParams(vmem_limit_bytes=LIMIT),
        name="invert",
    )(in_rows, out_rows, live)


def forward_kernel(
    taps, block, parts, odd_ref, col_ref, own_ref, face_ref, w_ref, up_ref,
    act_ref, gp_ref, keep_ref, give_ref, ext, acc, gt, turned,
):
    k = pl.program_id(0)
    own, ch = own_ref.shape
    rows = ext.shape[0]
    half = ch // 2

    @pl.when(k == 0)
    def _():
        ext[pl.ds(0, own), :] = own_ref[...]
        ext[pl.ds(own, rows - own), :] = face_ref[...]
        acc[...] = jnp.zeros_like(acc)

    lanes = lax.broadcasted_iota(jnp.int32, (block, rows), 1)
    for h in range(parts):
        place = (col_ref[0, :, h : h + 1] + col_ref[0, :, h + 4 : h + 5]).astype(jnp.int32)
        got = dot(one_hot(lanes == place), ext[...]).astype(BF)
        gt[pl.ds(pl.multiple_of(k * ch, ch), ch), pl.ds(h * block, block)] = got.T
        acc[pl.ds(h * block, block), :] += dot(got, w_ref[0])

    @pl.when(k == taps - 1)
    def _():
        v = acc[...]
        s = jax.nn.sigmoid(v)
        act_ref[...] = (v * s).astype(BF)
        g = up_ref[...].astype(F32) * (s * (1.0 + v * (1.0 - s)))
        gp_ref[...] = g.astype(BF)
        first = jnp.where(odd_ref[0] > 0, g[:, half:], g[:, :half])
        second = jnp.where(odd_ref[0] > 0, g[:, :half], g[:, half:])
        turned[:, :half] = first.astype(BF)
        turned[:, half:] = second.astype(BF)

        def one(t, carried):
            at = pl.multiple_of(t * ch, ch)
            r = dot(gt[pl.ds(at, ch), :], turned[...]).astype(BF)
            keep_ref[pl.ds(at, ch), :] = r[:, :half]
            give_ref[pl.ds(at, ch), :] = r[:, half:]
            return carried

        lax.fori_loop(0, taps, one, 0, unroll=3)


def forward(odd, col, own_features, faces, weight, upstream):
    taps, block, _ = col.shape
    own, ch = own_features.shape
    rows = own + faces.shape[0]
    like = jax.ShapeDtypeStruct
    return pl.pallas_call(
        lambda *refs: forward_kernel(taps, block, own // block, *refs),
        grid=(taps,),
        in_specs=[
            pl.BlockSpec(memory_space=pltpu.SMEM),
            pl.BlockSpec((1, block, 8), lambda k: (k, 0, 0)),
            whole((own, ch)),
            whole(faces.shape),
            pl.BlockSpec((1, ch, ch), lambda k: (k, 0, 0)),
            whole((own, ch)),
        ],
        out_specs=[whole((own, ch)), whole((own, ch)), whole((taps * ch, ch // 2)), whole((taps * ch, ch // 2))],
        out_shape=[
            like((own, ch), BF),
            like((own, ch), BF),
            like((taps * ch, ch // 2), BF),
            like((taps * ch, ch // 2), BF),
        ],
        scratch_shapes=[
            pltpu.VMEM((rows, ch), BF),
            pltpu.VMEM((own, ch), F32),
            pltpu.VMEM((taps * ch, own), BF),
            pltpu.VMEM((own, ch), BF),
        ],
        compiler_params=pltpu.CompilerParams(vmem_limit_bytes=LIMIT),
        name="forward",
    )(odd, col, own_features, faces, weight, upstream)


def backward_kernel(parts, step, row_ref, gp_ref, w_ref, *rest):
    out_ref = rest[-1]
    k = pl.program_id(0)
    rows = out_ref.shape[0]
    block = row_ref.shape[2]

    @pl.when(k == 0)
    def _():
        out_ref[...] = rest[0][...] if len(rest) > 1 else jnp.zeros_like(out_ref)

    for r in range(0, rows, step):
        size = min(step, rows - r)
        lines = lax.broadcasted_iota(jnp.int32, (size, block), 0) + r
        hots = []
        for h in range(parts):
            place = (row_ref[0, h : h + 1, :] + row_ref[0, h + 4 : h + 5, :]).astype(jnp.int32)
            hots.append(one_hot(lines == place))
        got = dot(jnp.concatenate(hots, axis=1), gp_ref[...]).astype(BF)
        out_ref[pl.ds(r, size), :] += dot(got, w_ref[0], NT)


def backward(row, gp, weight, first, count, before, rows):
    block = row.shape[2]
    own, ch = gp.shape
    specs = [
        pl.BlockSpec((1, 8, block), lambda k: (k + first, 0, 0)),
        whole((own, ch)),
        pl.BlockSpec((1, ch, ch), lambda k: (k + first, 0, 0)),
    ]
    args = [row, gp, weight]
    if before is not None:
        specs.append(whole((rows, ch)))
        args.append(before)
    return pl.pallas_call(
        lambda *refs: backward_kernel(own // block, 448, *refs),
        grid=(count,),
        in_specs=specs,
        out_specs=whole((rows, ch)),
        out_shape=jax.ShapeDtypeStruct((rows, ch), F32),
        compiler_params=pltpu.CompilerParams(vmem_limit_bytes=LIMIT),
        name="backward",
    )(*args)


def finish_kernel(rows_ref, grad_ref, back_ref, out_ref):
    directions, face = rows_ref.shape
    own = out_ref.shape[0]
    places = lax.broadcasted_iota(jnp.int32, (own, face), 0)
    total = grad_ref[...]
    for d in range(directions):
        hot = one_hot(places == rows_ref[d : d + 1, :])
        total = total + dot(hot, back_ref[d])
    out_ref[...] = total.astype(BF)


def finish(rows, grad_extended, returned, own):
    ch = grad_extended.shape[1]
    return pl.pallas_call(
        finish_kernel,
        grid=(1,),
        in_specs=[whole(rows.shape), whole((own, ch)), whole(returned.shape)],
        out_specs=whole((own, ch)),
        out_shape=jax.ShapeDtypeStruct((own, ch), BF),
        compiler_params=pltpu.CompilerParams(vmem_limit_bytes=LIMIT),
        name="finish",
    )(rows, grad_extended, returned)


def trade(faces):
    got = [None] * 6
    for i, axis in enumerate(AXES):
        lower, upper = 2 * i, 2 * i + 1
        n = lax.axis_size(axis)
        if n == 2:
            last = lax.axis_index(axis) == 1
            moved = lax.ppermute(jnp.where(last, faces[lower], faces[upper]), axis, [(0, 1), (1, 0)])
            blank = jnp.zeros_like(moved)
            got[lower] = jnp.where(last, moved, blank)
            got[upper] = jnp.where(last, blank, moved)
        else:
            got[lower] = lax.ppermute(faces[upper], axis, [(j, j + 1) for j in range(n - 1)])
            got[upper] = lax.ppermute(faces[lower], axis, [(j + 1, j) for j in range(n - 1)])
    return jnp.stack(got)


def add(a, b):
    return (a.astype(F32) + b.astype(F32)).astype(BF)


def swap(x, axis, bit):
    n = lax.axis_size(axis)
    return lax.ppermute(x, axis, [(j, j ^ (1 << bit)) for j in range(n)])


def side(axis, bit):
    return (lax.axis_index(axis) >> bit) & 1


def cut(x, which):
    half = x.shape[0] // 2
    return lax.dynamic_slice_in_dim(x, which * half, half, 0)


def join(mine, other, which):
    half = mine.shape[0]
    out = jnp.zeros((2 * half,) + mine.shape[1:], mine.dtype)
    out = lax.dynamic_update_slice_in_dim(out, mine, which * half, 0)
    return lax.dynamic_update_slice_in_dim(out, other, (1 - which) * half, 0)


def reduce_all(keep, give, scaling):
    bits = lambda axis, low: [(axis, b) for b in range(low, lax.axis_size(axis).bit_length() - 1)]
    plane = [bits("gx", 0) + bits("gz", 1), bits("gz", 1) + bits("gx", 0)]
    x = add(keep, swap(give, "gz", 0))
    rows, ch = x.shape
    pieces = [x[: rows // 2], x[rows // 2 :]]
    for turn in range(len(plane[0])):
        for i in range(2):
            axis, bit = plane[i][turn]
            mine = side(axis, bit)
            pieces[i] = add(cut(pieces[i], mine), swap(cut(pieces[i], 1 - mine), axis, bit))
    n = lax.axis_size("gy")
    at = lax.axis_index("gy")
    joint = jnp.concatenate([p.reshape(n, -1, ch) for p in pieces], axis=1)
    slot = lambda s: lax.dynamic_index_in_dim(joint, (at + s) % n, 0, keepdims=False)
    turn_by = lambda y, s: lax.ppermute(y, "gy", [(j, (j + s) % n) for j in range(n)])
    total = slot(0).astype(F32)
    for s in range(1, n):
        total = total + turn_by(slot(s), s).astype(F32)
    mine = (total * scaling).astype(BF)
    full = jnp.zeros_like(joint)
    full = lax.dynamic_update_index_in_dim(full, mine, at, 0)
    for s in range(1, n):
        full = lax.dynamic_update_index_in_dim(full, turn_by(mine, s), (at - s) % n, 0)
    size = full.shape[1] // 2
    pieces = [full[:, :size].reshape(-1, ch), full[:, size:].reshape(-1, ch)]
    for turn in reversed(range(len(plane[0]))):
        for i in range(2):
            axis, bit = plane[i][turn]
            pieces[i] = join(pieces[i], swap(pieces[i], axis, bit), side(axis, bit))
    mine = jnp.concatenate(pieces, axis=0)
    other = swap(mine, "gz", 0)
    odd = side("gz", 0) == 1
    return jnp.concatenate([jnp.where(odd, other, mine), jnp.where(odd, mine, other)], axis=1)


def shards(features, weight, upstream, send_rows, in_rows, out_rows, tap_pair_exists):
    own_features = features[0, 0, 0]
    own, ch = own_features.shape
    sends = send_rows[0, 0, 0]
    taps = weight.shape[0]
    block = 256
    sent = send(sends, own_features)
    faces = trade([sent[d] for d in range(6)]).reshape(-1, ch)
    rows = own + faces.shape[0]
    col, row = invert(in_rows[0, 0, 0], out_rows[0, 0, 0], tap_pair_exists[0, 0, 0], 2000, block)
    odd = side("gz", 0).reshape(1)
    activated, gp, keep, give = forward(odd, col, own_features, faces, weight, upstream[0, 0, 0])
    devices = lax.axis_size("gx") * lax.axis_size("gy") * lax.axis_size("gz")
    grad_weight = reduce_all(keep, give, float(devices * own) ** -0.5).reshape(weight.shape)
    grad = None
    for first in range(0, taps, 9):
        grad = backward(row, gp, weight, first, 9, grad, rows)
    back = grad[own:].astype(BF).reshape(6, -1, ch)
    returned = trade([back[d] for d in range(6)])
    grad_features = finish(sends, grad, returned, own)
    return activated[None, None, None], grad_features[None, None, None], grad_weight


def solution(mesh):
    part = P("gx", "gy", "gz", None, None)
    return jax.shard_map(
        shards,
        mesh=mesh,
        in_specs=(part, P(), part, part, part, part, part),
        out_specs=(part, part, P()),
        check_vma=False,
    )
```

```python
import jax
import jax.numpy as jnp
from jax import lax
from jax.experimental import pallas as pl
from jax.experimental.pallas import tpu as pltpu
from jax.sharding import PartitionSpec as P

BF = jnp.bfloat16
F32 = jnp.float32
NT = (((1,), (1,)), ((), ()))
NN = (((1,), (0,)), ((), ()))
TN = (((0,), (0,)), ((), ()))
LIMIT = 24 << 20
AXES = ("gx", "gy", "gz")


def dot(a, b, dims=NN):
    return lax.dot_general(a, b, dims, preferred_element_type=F32)


def one_hot(mask):
    return jnp.where(mask, jnp.ones((), F32), jnp.zeros((), F32)).astype(BF)


def whole(shape):
    return pl.BlockSpec(shape, lambda k: (0,) * len(shape))


def send_kernel(rows_ref, own_ref, sent_ref):
    directions, face = rows_ref.shape
    own = own_ref.shape[0]
    places = lax.broadcasted_iota(jnp.int32, (own, face), 0)
    for d in range(directions):
        hot = one_hot(places == rows_ref[d : d + 1, :])
        sent_ref[d] = dot(hot, own_ref[...], TN).astype(BF)


def send(rows, own_features):
    directions, face = rows.shape
    return pl.pallas_call(
        send_kernel,
        out_shape=jax.ShapeDtypeStruct((directions, face, own_features.shape[1]), BF),
        compiler_params=pltpu.CompilerParams(vmem_limit_bytes=LIMIT),
        name="send",
    )(rows, own_features)


def invert_kernel(block, missing, in_ref, out_ref, live_ref, col_ref, row_ref):
    taps, own = in_ref.shape
    lows = lax.broadcasted_iota(jnp.int32, (block, own), 0)
    ranks = lax.broadcasted_iota(jnp.int32, (8, own), 0)
    for k in range(taps):
        target = out_ref[pl.ds(k, 1), :]
        source = jnp.where(live_ref[pl.ds(k, 1), :] > 0, in_ref[pl.ds(k, 1), :], missing)
        high = target // block
        hot = one_hot(lows == target - high * block)
        big = (source // 16) * 16
        spread = jnp.where(ranks == high, big, jnp.where(ranks - 4 == high, source - big, 0))
        spread = spread.astype(F32).astype(BF)
        col_ref[k] = dot(hot, spread, NT)
        row_ref[k] = dot(spread, hot, NT)


def invert(in_rows, out_rows, live, missing, block):
    taps, own = in_rows.shape
    return pl.pallas_call(
        lambda *refs: invert_kernel(block, missing, *refs),
        out_shape=(
            jax.ShapeDtypeStruct((taps, block, 8), F32),
            jax.ShapeDtypeStruct((taps, 8, block), F32),
        ),
        compiler_params=pltpu.CompilerParams(vmem_limit_bytes=LIMIT),
        name="invert",
    )(in_rows, out_rows, live)


def forward_kernel(
    block, parts, odd_ref, col_ref, own_ref, face_ref, w_hbm, up_ref,
    act_ref, gp_ref, keep_ref, give_ref, ext, got, turned_got, weights, turned, sem,
):
    taps = col_ref.shape[0]
    own, ch = own_ref.shape
    rows = ext.shape[0]
    half = ch // 2
    fetch = pltpu.make_async_copy(w_hbm, weights, sem)
    fetch.start()
    ext[pl.ds(0, own), :] = own_ref[...]
    ext[pl.ds(own, rows - own), :] = face_ref[...]
    lanes = lax.broadcasted_iota(jnp.int32, (block, rows), 1)

    def gather(k, carried):
        at = pl.multiple_of(k * ch, ch)
        for h in range(parts):
            place = (col_ref[k, :, h : h + 1] + col_ref[k, :, h + 4 : h + 5]).astype(jnp.int32)
            picked = dot(one_hot(lanes == place), ext[...]).astype(BF)
            got[pl.ds(h * block, block), pl.ds(at, ch)] = picked
            turned_got[pl.ds(at, ch), pl.ds(h * block, block)] = picked.T
        return carried

    lax.fori_loop(0, taps, gather, 0, unroll=9)
    fetch.wait()
    for h in range(parts):
        part = pl.ds(h * block, block)
        v = dot(got[part, :], weights[...])
        s = jax.nn.sigmoid(v)
        act_ref[part, :] = (v * s).astype(BF)
        g = up_ref[part, :].astype(F32) * (s * (1.0 + v * (1.0 - s)))
        gp_ref[part, :] = g.astype(BF)
        turned[part, :half] = jnp.where(odd_ref[0] > 0, g[:, half:], g[:, :half]).astype(BF)
        turned[part, half:] = jnp.where(odd_ref[0] > 0, g[:, :half], g[:, half:]).astype(BF)

    def one(t, carried):
        at = pl.multiple_of(t * ch, ch)
        r = dot(turned_got[pl.ds(at, ch), :], turned[...])
        keep_ref[pl.ds(at, ch), :] = r[:, :half]
        give_ref[pl.ds(at, ch), :] = r[:, half:].astype(BF)
        return carried

    lax.fori_loop(0, taps, one, 0, unroll=3)


def forward(odd, col, own_features, faces, weight, upstream):
    taps, block, _ = col.shape
    own, ch = own_features.shape
    rows = own + faces.shape[0]
    like = jax.ShapeDtypeStruct
    vmem = pl.BlockSpec(memory_space=pltpu.VMEM)
    return pl.pallas_call(
        lambda *refs: forward_kernel(block, own // block, *refs),
        in_specs=[
            pl.BlockSpec(memory_space=pltpu.SMEM),
            vmem,
            vmem,
            vmem,
            pl.BlockSpec(memory_space=pl.ANY),
            vmem,
        ],
        out_specs=[vmem, vmem, vmem, vmem],
        out_shape=[
            like((own, ch), BF),
            like((own, ch), BF),
            like((taps * ch, ch // 2), F32),
            like((taps * ch, ch // 2), BF),
        ],
        scratch_shapes=[
            pltpu.VMEM((rows, ch), BF),
            pltpu.VMEM((own, taps * ch), BF),
            pltpu.VMEM((taps * ch, own), BF),
            pltpu.VMEM((taps * ch, ch), BF),
            pltpu.VMEM((own, ch), BF),
            pltpu.SemaphoreType.DMA,
        ],
        compiler_params=pltpu.CompilerParams(vmem_limit_bytes=44 << 20),
        name="forward",
    )(odd, col, own_features, faces, weight.reshape(taps * ch, ch), upstream)


def backward_kernel(first, count, row_ref, gp_ref, w_hbm, *rest):
    before = rest[:-4]
    out_ref, got, weights, sems = rest[-4:]
    rows, ch = out_ref.shape
    block = row_ref.shape[2]
    parts = gp_ref.shape[0] // block
    step = 336
    fetches = [
        pltpu.make_async_copy(w_hbm.at[first + j], weights.at[:, pl.ds(j * ch, ch)], sems.at[j])
        for j in range(count)
    ]
    for fetch in fetches:
        fetch.start()

    def gather(j, carried):
        at = pl.multiple_of(j * ch, ch)
        for r in range(0, rows, step):
            lines = lax.broadcasted_iota(jnp.int32, (step, block), 0) + r
            hots = []
            for h in range(parts):
                k = first + j
                place = (row_ref[k, h : h + 1, :] + row_ref[k, h + 4 : h + 5, :]).astype(jnp.int32)
                hots.append(one_hot(lines == place))
            got[pl.ds(r, step), pl.ds(at, ch)] = dot(jnp.concatenate(hots, axis=1), gp_ref[...]).astype(BF)
        return carried

    lax.fori_loop(0, count, gather, 0, unroll=3)
    for fetch in fetches:
        fetch.wait()
    for r in range(0, rows, step):
        total = dot(got[pl.ds(r, step), :], weights[...], NT)
        if before:
            total = total + before[0][pl.ds(r, step), :]
        out_ref[pl.ds(r, step), :] = total


def backward(row, gp, weight, first, count, before, rows):
    own, ch = gp.shape
    vmem = pl.BlockSpec(memory_space=pltpu.VMEM)
    specs = [vmem, vmem, pl.BlockSpec(memory_space=pl.ANY)]
    args = [row, gp, weight]
    if before is not None:
        specs.append(vmem)
        args.append(before)
    return pl.pallas_call(
        lambda *refs: backward_kernel(first, count, *refs),
        in_specs=specs,
        out_specs=vmem,
        out_shape=jax.ShapeDtypeStruct((rows, ch), F32),
        scratch_shapes=[
            pltpu.VMEM((rows, count * ch), BF),
            pltpu.VMEM((ch, count * ch), BF),
            pltpu.SemaphoreType.DMA((count,)),
        ],
        compiler_params=pltpu.CompilerParams(vmem_limit_bytes=24 << 20),
        name="backward",
    )(*args)


def finish_kernel(rows_ref, grad_ref, back_ref, out_ref):
    directions, face = rows_ref.shape
    own = out_ref.shape[0]
    places = lax.broadcasted_iota(jnp.int32, (own, face), 0)
    total = grad_ref[...]
    for d in range(directions):
        hot = one_hot(places == rows_ref[d : d + 1, :])
        total = total + dot(hot, back_ref[d])
    out_ref[...] = total.astype(BF)


def finish(rows, grad_extended, returned, own):
    ch = grad_extended.shape[1]
    return pl.pallas_call(
        finish_kernel,
        grid=(1,),
        in_specs=[whole(rows.shape), whole((own, ch)), whole(returned.shape)],
        out_specs=whole((own, ch)),
        out_shape=jax.ShapeDtypeStruct((own, ch), BF),
        compiler_params=pltpu.CompilerParams(vmem_limit_bytes=LIMIT),
        name="finish",
    )(rows, grad_extended, returned)


def trade(faces):
    got = [None] * 6
    for i, axis in enumerate(AXES):
        lower, upper = 2 * i, 2 * i + 1
        n = lax.axis_size(axis)
        if n == 2:
            last = lax.axis_index(axis) == 1
            moved = lax.ppermute(jnp.where(last, faces[lower], faces[upper]), axis, [(0, 1), (1, 0)])
            blank = jnp.zeros_like(moved)
            got[lower] = jnp.where(last, moved, blank)
            got[upper] = jnp.where(last, blank, moved)
        else:
            got[lower] = lax.ppermute(faces[upper], axis, [(j, j + 1) for j in range(n - 1)])
            got[upper] = lax.ppermute(faces[lower], axis, [(j + 1, j) for j in range(n - 1)])
    return jnp.stack(got)


def swap(x, axis, bit):
    n = lax.axis_size(axis)
    return lax.ppermute(x, axis, [(j, j ^ (1 << bit)) for j in range(n)])


def side(axis, bit):
    return (lax.axis_index(axis) >> bit) & 1


def cut(pair, which, size):
    kept, came = (lax.dynamic_slice_in_dim(x, which * size, size, 0) for x in pair)
    return kept + came.astype(F32)


def join(mine, other, which):
    half = mine.shape[0]
    out = jnp.zeros((2 * half,) + mine.shape[1:], mine.dtype)
    out = lax.dynamic_update_slice_in_dim(out, mine, which * half, 0)
    return lax.dynamic_update_slice_in_dim(out, other, (1 - which) * half, 0)


def reduce_all(keep, give, scaling, beside):
    bits = lambda axis, low: [(axis, b) for b in range(low, lax.axis_size(axis).bit_length() - 1)]
    plane = [bits("gx", 0) + bits("gz", 1), bits("gz", 1) + bits("gx", 0)]
    turns = len(plane[0])
    came = swap(give, "gz", 0)
    rows, ch = keep.shape
    pairs = [(keep[: rows // 2], came[: rows // 2]), (keep[rows // 2 :], came[rows // 2 :])]
    for turn in range(turns):
        where = [(axis, bit, side(axis, bit)) for axis, bit in (plane[i][turn] for i in range(2))]
        size = pairs[0][0].shape[0] // 2
        out = [cut(pairs[i], 1 - where[i][2], size).astype(BF) for i in range(2)]
        came = [swap(out[i], *where[i][:2]) for i in range(2)]
        came = beside(out, came)
        pairs = [(cut(pairs[i], where[i][2], size), came[i]) for i in range(2)]
    n = lax.axis_size("gy")
    at = lax.axis_index("gy")
    size = pairs[0][0].shape[0] // n
    slot = lambda s: jnp.concatenate([cut(p, (at + s) % n, size) for p in pairs], axis=0)
    turn_by = lambda y, s: lax.ppermute(y, "gy", [(j, (j + s) % n) for j in range(n)])
    out = [slot(s).astype(BF) for s in range(1, n)]
    came = beside(out, [turn_by(y, s + 1) for s, y in enumerate(out)])
    total = slot(0)
    for y in came:
        total = total + y.astype(F32)
    mine = (total * scaling).astype(BF)
    came = beside([mine], [turn_by(mine, s) for s in range(1, n)])
    full = jnp.zeros((n, 2 * size, ch), BF)
    full = lax.dynamic_update_index_in_dim(full, mine, at, 0)
    for s, y in enumerate(came):
        full = lax.dynamic_update_index_in_dim(full, y, (at - s - 1) % n, 0)
    pieces = [full[:, :size].reshape(-1, ch), full[:, size:].reshape(-1, ch)]
    for turn in reversed(range(turns)):
        came = beside(pieces, [swap(pieces[i], *plane[i][turn]) for i in range(2)])
        pieces = [join(pieces[i], came[i], side(*plane[i][turn])) for i in range(2)]
    mine = jnp.concatenate(pieces, axis=0)
    other = swap(mine, "gz", 0)
    odd = side("gz", 0) == 1
    return jnp.concatenate([jnp.where(odd, other, mine), jnp.where(odd, mine, other)], axis=1)


def shards(features, weight, upstream, send_rows, in_rows, out_rows, tap_pair_exists):
    own_features = features[0, 0, 0]
    own, ch = own_features.shape
    sends = send_rows[0, 0, 0]
    taps = weight.shape[0]
    block = 256
    sent = send(sends, own_features)
    faces = trade([sent[d] for d in range(6)]).reshape(-1, ch)
    rows = own + faces.shape[0]
    col, row = invert(in_rows[0, 0, 0], out_rows[0, 0, 0], tap_pair_exists[0, 0, 0], 2000, block)
    odd = side("gz", 0).reshape(1)
    activated, gp, keep, give = forward(odd, col, own_features, faces, weight, upstream[0, 0, 0])
    devices = lax.axis_size("gx") * lax.axis_size("gy") * lax.axis_size("gz")
    steps = [(0, 9), (9, 6), (15, 6), (21, taps - 21)]
    state = {"turn": 0, "grad": None, "returned": None}

    def beside(out, came):
        turn = state["turn"]
        state["turn"] = turn + 1
        if turn < len(steps):
            held = lax.optimization_barrier((gp, *out))
            grad = backward(row, held[0], weight, *steps[turn], state["grad"], rows)
            held = lax.optimization_barrier((grad, *came))
            state["grad"] = held[0]
            return list(held[1:])
        if turn == len(steps):
            back = state["grad"][own:].astype(BF).reshape(6, -1, ch)
            held = lax.optimization_barrier((back, *out))
            state["returned"] = trade([held[0][d] for d in range(6)])
            held = lax.optimization_barrier((state["returned"], *came))
            state["returned"] = held[0]
            return list(held[1:])
        return came

    grad_weight = reduce_all(keep, give, float(devices * own) ** -0.5, beside).reshape(weight.shape)
    grad_features = finish(sends, state["grad"], state["returned"], own)
    return activated[None, None, None], grad_features[None, None, None], grad_weight


def solution(mesh):
    part = P("gx", "gy", "gz", None, None)
    return jax.shard_map(
        shards,
        mesh=mesh,
        in_specs=(part, P(), part, part, part, part, part),
        out_specs=(part, part, P()),
        check_vma=False,
    )
```

```python
import jax
import jax.numpy as jnp
from jax import lax
from jax.experimental import pallas as pl
from jax.experimental.pallas import tpu as pltpu
from jax.sharding import PartitionSpec as P

BF = jnp.bfloat16
F32 = jnp.float32
NT = (((1,), (1,)), ((), ()))
NN = (((1,), (0,)), ((), ()))
TN = (((0,), (0,)), ((), ()))
AXES = ("gx", "gy", "gz")
MISSING = 2000
VMEM = pl.BlockSpec(memory_space=pltpu.VMEM)
SMEM = pl.BlockSpec(memory_space=pltpu.SMEM)
ANY = pl.BlockSpec(memory_space=pl.ANY)
HBM = pl.BlockSpec(memory_space=pltpu.HBM)


def dot(a, b, dims=NN):
    return lax.dot_general(a, b, dims, preferred_element_type=F32)


def one_hot(mask):
    return jnp.where(mask, jnp.ones((), F32), jnp.zeros((), F32)).astype(BF)


def hold(x):
    return pltpu.with_memory_space_constraint(x, pltpu.HBM)


def params(megabytes):
    return pltpu.CompilerParams(vmem_limit_bytes=megabytes << 20)


def routes():
    out = []
    for i, axis in enumerate(AXES):
        if lax.axis_size(axis) == 2:
            out.append(("pair", i))
        else:
            out.extend([("up", i), ("down", i)])
    return out


def exchange(arrays, ways):
    got = []
    for array, (kind, i) in zip(arrays, ways):
        n = lax.axis_size(AXES[i])
        if kind == "pair":
            pairs = [(0, 1), (1, 0)]
        elif kind == "up":
            pairs = [(j, j + 1) for j in range(n - 1)]
        else:
            pairs = [(j + 1, j) for j in range(n - 1)]
        got.append(lax.ppermute(array, AXES[i], pairs))
    return got


def send_kernel(ways, flags, rows_ref, own_ref, *outs):
    face = rows_ref.shape[1]
    own = own_ref.shape[0]
    places = lax.broadcasted_iota(jnp.int32, (own, face), 0)
    for out, (kind, i) in zip(outs, ways):
        lower, upper = rows_ref[2 * i : 2 * i + 1, :], rows_ref[2 * i + 1 : 2 * i + 2, :]
        if kind == "pair":
            rows = jnp.where(flags[1 + i] > 0, lower, upper)
        else:
            rows = upper if kind == "up" else lower
        out[...] = dot(one_hot(places == rows), own_ref[...], TN).astype(BF)


def send(ways, flags, rows, own_features):
    shape = jax.ShapeDtypeStruct((rows.shape[1], own_features.shape[1]), BF)
    return pl.pallas_call(
        lambda *refs: send_kernel(ways, *refs),
        in_specs=[SMEM, VMEM, VMEM],
        out_specs=[VMEM] * len(ways),
        out_shape=[shape] * len(ways),
        compiler_params=params(8),
        name="send",
    )(flags, rows, own_features)


def invert_kernel(block, in_hbm, out_hbm, live_hbm, col_ref, row_hbm, tables, row_ref, sems):
    copies = [
        pltpu.make_async_copy(hbm, tables.at[j], sems.at[j])
        for j, hbm in enumerate((in_hbm, out_hbm, live_hbm))
    ]
    for copy in copies:
        copy.start()
    taps, own = in_hbm.shape
    lows = lax.broadcasted_iota(jnp.int32, (block, own), 0)
    ranks = lax.broadcasted_iota(jnp.int32, (8, own), 0)
    for copy in copies:
        copy.wait()
    for k in range(taps):
        target = tables[1, pl.ds(k, 1), :]
        source = jnp.where(tables[2, pl.ds(k, 1), :] > 0, tables[0, pl.ds(k, 1), :], MISSING)
        high = target // block
        hot = one_hot(lows == target - high * block)
        big = (source // 16) * 16
        spread = jnp.where(ranks == high, big, jnp.where(ranks - 4 == high, source - big, 0))
        spread = spread.astype(F32).astype(BF)
        col_ref[k] = dot(hot, spread, NT)
        row_ref[k] = dot(spread, hot, NT)
    copy = pltpu.make_async_copy(row_ref, row_hbm, sems.at[3])
    copy.start()
    copy.wait()


def invert(in_rows, out_rows, live, block):
    taps, own = in_rows.shape
    return pl.pallas_call(
        lambda *refs: invert_kernel(block, *refs),
        in_specs=[HBM, HBM, HBM],
        out_specs=[VMEM, HBM],
        out_shape=(
            jax.ShapeDtypeStruct((taps, block, 8), F32),
            pltpu.HBM((taps, 8, block), F32),
        ),
        scratch_shapes=[
            pltpu.VMEM((3, taps, own), jnp.int32),
            pltpu.VMEM((taps, 8, block), F32),
            pltpu.SemaphoreType.DMA((4,)),
        ],
        compiler_params=params(12),
        name="invert",
    )(hold(in_rows), hold(out_rows), hold(live))


def forward_kernel(ways, block, flags, col_ref, own_hbm, w_hbm, up_hbm, *rest):
    faces = rest[: len(ways)]
    act_hbm, gp_hbm, keep_hbm, give_hbm = rest[len(ways) : len(ways) + 4]
    ext, got, got_t, weights, turned, up, act, gp, keep, give, sems = rest[len(ways) + 4 :]
    taps = col_ref.shape[0]
    own, ch = up.shape
    rows = ext.shape[0]
    half = ch // 2
    parts = own // block
    w_copy = pltpu.make_async_copy(w_hbm, weights, sems.at[0])
    up_copy = pltpu.make_async_copy(up_hbm, up, sems.at[1])
    own_copy = pltpu.make_async_copy(own_hbm, ext.at[pl.ds(0, own), :], sems.at[2])
    own_copy.start()
    w_copy.start()
    up_copy.start()
    face = faces[0].shape[0]
    for came, (kind, i) in zip(faces, ways):
        low, high = own + 2 * i * face, own + (2 * i + 1) * face
        if kind == "pair":
            value = came[...].astype(F32)
            blank = jnp.zeros_like(value)
            last = flags[1 + i] > 0
            ext[pl.ds(low, face), :] = jnp.where(last, value, blank).astype(BF)
            ext[pl.ds(high, face), :] = jnp.where(last, blank, value).astype(BF)
        elif kind == "up":
            ext[pl.ds(low, face), :] = came[...]
        else:
            ext[pl.ds(high, face), :] = came[...]
    own_copy.wait()
    lanes = lax.broadcasted_iota(jnp.int32, (block, rows), 1)

    def gather(k, carried):
        at = pl.multiple_of(k * ch, ch)
        for h in range(parts):
            place = (col_ref[k, :, h : h + 1] + col_ref[k, :, h + 4 : h + 5]).astype(jnp.int32)
            picked = dot(one_hot(lanes == place), ext[...]).astype(BF)
            got[pl.ds(h * block, block), pl.ds(at, ch)] = picked
            got_t[pl.ds(at, ch), pl.ds(h * block, block)] = picked.T
        return carried

    lax.fori_loop(0, taps, gather, 0, unroll=9)
    w_copy.wait()
    up_copy.wait()
    odd = flags[0] > 0
    for h in range(parts):
        part = pl.ds(h * block, block)
        v = dot(got[part, :], weights[...])
        s = jax.nn.sigmoid(v)
        act[part, :] = (v * s).astype(BF)
        g = up[part, :].astype(F32) * (s * (1.0 + v * (1.0 - s)))
        gp[part, :] = g.astype(BF)
        turned[part, :half] = jnp.where(odd, g[:, half:], g[:, :half]).astype(BF)
        turned[part, half:] = jnp.where(odd, g[:, :half], g[:, half:]).astype(BF)
    out_copies = [
        pltpu.make_async_copy(act, act_hbm, sems.at[3]),
        pltpu.make_async_copy(gp, gp_hbm, sems.at[4]),
    ]
    for copy in out_copies:
        copy.start()

    def one(t, carried):
        at = pl.multiple_of(t * ch, ch)
        r = dot(got_t[pl.ds(at, ch), :], turned[...])
        keep[pl.ds(at, ch), :] = r[:, :half]
        give[pl.ds(at, ch), :] = r[:, half:].astype(BF)
        return carried

    bounds = [0, 9, 18, taps] if taps > 18 else [0, taps]
    for j in range(len(bounds) - 1):
        lax.fori_loop(bounds[j], bounds[j + 1], one, 0, unroll=3)
        part = pl.ds(bounds[j] * ch, (bounds[j + 1] - bounds[j]) * ch)
        for source, target, sem in ((give, give_hbm, 5 + j), (keep, keep_hbm, 8 + j)):
            copy = pltpu.make_async_copy(source.at[part, :], target.at[part, :], sems.at[sem])
            copy.start()
            out_copies.append(copy)
    for copy in out_copies:
        copy.wait()


def forward(ways, flags, col, own_features, faces, weight, upstream):
    taps, block, _ = col.shape
    own, ch = own_features.shape
    rows = own + 6 * faces[0].shape[0]
    like = jax.ShapeDtypeStruct
    return pl.pallas_call(
        lambda *refs: forward_kernel(ways, block, *refs),
        in_specs=[SMEM, VMEM, HBM, HBM, HBM] + [VMEM] * len(faces),
        out_specs=[HBM, HBM, ANY, ANY],
        out_shape=[
            pltpu.HBM((own, ch), BF),
            pltpu.HBM((own, ch), BF),
            like((taps * ch, ch // 2), F32),
            like((taps * ch, ch // 2), BF),
        ],
        scratch_shapes=[
            pltpu.VMEM((rows, ch), BF),
            pltpu.VMEM((own, taps * ch), BF),
            pltpu.VMEM((taps * ch, own), BF),
            pltpu.VMEM((taps * ch, ch), BF),
            pltpu.VMEM((own, ch), BF),
            pltpu.VMEM((own, ch), BF),
            pltpu.VMEM((own, ch), BF),
            pltpu.VMEM((own, ch), BF),
            pltpu.VMEM((taps * ch, ch // 2), F32),
            pltpu.VMEM((taps * ch, ch // 2), BF),
            pltpu.SemaphoreType.DMA((11,)),
        ],
        compiler_params=params(36),
        name="forward",
    )(flags, col, hold(own_features), hold(weight.reshape(taps * ch, ch)), hold(upstream), *faces)


def backward_kernel(ways, first, count, final, more, *refs):
    refs = list(refs)
    flags = refs.pop(0) if final else None
    row_hbm, gp_hbm, w_hbm = refs[:3]
    before_hbm = refs[3] if more else None
    outs = refs[3 + more : -6]
    row, gp, got, weights, total, sems = refs[-6:]
    rows, ch = total.shape
    block = row.shape[2]
    own = gp.shape[0]
    parts = own // block
    step = 336
    row_copy = pltpu.make_async_copy(row_hbm.at[pl.ds(first, count)], row, sems.at[0])
    gp_copy = pltpu.make_async_copy(gp_hbm, gp, sems.at[1])
    row_copy.start()
    gp_copy.start()
    later = [
        pltpu.make_async_copy(w_hbm.at[first + j], weights.at[:, pl.ds(j * ch, ch)], sems.at[3 + j])
        for j in range(count)
    ]
    if more:
        later.append(pltpu.make_async_copy(before_hbm, total, sems.at[2]))
    for copy in later:
        copy.start()
    row_copy.wait()
    gp_copy.wait()

    def gather(j, carried):
        at = pl.multiple_of(j * ch, ch)
        for r in range(0, rows, step):
            lines = lax.broadcasted_iota(jnp.int32, (step, block), 0) + r
            hots = []
            for h in range(parts):
                place = (row[j, h : h + 1, :] + row[j, h + 4 : h + 5, :]).astype(jnp.int32)
                hots.append(one_hot(lines == place))
            got[pl.ds(r, step), pl.ds(at, ch)] = dot(jnp.concatenate(hots, axis=1), gp[...]).astype(BF)
        return carried

    lax.fori_loop(0, count, gather, 0, unroll=3)
    for copy in later:
        copy.wait()
    for r in range(0, rows, step):
        value = dot(got[pl.ds(r, step), :], weights[...], NT)
        total[pl.ds(r, step), :] = value + total[pl.ds(r, step), :] if more else value
    if final:
        copy = pltpu.make_async_copy(total.at[pl.ds(0, own), :], outs[0], sems.at[0])
        copy.start()
        face = outs[1].shape[0]
        for out, (kind, i) in zip(outs[1:], ways):
            lower = total[pl.ds(own + 2 * i * face, face), :]
            upper = total[pl.ds(own + (2 * i + 1) * face, face), :]
            if kind == "pair":
                out[...] = jnp.where(flags[1 + i] > 0, lower, upper).astype(BF)
            else:
                out[...] = (upper if kind == "up" else lower).astype(BF)
    else:
        copy = pltpu.make_async_copy(total, outs[0], sems.at[0])
        copy.start()
    copy.wait()


def backward(ways, flags, row, gp, weight, first, count, before, rows, final):
    block = row.shape[2]
    own, ch = gp.shape
    face = (rows - own) // 6
    args = [hold(x) for x in [row, gp, weight] + ([] if before is None else [before])]
    args = ([flags] if final else []) + args
    specs = ([SMEM] if final else []) + [HBM] * (len(args) - (1 if final else 0))
    like = jax.ShapeDtypeStruct
    if final:
        out_shape = [pltpu.HBM((own, ch), F32)] + [like((face, ch), BF)] * len(ways)
        out_specs = [HBM] + [VMEM] * len(ways)
    else:
        out_shape = [pltpu.HBM((rows, ch), F32)]
        out_specs = [HBM]
    return pl.pallas_call(
        lambda *refs: backward_kernel(ways, first, count, final, int(before is not None), *refs),
        in_specs=specs,
        out_specs=out_specs,
        out_shape=out_shape,
        scratch_shapes=[
            pltpu.VMEM((count,) + row.shape[1:], F32),
            pltpu.VMEM((own, ch), BF),
            pltpu.VMEM((rows, count * ch), BF),
            pltpu.VMEM((ch, count * ch), BF),
            pltpu.VMEM((rows, ch), F32),
            pltpu.SemaphoreType.DMA((3 + count,)),
        ],
        compiler_params=params(12),
        name="backward",
    )(*args)


def finish_kernel(ways, flags, rows_ref, grad_hbm, *rest):
    faces = rest[: len(ways)]
    out_ref, grad, sem = rest[len(ways) :]
    copy = pltpu.make_async_copy(grad_hbm, grad, sem)
    copy.start()
    face = rows_ref.shape[1]
    own = out_ref.shape[0]
    places = lax.broadcasted_iota(jnp.int32, (own, face), 0)
    total = None
    for came, (kind, i) in zip(faces, ways):
        lower, upper = rows_ref[2 * i : 2 * i + 1, :], rows_ref[2 * i + 1 : 2 * i + 2, :]
        if kind == "pair":
            rows = jnp.where(flags[1 + i] > 0, lower, upper)
        else:
            rows = lower if kind == "up" else upper
        term = dot(one_hot(places == rows), came[...])
        total = term if total is None else total + term
    copy.wait()
    out_ref[...] = (grad[...] + total).astype(BF)


def finish(ways, flags, rows, grad, returned):
    return pl.pallas_call(
        lambda *refs: finish_kernel(ways, *refs),
        in_specs=[SMEM, VMEM, HBM] + [VMEM] * len(returned),
        out_specs=VMEM,
        out_shape=jax.ShapeDtypeStruct(grad.shape, BF),
        scratch_shapes=[pltpu.VMEM(grad.shape, F32), pltpu.SemaphoreType.DMA],
        compiler_params=params(8),
        name="finish",
    )(flags, rows, hold(grad), *returned)


def swap(x, axis, bit):
    n = lax.axis_size(axis)
    return lax.ppermute(x, axis, [(j, j ^ (1 << bit)) for j in range(n)])


def side(axis, bit):
    return (lax.axis_index(axis) >> bit) & 1


def place_kernel(size, spots_ref, *refs):
    count = len(refs) - 2
    arrays, out, sem = refs[: count - (count % 2)], refs[-2], refs[-1]
    copies = []
    for a, array in enumerate(arrays):
        blocks = array.shape[0] // size
        for b in range(blocks):
            at = pl.multiple_of(spots_ref[a * blocks + b], 8)
            lane = pl.multiple_of(spots_ref[len(arrays) * blocks + a], 128)
            target = out.at[pl.ds(at, size), pl.ds(lane, array.shape[1])]
            copies.append(pltpu.make_async_copy(array.at[pl.ds(b * size, size), :], target, sem.at[a * blocks + b]))
    for copy in copies:
        copy.start()
    for copy in copies:
        copy.wait()


def place(spots, arrays, size, rows, before):
    blocks = len(arrays) * (arrays[0].shape[0] // size)
    args = list(arrays) + ([] if before is None else [before])
    return pl.pallas_call(
        lambda *refs: place_kernel(size, *refs),
        in_specs=[SMEM] + [ANY] * len(arrays) + [HBM] * (len(args) - len(arrays)),
        out_specs=HBM,
        out_shape=jax.ShapeDtypeStruct((rows, 2 * arrays[0].shape[1]), BF),
        scratch_shapes=[pltpu.SemaphoreType.DMA((blocks,))],
        input_output_aliases={} if before is None else {len(args): 0},
        compiler_params=params(4),
        name="place",
    )(spots, *args)


def reduce_all(keep, give, scaling, beside):
    bits = lambda axis, low: [(axis, b) for b in range(low, lax.axis_size(axis).bit_length() - 1)]
    plane = [bits("gx", 0) + bits("gz", 1), bits("gz", 1) + bits("gx", 0)]
    turns = len(plane[0])
    rows, ch = keep.shape
    came = swap(give, "gz", 0)
    terms = [[(keep, i * (rows // 2)), (came, i * (rows // 2))] for i in range(2)]

    def total(i, extra, size):
        out = None
        for array, start in terms[i]:
            value = lax.dynamic_slice_in_dim(array, start + extra, size, 0).astype(F32)
            out = value if out is None else out + value
        return out

    size = rows // 2
    for turn in range(turns):
        size = size // 2
        mine = [side(*plane[i][turn]) for i in range(2)]
        out = [total(i, (1 - mine[i]) * size, size).astype(BF) for i in range(2)]
        came = beside(out, [swap(out[i], *plane[i][turn]) for i in range(2)])
        for i in range(2):
            terms[i] = [(a, start + mine[i] * size) for a, start in terms[i]] + [(came[i], 0)]
    n = lax.axis_size("gy")
    at = lax.axis_index("gy")
    size = size // n
    slot = lambda s: jnp.concatenate([total(i, ((at + s) % n) * size, size) for i in range(2)], axis=0)
    turn_by = lambda y, s: lax.ppermute(y, "gy", [(j, (j + s) % n) for j in range(n)])
    out = [slot(s).astype(BF) for s in range(1, n)]
    came = beside(out, [turn_by(y, s + 1) for s, y in enumerate(out)])
    final = slot(0)
    for y in came:
        final = final + y.astype(F32)
    mine = (final * scaling).astype(BF)
    came = beside([mine], [turn_by(mine, s) for s in range(1, n)])
    pieces = [jnp.concatenate([y[i * size : (i + 1) * size] for y in [mine] + came], axis=0) for i in range(2)]
    for turn in range(turns - 1, 0, -1):
        came = beside(pieces, [swap(pieces[i], *plane[i][turn]) for i in range(2)])
        pieces = [jnp.concatenate([pieces[i], came[i]], axis=0) for i in range(2)]
    odd = side("gz", 0)
    cross = lambda arrays: [swap(y, "gz", 0) for y in arrays]
    came = [swap(pieces[i], *plane[i][0]) for i in range(2)]
    twins = cross(pieces)
    sides = [[side(*plane[i][t]) for t in range(turns)] for i in range(2)]
    if size % 8 == 0:
        lanes = jnp.stack([odd, odd, 1 - odd, 1 - odd]) * ch

        def spots(flip):
            out = []
            for i in range(2):
                base = jnp.asarray(i * (rows // 2) + (sides[i][0] ^ flip) * (rows // 4))[None]
                for t in range(1, turns):
                    order = jnp.stack([sides[i][t], 1 - sides[i][t]]) * (rows // (4 << t))
                    base = (base[:, None] + order[None, :]).reshape(-1)
                order = ((at - jnp.arange(n)) % n) * size
                out.append((base[:, None] + order[None, :]).reshape(-1))
            return jnp.concatenate(out + out + [lanes]).astype(jnp.int32)

        half = place(spots(0), pieces + twins, size, rows, None)
        came = beside(pieces, came + [half])
        half = came.pop()
        last = beside(came, cross(came))
        return place(spots(1), came + last, size, rows, half)
    came = beside(pieces, came)
    last = beside(came, cross(came))

    def ordered(i, first, second):
        x = jnp.concatenate([first, second], axis=0).reshape((2,) * turns + (n, size, ch))
        for t in range(turns):
            x = jnp.where(sides[i][t] == 1, jnp.flip(x, t), x)
        x = jnp.take(x, (at - jnp.arange(n)) % n, axis=turns)
        return x.reshape(rows // 2, ch)

    mine = jnp.concatenate([ordered(i, pieces[i], came[i]) for i in range(2)], axis=0)
    other = jnp.concatenate([ordered(i, twins[i], last[i]) for i in range(2)], axis=0)
    low, high = jnp.where(odd == 1, other, mine), jnp.where(odd == 1, mine, other)
    return jnp.concatenate([low, high], axis=1)


def shards(features, weight, upstream, send_rows, in_rows, out_rows, tap_pair_exists):
    own_features = features[0, 0, 0]
    own, ch = own_features.shape
    sends = send_rows[0, 0, 0]
    taps = weight.shape[0]
    block = 256
    ways = routes()
    last = [lax.axis_index(a) == lax.axis_size(a) - 1 for a in AXES]
    flags = jnp.stack([side("gz", 0)] + last).astype(jnp.int32)
    faces = exchange(send(ways, flags, sends, own_features), ways)
    rows = own + 6 * sends.shape[1]
    col, row = invert(in_rows[0, 0, 0], out_rows[0, 0, 0], tap_pair_exists[0, 0, 0], block)
    activated, gp, keep, give = forward(ways, flags, col, own_features, faces, weight, upstream[0, 0, 0])
    devices = lax.axis_size("gx") * lax.axis_size("gy") * lax.axis_size("gz")
    counts = [9, 6, 6, 3, 3]
    steps = [(sum(counts[:j]), c) for j, c in enumerate(counts)]
    steps[-1] = (steps[-1][0], taps - steps[-1][0])
    state = {"turn": 0, "grad": None}

    def beside(out, came):
        turn = state["turn"]
        state["turn"] = turn + 1
        if turn < len(steps):
            final = turn == len(steps) - 1
            held = lax.optimization_barrier((gp, *out))
            grad = backward(ways, flags, row, held[0], weight, *steps[turn], state["grad"], rows, final)
            held = lax.optimization_barrier((*grad, *came))
            state["grad"] = held[0]
            state["back"] = held[1 : len(grad)]
            return list(held[len(grad) :])
        if turn == len(steps):
            held = lax.optimization_barrier((*state["back"], *out))
            returned = exchange(held[: len(ways)], ways)
            held = lax.optimization_barrier((*returned, *came))
            state["returned"] = list(held[: len(ways)])
            return list(held[len(ways) :])
        if turn == len(steps) + 1:
            held = lax.optimization_barrier((state["grad"], *out))
            state["done"] = finish(ways, flags, sends, held[0], state["returned"])
        return came

    grad_weight = reduce_all(keep, give, float(devices * own) ** -0.5, beside).reshape(weight.shape)
    return activated[None, None, None], state["done"][None, None, None], grad_weight


def solution(mesh):
    part = P("gx", "gy", "gz", None, None)
    return jax.shard_map(
        shards,
        mesh=mesh,
        in_specs=(part, P(), part, part, part, part, part),
        out_specs=(part, part, P()),
        check_vma=False,
    )
```

```python
import jax
import jax.numpy as jnp
from jax import lax
from jax.experimental import pallas as pl
from jax.experimental.pallas import tpu as pltpu
from jax.sharding import PartitionSpec as P

BF = jnp.bfloat16
F32 = jnp.float32
NT = (((1,), (1,)), ((), ()))
NN = (((1,), (0,)), ((), ()))
TN = (((0,), (0,)), ((), ()))
AXES = ("gx", "gy", "gz")
MISSING = 2000
VMEM = pl.BlockSpec(memory_space=pltpu.VMEM)
SMEM = pl.BlockSpec(memory_space=pltpu.SMEM)
ANY = pl.BlockSpec(memory_space=pl.ANY)
HBM = pl.BlockSpec(memory_space=pltpu.HBM)


def dot(a, b, dims=NN):
    return lax.dot_general(a, b, dims, preferred_element_type=F32)


def one_hot(mask):
    return jnp.where(mask, jnp.ones((), F32), jnp.zeros((), F32)).astype(BF)


def hold(x):
    return pltpu.with_memory_space_constraint(x, pltpu.HBM)


def params(megabytes):
    return pltpu.CompilerParams(vmem_limit_bytes=megabytes << 20)


def routes():
    out = []
    for i, axis in enumerate(AXES):
        if lax.axis_size(axis) == 2:
            out.append(("pair", i))
        else:
            out.extend([("up", i), ("down", i)])
    return out


def exchange(arrays, ways):
    got = []
    for array, (kind, i) in zip(arrays, ways):
        n = lax.axis_size(AXES[i])
        if kind == "pair":
            pairs = [(0, 1), (1, 0)]
        elif kind == "up":
            pairs = [(j, j + 1) for j in range(n - 1)]
        else:
            pairs = [(j + 1, j) for j in range(n - 1)]
        got.append(lax.ppermute(array, AXES[i], pairs))
    return got


def send_kernel(ways, flags, rows_ref, own_ref, *outs):
    face = rows_ref.shape[2]
    own = own_ref.shape[0]
    places = lax.broadcasted_iota(jnp.int32, (own, face), 0)
    for out, (kind, i) in zip(outs, ways):
        lower, upper = rows_ref[2 * i], rows_ref[2 * i + 1]
        if kind == "pair":
            rows = jnp.where(flags[1 + i] > 0, lower, upper)
        else:
            rows = upper if kind == "up" else lower
        out[...] = dot(one_hot(places == rows), own_ref[...], TN).astype(BF)


def send(ways, flags, rows, own_features):
    shape = jax.ShapeDtypeStruct((rows.shape[2], own_features.shape[1]), BF)
    return pl.pallas_call(
        lambda *refs: send_kernel(ways, *refs),
        in_specs=[SMEM, VMEM, VMEM],
        out_specs=[VMEM] * len(ways),
        out_shape=[shape] * len(ways),
        compiler_params=params(8),
        name="send",
    )(flags, rows, own_features)


def invert_kernel(block, in_hbm, out_hbm, live_hbm, col_ref, row_hbm, tables, row_ref, sems):
    copies = [
        pltpu.make_async_copy(hbm, tables.at[j], sems.at[j])
        for j, hbm in enumerate((in_hbm, out_hbm, live_hbm))
    ]
    for copy in copies:
        copy.start()
    taps, _, own = in_hbm.shape
    lows = lax.broadcasted_iota(jnp.int32, (block, own), 0)
    ranks = lax.broadcasted_iota(jnp.int32, (8, own), 0)
    for copy in copies:
        copy.wait()
    for k in range(taps):
        target = tables[1, k]
        source = jnp.where(tables[2, k] > 0, tables[0, k], MISSING)
        high = target // block
        hot = one_hot(lows == target - high * block)
        big = (source // 16) * 16
        spread = jnp.where(ranks == high, big, jnp.where(ranks - 4 == high, source - big, 0))
        spread = spread.astype(F32).astype(BF)
        col_ref[k] = dot(hot, spread, NT)
        row_ref[k] = dot(spread, hot, NT)
    copy = pltpu.make_async_copy(row_ref, row_hbm, sems.at[3])
    copy.start()
    copy.wait()


def invert(in_rows, out_rows, live, block):
    taps, _, own = in_rows.shape
    return pl.pallas_call(
        lambda *refs: invert_kernel(block, *refs),
        in_specs=[HBM, HBM, HBM],
        out_specs=[VMEM, HBM],
        out_shape=(
            jax.ShapeDtypeStruct((taps, block, 8), F32),
            pltpu.HBM((taps, 8, block), F32),
        ),
        scratch_shapes=[
            pltpu.VMEM((3, taps, 1, own), jnp.int32),
            pltpu.VMEM((taps, 8, block), F32),
            pltpu.SemaphoreType.DMA((4,)),
        ],
        compiler_params=params(12),
        name="invert",
    )(hold(in_rows), hold(out_rows), hold(live))


def forward_kernel(ways, block, flags, col_ref, own_hbm, w_hbm, up_hbm, *rest):
    faces = rest[: len(ways)]
    act_hbm, gp_hbm, keep_hbm, give_hbm = rest[len(ways) : len(ways) + 4]
    ext, got, got_t, weights, turned, up, act, gp, keep, give, sems = rest[len(ways) + 4 :]
    taps = col_ref.shape[0]
    own, ch = up.shape
    rows = ext.shape[0]
    half = ch // 2
    parts = own // block
    w_copy = pltpu.make_async_copy(w_hbm, weights, sems.at[0])
    up_copy = pltpu.make_async_copy(up_hbm, up, sems.at[1])
    own_copy = pltpu.make_async_copy(own_hbm, ext.at[pl.ds(0, own), :], sems.at[2])
    own_copy.start()
    w_copy.start()
    up_copy.start()
    face = faces[0].shape[0]
    for came, (kind, i) in zip(faces, ways):
        low, high = own + 2 * i * face, own + (2 * i + 1) * face
        if kind == "pair":
            value = came[...].astype(F32)
            blank = jnp.zeros_like(value)
            last = flags[1 + i] > 0
            ext[pl.ds(low, face), :] = jnp.where(last, value, blank).astype(BF)
            ext[pl.ds(high, face), :] = jnp.where(last, blank, value).astype(BF)
        elif kind == "up":
            ext[pl.ds(low, face), :] = came[...]
        else:
            ext[pl.ds(high, face), :] = came[...]
    own_copy.wait()
    lanes = lax.broadcasted_iota(jnp.int32, (block, rows), 1)

    def gather(k, carried):
        at = pl.multiple_of(k * ch, ch)
        for h in range(parts):
            place = (col_ref[k, :, h : h + 1] + col_ref[k, :, h + 4 : h + 5]).astype(jnp.int32)
            picked = dot(one_hot(lanes == place), ext[...]).astype(BF)
            got[pl.ds(h * block, block), pl.ds(at, ch)] = picked
            got_t[pl.ds(at, ch), pl.ds(h * block, block)] = picked.T
        return carried

    lax.fori_loop(0, taps, gather, 0, unroll=9)
    w_copy.wait()
    up_copy.wait()
    odd = flags[0] > 0
    for h in range(parts):
        part = pl.ds(h * block, block)
        v = dot(got[part, :], weights[...])
        s = jax.nn.sigmoid(v)
        act[part, :] = (v * s).astype(BF)
        g = up[part, :].astype(F32) * (s * (1.0 + v * (1.0 - s)))
        gp[part, :] = g.astype(BF)
        turned[part, :half] = jnp.where(odd, g[:, half:], g[:, :half]).astype(BF)
        turned[part, half:] = jnp.where(odd, g[:, :half], g[:, half:]).astype(BF)
    out_copies = [
        pltpu.make_async_copy(act, act_hbm, sems.at[3]),
        pltpu.make_async_copy(gp, gp_hbm, sems.at[4]),
    ]
    for copy in out_copies:
        copy.start()

    def one(t, carried):
        at = pl.multiple_of(t * ch, ch)
        r = dot(got_t[pl.ds(at, ch), :], turned[...])
        keep[pl.ds(at, ch), :] = r[:, :half]
        give[pl.ds(at, ch), :] = r[:, half:].astype(BF)
        return carried

    bounds = [0, 9, 18, taps] if taps > 18 else [0, taps]
    for j in range(len(bounds) - 1):
        lax.fori_loop(bounds[j], bounds[j + 1], one, 0, unroll=3)
        part = pl.ds(bounds[j] * ch, (bounds[j + 1] - bounds[j]) * ch)
        for source, target, sem in ((give, give_hbm, 5 + j), (keep, keep_hbm, 8 + j)):
            copy = pltpu.make_async_copy(source.at[part, :], target.at[part, :], sems.at[sem])
            copy.start()
            out_copies.append(copy)
    for copy in out_copies:
        copy.wait()


def forward(ways, flags, col, own_features, faces, weight, upstream):
    taps, block, _ = col.shape
    own, ch = own_features.shape
    rows = own + 6 * faces[0].shape[0]
    like = jax.ShapeDtypeStruct
    return pl.pallas_call(
        lambda *refs: forward_kernel(ways, block, *refs),
        in_specs=[SMEM, VMEM, HBM, HBM, HBM] + [VMEM] * len(faces),
        out_specs=[HBM, HBM, ANY, ANY],
        out_shape=[
            pltpu.HBM((own, ch), BF),
            pltpu.HBM((own, ch), BF),
            like((taps * ch, ch // 2), F32),
            like((taps * ch, ch // 2), BF),
        ],
        scratch_shapes=[
            pltpu.VMEM((rows, ch), BF),
            pltpu.VMEM((own, taps * ch), BF),
            pltpu.VMEM((taps * ch, own), BF),
            pltpu.VMEM((taps * ch, ch), BF),
            pltpu.VMEM((own, ch), BF),
            pltpu.VMEM((own, ch), BF),
            pltpu.VMEM((own, ch), BF),
            pltpu.VMEM((own, ch), BF),
            pltpu.VMEM((taps * ch, ch // 2), F32),
            pltpu.VMEM((taps * ch, ch // 2), BF),
            pltpu.SemaphoreType.DMA((11,)),
        ],
        compiler_params=params(36),
        name="forward",
    )(flags, col, hold(own_features), hold(weight.reshape(taps * ch, ch)), hold(upstream), *faces)


def backward_kernel(ways, first, count, final, more, *refs):
    refs = list(refs)
    flags = refs.pop(0) if final else None
    row_hbm, gp_hbm, w_hbm = refs[:3]
    before_hbm = refs[3] if more else None
    outs = refs[3 + more : -6]
    row, gp, got, weights, total, sems = refs[-6:]
    rows, ch = total.shape
    block = row.shape[2]
    own = gp.shape[0]
    parts = own // block
    step = 336
    row_copy = pltpu.make_async_copy(row_hbm.at[pl.ds(first, count)], row, sems.at[0])
    gp_copy = pltpu.make_async_copy(gp_hbm, gp, sems.at[1])
    row_copy.start()
    gp_copy.start()
    later = [
        pltpu.make_async_copy(w_hbm.at[first + j], weights.at[:, pl.ds(j * ch, ch)], sems.at[3 + j])
        for j in range(count)
    ]
    if more:
        later.append(pltpu.make_async_copy(before_hbm, total, sems.at[2]))
    for copy in later:
        copy.start()
    row_copy.wait()
    gp_copy.wait()

    def gather(j, carried):
        at = pl.multiple_of(j * ch, ch)
        for r in range(0, rows, step):
            lines = lax.broadcasted_iota(jnp.int32, (step, block), 0) + r
            hots = []
            for h in range(parts):
                place = (row[j, h : h + 1, :] + row[j, h + 4 : h + 5, :]).astype(jnp.int32)
                hots.append(one_hot(lines == place))
            got[pl.ds(r, step), pl.ds(at, ch)] = dot(jnp.concatenate(hots, axis=1), gp[...]).astype(BF)
        return carried

    lax.fori_loop(0, count, gather, 0, unroll=3)
    for copy in later:
        copy.wait()
    for r in range(0, rows, step):
        value = dot(got[pl.ds(r, step), :], weights[...], NT)
        total[pl.ds(r, step), :] = value + total[pl.ds(r, step), :] if more else value
    if final:
        copy = pltpu.make_async_copy(total.at[pl.ds(0, own), :], outs[0], sems.at[0])
        copy.start()
        face = outs[1].shape[0]
        for out, (kind, i) in zip(outs[1:], ways):
            lower = total[pl.ds(own + 2 * i * face, face), :]
            upper = total[pl.ds(own + (2 * i + 1) * face, face), :]
            if kind == "pair":
                out[...] = jnp.where(flags[1 + i] > 0, lower, upper).astype(BF)
            else:
                out[...] = (upper if kind == "up" else lower).astype(BF)
    else:
        copy = pltpu.make_async_copy(total, outs[0], sems.at[0])
        copy.start()
    copy.wait()


def backward(ways, flags, row, gp, weight, first, count, before, rows, final):
    block = row.shape[2]
    own, ch = gp.shape
    face = (rows - own) // 6
    args = [hold(x) for x in [row, gp, weight] + ([] if before is None else [before])]
    args = ([flags] if final else []) + args
    specs = ([SMEM] if final else []) + [HBM] * (len(args) - (1 if final else 0))
    like = jax.ShapeDtypeStruct
    if final:
        out_shape = [pltpu.HBM((own, ch), F32)] + [like((face, ch), BF)] * len(ways)
        out_specs = [HBM] + [VMEM] * len(ways)
    else:
        out_shape = [pltpu.HBM((rows, ch), F32)]
        out_specs = [HBM]
    return pl.pallas_call(
        lambda *refs: backward_kernel(ways, first, count, final, int(before is not None), *refs),
        in_specs=specs,
        out_specs=out_specs,
        out_shape=out_shape,
        scratch_shapes=[
            pltpu.VMEM((count,) + row.shape[1:], F32),
            pltpu.VMEM((own, ch), BF),
            pltpu.VMEM((rows, count * ch), BF),
            pltpu.VMEM((ch, count * ch), BF),
            pltpu.VMEM((rows, ch), F32),
            pltpu.SemaphoreType.DMA((3 + count,)),
        ],
        compiler_params=params(16),
        name="backward",
    )(*args)


def finish_kernel(ways, flags, rows_ref, grad_hbm, *rest):
    faces = rest[: len(ways)]
    out_ref, grad, sem = rest[len(ways) :]
    copy = pltpu.make_async_copy(grad_hbm, grad, sem)
    copy.start()
    face = rows_ref.shape[2]
    own = out_ref.shape[0]
    places = lax.broadcasted_iota(jnp.int32, (own, face), 0)
    total = None
    for came, (kind, i) in zip(faces, ways):
        lower, upper = rows_ref[2 * i], rows_ref[2 * i + 1]
        if kind == "pair":
            rows = jnp.where(flags[1 + i] > 0, lower, upper)
        else:
            rows = lower if kind == "up" else upper
        term = dot(one_hot(places == rows), came[...])
        total = term if total is None else total + term
    copy.wait()
    out_ref[...] = (grad[...] + total).astype(BF)


def finish(ways, flags, rows, grad, returned):
    return pl.pallas_call(
        lambda *refs: finish_kernel(ways, *refs),
        in_specs=[SMEM, VMEM, HBM] + [VMEM] * len(returned),
        out_specs=VMEM,
        out_shape=jax.ShapeDtypeStruct(grad.shape, BF),
        scratch_shapes=[pltpu.VMEM(grad.shape, F32), pltpu.SemaphoreType.DMA],
        compiler_params=params(8),
        name="finish",
    )(flags, rows, hold(grad), *returned)


def swap(x, axis, bit):
    n = lax.axis_size(axis)
    return lax.ppermute(x, axis, [(j, j ^ (1 << bit)) for j in range(n)])


def side(axis, bit):
    return (lax.axis_index(axis) >> bit) & 1


def place_kernel(size, spots_ref, *refs):
    count = len(refs) - 2
    arrays, out, sem = refs[: count - (count % 2)], refs[-2], refs[-1]
    copies = []
    for a, array in enumerate(arrays):
        blocks = array.shape[0] // size
        for b in range(blocks):
            at = pl.multiple_of(spots_ref[a * blocks + b], 8)
            lane = pl.multiple_of(spots_ref[len(arrays) * blocks + a], 128)
            target = out.at[pl.ds(at, size), pl.ds(lane, array.shape[1])]
            copies.append(pltpu.make_async_copy(array.at[pl.ds(b * size, size), :], target, sem.at[a * blocks + b]))
    for copy in copies:
        copy.start()
    for copy in copies:
        copy.wait()


def place(spots, arrays, size, rows, before):
    blocks = len(arrays) * (arrays[0].shape[0] // size)
    args = list(arrays) + ([] if before is None else [before])
    return pl.pallas_call(
        lambda *refs: place_kernel(size, *refs),
        in_specs=[SMEM] + [ANY] * len(arrays) + [HBM] * (len(args) - len(arrays)),
        out_specs=HBM,
        out_shape=jax.ShapeDtypeStruct((rows, 2 * arrays[0].shape[1]), BF),
        scratch_shapes=[pltpu.SemaphoreType.DMA((blocks,))],
        input_output_aliases={} if before is None else {len(args): 0},
        compiler_params=params(4),
        name="place",
    )(spots, *args)


def reduce_all(keep, give, scaling, beside, after):
    bits = lambda axis, low: [(axis, b) for b in range(low, lax.axis_size(axis).bit_length() - 1)]
    plane = [bits("gx", 0) + bits("gz", 1), bits("gz", 1) + bits("gx", 0)]
    turns = len(plane[0])
    rows, ch = keep.shape
    came = swap(give, "gz", 0)
    terms = [[(keep, i * (rows // 2)), (came, i * (rows // 2))] for i in range(2)]

    def total(i, extra, size):
        out = None
        for array, start in terms[i]:
            value = lax.dynamic_slice_in_dim(array, start + extra, size, 0).astype(F32)
            out = value if out is None else out + value
        return out

    size = rows // 2
    for turn in range(turns):
        size = size // 2
        mine = [side(*plane[i][turn]) for i in range(2)]
        out = [total(i, (1 - mine[i]) * size, size).astype(BF) for i in range(2)]
        came = beside(out, [swap(out[i], *plane[i][turn]) for i in range(2)])
        for i in range(2):
            terms[i] = [(a, start + mine[i] * size) for a, start in terms[i]] + [(came[i], 0)]
    n = lax.axis_size("gy")
    at = lax.axis_index("gy")
    size = size // n
    slot = lambda s: jnp.concatenate([total(i, ((at + s) % n) * size, size) for i in range(2)], axis=0)
    turn_by = lambda y, s: lax.ppermute(y, "gy", [(j, (j + s) % n) for j in range(n)])
    out = [slot(s).astype(BF) for s in range(1, n)]
    came = beside(out, [turn_by(y, s + 1) for s, y in enumerate(out)])
    final = slot(0)
    for y in came:
        final = final + y.astype(F32)
    mine = (final * scaling).astype(BF)
    came = beside([mine], [turn_by(mine, s) for s in range(1, n)])
    pieces = [jnp.concatenate([y[i * size : (i + 1) * size] for y in [mine] + came], axis=0) for i in range(2)]
    for turn in range(turns - 1, 0, -1):
        came = beside(pieces, [swap(pieces[i], *plane[i][turn]) for i in range(2)])
        pieces = [jnp.concatenate([pieces[i], came[i]], axis=0) for i in range(2)]
    odd = side("gz", 0)
    cross = lambda arrays: [swap(y, "gz", 0) for y in arrays]
    came = beside(pieces, [swap(pieces[i], *plane[i][0]) for i in range(2)])
    twins = cross(after(pieces))
    sides = [[side(*plane[i][t]) for t in range(turns)] for i in range(2)]
    if size % 8 == 0:
        lanes = jnp.stack([odd, odd, 1 - odd, 1 - odd]) * ch

        def spots(flip):
            out = []
            for i in range(2):
                base = jnp.asarray(i * (rows // 2) + (sides[i][0] ^ flip) * (rows // 4))[None]
                for t in range(1, turns):
                    order = jnp.stack([sides[i][t], 1 - sides[i][t]]) * (rows // (4 << t))
                    base = (base[:, None] + order[None, :]).reshape(-1)
                order = ((at - jnp.arange(n)) % n) * size
                out.append((base[:, None] + order[None, :]).reshape(-1))
            return jnp.concatenate(out + out + [lanes]).astype(jnp.int32)

        half = place(spots(0), pieces + twins, size, rows, None)
        came = lax.optimization_barrier((half, *came))
        half, came = came[0], list(came[1:])
        last = cross(came)
        return place(spots(1), came + last, size, rows, half)
    last = cross(came)

    def ordered(i, first, second):
        x = jnp.concatenate([first, second], axis=0).reshape((2,) * turns + (n, size, ch))
        for t in range(turns):
            x = jnp.where(sides[i][t] == 1, jnp.flip(x, t), x)
        x = jnp.take(x, (at - jnp.arange(n)) % n, axis=turns)
        return x.reshape(rows // 2, ch)

    mine = jnp.concatenate([ordered(i, pieces[i], came[i]) for i in range(2)], axis=0)
    other = jnp.concatenate([ordered(i, twins[i], last[i]) for i in range(2)], axis=0)
    low, high = jnp.where(odd == 1, other, mine), jnp.where(odd == 1, mine, other)
    return jnp.concatenate([low, high], axis=1)


def shards(features, weight, upstream, send_rows, in_rows, out_rows, tap_pair_exists):
    own_features = features[0, 0, 0]
    own, ch = own_features.shape
    single = lambda x: x[0, 0, 0][:, None, :]
    sends = single(send_rows)
    taps = weight.shape[0]
    block = 256
    ways = routes()
    last = [lax.axis_index(a) == lax.axis_size(a) - 1 for a in AXES]
    flags = jnp.stack([side("gz", 0)] + last).astype(jnp.int32)
    faces = exchange(send(ways, flags, sends, own_features), ways)
    rows = own + 6 * sends.shape[2]
    col, row = invert(single(in_rows), single(out_rows), single(tap_pair_exists), block)
    activated, gp, keep, give = forward(ways, flags, col, own_features, faces, weight, upstream[0, 0, 0])
    devices = lax.axis_size("gx") * lax.axis_size("gy") * lax.axis_size("gz")
    counts = [12, 6, 9]
    steps = [(sum(counts[:j]), c) for j, c in enumerate(counts)]
    steps[-1] = (steps[-1][0], taps - steps[-1][0])
    state = {"turn": 0, "grad": None, "returned": {}}
    early = [j for j, (_, i) in enumerate(ways) if i != 1][:2]
    late = [j for j in range(len(ways)) if j not in early]

    def beside(out, came):
        turn = state["turn"]
        state["turn"] = turn + 1
        if turn < len(steps):
            final = turn == len(steps) - 1
            held = lax.optimization_barrier((gp, *out))
            grad = backward(ways, flags, row, held[0], weight, *steps[turn], state["grad"], rows, final)
            held = lax.optimization_barrier((*grad, *came))
            state["grad"] = held[0]
            state["back"] = held[1 : len(grad)]
            return list(held[len(grad) :])
        if turn < len(steps) + 2:
            picks = early if turn == len(steps) else late
            held = lax.optimization_barrier((*[state["back"][j] for j in picks], *out))
            got = exchange(held[: len(picks)], [ways[j] for j in picks])
            held = lax.optimization_barrier((*got, *came))
            for j, face in zip(picks, held):
                state["returned"][j] = face
            return list(held[len(picks) :])
        if turn == len(steps) + 2:
            held = lax.optimization_barrier((state["grad"], *out))
            state["done"] = finish(ways, flags, sends, held[0], [state["returned"][j] for j in range(len(ways))])
        return came

    def after(out):
        held = lax.optimization_barrier((state["done"], *out))
        state["done"] = held[0]
        return list(held[1:])

    grad_weight = reduce_all(keep, give, float(devices * own) ** -0.5, beside, after).reshape(weight.shape)
    return activated[None, None, None], state["done"][None, None, None], grad_weight


def solution(mesh):
    part = P("gx", "gy", "gz", None, None)
    return jax.shard_map(
        shards,
        mesh=mesh,
        in_specs=(part, P(), part, part, part, part, part),
        out_specs=(part, part, P()),
        check_vma=False,
    )
```

```python
import jax
import jax.numpy as jnp
from jax import lax
from jax.experimental import pallas as pl
from jax.experimental.pallas import tpu as pltpu
from jax.sharding import PartitionSpec as P

BF = jnp.bfloat16
F32 = jnp.float32
NT = (((1,), (1,)), ((), ()))
NN = (((1,), (0,)), ((), ()))
TN = (((0,), (0,)), ((), ()))
AXES = ("gx", "gy", "gz")
MISSING = 2000
VMEM = pl.BlockSpec(memory_space=pltpu.VMEM)
SMEM = pl.BlockSpec(memory_space=pltpu.SMEM)
ANY = pl.BlockSpec(memory_space=pl.ANY)
HBM = pl.BlockSpec(memory_space=pltpu.HBM)


def dot(a, b, dims=NN):
    return lax.dot_general(a, b, dims, preferred_element_type=F32)


def one_hot(mask):
    return jnp.where(mask, jnp.ones((), F32), jnp.zeros((), F32)).astype(BF)


def hold(x):
    return pltpu.with_memory_space_constraint(x, pltpu.HBM)


def params(megabytes):
    return pltpu.CompilerParams(vmem_limit_bytes=megabytes << 20)


def routes():
    out = []
    for i, axis in enumerate(AXES):
        if lax.axis_size(axis) == 2:
            out.append(("pair", i))
        else:
            out.extend([("up", i), ("down", i)])
    return out


def exchange(arrays, ways):
    got = []
    for array, (kind, i) in zip(arrays, ways):
        n = lax.axis_size(AXES[i])
        if kind == "pair":
            pairs = [(0, 1), (1, 0)]
        elif kind == "up":
            pairs = [(j, j + 1) for j in range(n - 1)]
        else:
            pairs = [(j + 1, j) for j in range(n - 1)]
        got.append(lax.ppermute(array, AXES[i], pairs))
    return got


def send_kernel(ways, flags, rows_ref, own_ref, *outs):
    face = rows_ref.shape[2]
    own = own_ref.shape[0]
    places = lax.broadcasted_iota(jnp.int32, (own, face), 0)
    for out, (kind, i) in zip(outs, ways):
        lower, upper = rows_ref[2 * i], rows_ref[2 * i + 1]
        if kind == "pair":
            rows = jnp.where(flags[1 + i] > 0, lower, upper)
        else:
            rows = upper if kind == "up" else lower
        out[...] = dot(one_hot(places == rows), own_ref[...], TN).astype(BF)


def send(ways, flags, rows, own_features):
    shape = jax.ShapeDtypeStruct((rows.shape[2], own_features.shape[1]), BF)
    return pl.pallas_call(
        lambda *refs: send_kernel(ways, *refs),
        in_specs=[SMEM, VMEM, VMEM],
        out_specs=[VMEM] * len(ways),
        out_shape=[shape] * len(ways),
        compiler_params=params(8),
        name="send",
    )(flags, rows, own_features)


def invert_kernel(block, in_hbm, out_hbm, live_hbm, col_ref, row_hbm, tables, row_ref, sems):
    copies = [
        pltpu.make_async_copy(hbm, tables.at[j], sems.at[j])
        for j, hbm in enumerate((in_hbm, out_hbm, live_hbm))
    ]
    for copy in copies:
        copy.start()
    taps, _, own = in_hbm.shape
    lows = lax.broadcasted_iota(jnp.int32, (block, own), 0)
    ranks = lax.broadcasted_iota(jnp.int32, (16, own), 0)
    for copy in copies:
        copy.wait()
    for k in range(taps):
        target = tables[1, k]
        source = jnp.where(tables[2, k] > 0, tables[0, k], MISSING)
        high = target // block
        hot = one_hot(lows == target - high * block)
        big = (source // 16) * 16
        spread = jnp.where(ranks == high, big, jnp.where(ranks - 8 == high, source - big, 0))
        spread = spread.astype(F32).astype(BF)
        col = dot(hot, spread, NT)
        col_ref[k] = col
        row_ref[k] = col.T
    copy = pltpu.make_async_copy(row_ref, row_hbm, sems.at[3])
    copy.start()
    copy.wait()


def invert(in_rows, out_rows, live, block):
    taps, _, own = in_rows.shape
    return pl.pallas_call(
        lambda *refs: invert_kernel(block, *refs),
        in_specs=[HBM, HBM, HBM],
        out_specs=[VMEM, HBM],
        out_shape=(
            jax.ShapeDtypeStruct((taps, block, 16), F32),
            pltpu.HBM((taps, 16, block), F32),
        ),
        scratch_shapes=[
            pltpu.VMEM((3, taps, 1, own), jnp.int32),
            pltpu.VMEM((taps, 16, block), F32),
            pltpu.SemaphoreType.DMA((4,)),
        ],
        compiler_params=params(12),
        name="invert",
    )(hold(in_rows), hold(out_rows), hold(live))


def forward_kernel(ways, step, flags, col_ref, own_hbm, w_hbm, up_hbm, *rest):
    faces = rest[: len(ways)]
    act_hbm, gp_hbm, keep_hbm, give_hbm = rest[len(ways) : len(ways) + 4]
    ext, got, got_t, weights, turned, up, act, gp, keep, give, sems = rest[len(ways) + 4 :]
    taps = col_ref.shape[0]
    own, ch = up.shape
    rows = ext.shape[0]
    half = ch // 2
    parts = own // step
    block = col_ref.shape[1]
    w_copy = pltpu.make_async_copy(w_hbm, weights, sems.at[0])
    up_copy = pltpu.make_async_copy(up_hbm, up, sems.at[1])
    own_copy = pltpu.make_async_copy(own_hbm, ext.at[pl.ds(0, own), :], sems.at[2])
    own_copy.start()
    w_copy.start()
    up_copy.start()
    face = faces[0].shape[0]
    for came, (kind, i) in zip(faces, ways):
        low, high = own + 2 * i * face, own + (2 * i + 1) * face
        if kind == "pair":
            value = came[...].astype(F32)
            blank = jnp.zeros_like(value)
            last = flags[1 + i] > 0
            ext[pl.ds(low, face), :] = jnp.where(last, value, blank).astype(BF)
            ext[pl.ds(high, face), :] = jnp.where(last, blank, value).astype(BF)
        elif kind == "up":
            ext[pl.ds(low, face), :] = came[...]
        else:
            ext[pl.ds(high, face), :] = came[...]
    own_copy.wait()
    lanes = lax.broadcasted_iota(jnp.int32, (step, rows), 1)

    def gather(k, carried):
        at = pl.multiple_of(k * ch, ch)
        for h in range(parts):
            places = [
                col_ref[k, :, b : b + 1] + col_ref[k, :, b + 8 : b + 9]
                for b in range(h * step // block, (h + 1) * step // block)
            ]
            place = jnp.concatenate(places, axis=0).astype(jnp.int32)
            picked = dot(one_hot(lanes == place), ext[...]).astype(BF)
            got[pl.ds(h * step, step), pl.ds(at, ch)] = picked
            got_t[pl.ds(at, ch), pl.ds(h * step, step)] = picked.T
        return carried

    lax.fori_loop(0, taps, gather, 0, unroll=9)
    w_copy.wait()
    up_copy.wait()
    odd = flags[0] > 0
    for h in range(parts):
        part = pl.ds(h * step, step)
        v = dot(got[part, :], weights[...])
        s = jax.nn.sigmoid(v)
        act[part, :] = (v * s).astype(BF)
        g = up[part, :].astype(F32) * (s * (1.0 + v * (1.0 - s)))
        gp[part, :] = g.astype(BF)
        turned[part, :half] = jnp.where(odd, g[:, half:], g[:, :half]).astype(BF)
        turned[part, half:] = jnp.where(odd, g[:, :half], g[:, half:]).astype(BF)
    out_copies = [
        pltpu.make_async_copy(act, act_hbm, sems.at[3]),
        pltpu.make_async_copy(gp, gp_hbm, sems.at[4]),
    ]
    for copy in out_copies:
        copy.start()

    def one(t, carried):
        at = pl.multiple_of(t * ch, ch)
        r = dot(got_t[pl.ds(at, ch), :], turned[...])
        keep[pl.ds(at, ch), :] = r[:, :half]
        give[pl.ds(at, ch), :] = r[:, half:].astype(BF)
        return carried

    bounds = [0, 9, 18, taps] if taps > 18 else [0, taps]
    for j in range(len(bounds) - 1):
        lax.fori_loop(bounds[j], bounds[j + 1], one, 0, unroll=3)
        part = pl.ds(bounds[j] * ch, (bounds[j + 1] - bounds[j]) * ch)
        for source, target, sem in ((give, give_hbm, 5 + j), (keep, keep_hbm, 8 + j)):
            copy = pltpu.make_async_copy(source.at[part, :], target.at[part, :], sems.at[sem])
            copy.start()
            out_copies.append(copy)
    for copy in out_copies:
        copy.wait()


def forward(ways, flags, col, own_features, faces, weight, upstream):
    taps, block, _ = col.shape
    own, ch = own_features.shape
    rows = own + 6 * faces[0].shape[0]
    like = jax.ShapeDtypeStruct
    return pl.pallas_call(
        lambda *refs: forward_kernel(ways, 256, *refs),
        in_specs=[SMEM, VMEM, HBM, HBM, HBM] + [VMEM] * len(faces),
        out_specs=[HBM, HBM, ANY, ANY],
        out_shape=[
            pltpu.HBM((own, ch), BF),
            pltpu.HBM((own, ch), BF),
            like((taps * ch, ch // 2), F32),
            like((taps * ch, ch // 2), BF),
        ],
        scratch_shapes=[
            pltpu.VMEM((rows, ch), BF),
            pltpu.VMEM((own, taps * ch), BF),
            pltpu.VMEM((taps * ch, own), BF),
            pltpu.VMEM((taps * ch, ch), BF),
            pltpu.VMEM((own, ch), BF),
            pltpu.VMEM((own, ch), BF),
            pltpu.VMEM((own, ch), BF),
            pltpu.VMEM((own, ch), BF),
            pltpu.VMEM((taps * ch, ch // 2), F32),
            pltpu.VMEM((taps * ch, ch // 2), BF),
            pltpu.SemaphoreType.DMA((11,)),
        ],
        compiler_params=params(36),
        name="forward",
    )(flags, col, hold(own_features), hold(weight.reshape(taps * ch, ch)), hold(upstream), *faces)


def backward_body(start, first, count, step, row_hbm, gp_hbm, w_hbm, before_hbm, row, gp, got, weights, total, sems):
    size, ch = total.shape
    block = row.shape[2]
    parts = gp.shape[0] // block
    row_copy = pltpu.make_async_copy(row_hbm.at[pl.ds(first, count)], row, sems.at[0])
    gp_copy = pltpu.make_async_copy(gp_hbm, gp, sems.at[1])
    row_copy.start()
    gp_copy.start()
    later = [
        pltpu.make_async_copy(w_hbm.at[first + j], weights.at[:, pl.ds(j * ch, ch)], sems.at[3 + j])
        for j in range(count)
    ]
    if before_hbm is not None:
        later.append(pltpu.make_async_copy(before_hbm, total, sems.at[2]))
    for copy in later:
        copy.start()
    row_copy.wait()
    gp_copy.wait()

    def gather(j, carried):
        at = pl.multiple_of(j * ch, ch)
        for r in range(0, size, step):
            lines = lax.broadcasted_iota(jnp.int32, (step, block), 0) + (start + r)
            hots = []
            for h in range(parts):
                place = (row[j, h : h + 1, :] + row[j, h + 8 : h + 9, :]).astype(jnp.int32)
                hots.append(one_hot(lines == place))
            got[pl.ds(r, step), pl.ds(at, ch)] = dot(jnp.concatenate(hots, axis=1), gp[...]).astype(BF)
        return carried

    lax.fori_loop(0, count, gather, 0, unroll=3)
    for copy in later:
        copy.wait()
    for r in range(0, size, step):
        value = dot(got[pl.ds(r, step), :], weights[...], NT)
        total[pl.ds(r, step), :] = value if before_hbm is None else value + total[pl.ds(r, step), :]


def backward_scratch(row, gp, size, count):
    own, ch = gp.shape
    return [
        pltpu.VMEM((count,) + row.shape[1:], F32),
        pltpu.VMEM((own, ch), BF),
        pltpu.VMEM((size, count * ch), BF),
        pltpu.VMEM((ch, count * ch), BF),
        pltpu.VMEM((size, ch), F32),
        pltpu.SemaphoreType.DMA((3 + count,)),
    ]


def faces_kernel(ways, start, count, flags, row_hbm, gp_hbm, w_hbm, *rest):
    outs, scratch = rest[: len(ways)], rest[len(ways) :]
    total = scratch[4]
    face = outs[0].shape[0]
    backward_body(start, 0, count, 3 * face, row_hbm, gp_hbm, w_hbm, None, *scratch)
    for out, (kind, i) in zip(outs, ways):
        lower = total[pl.ds(2 * i * face, face), :]
        upper = total[pl.ds((2 * i + 1) * face, face), :]
        if kind == "pair":
            out[...] = jnp.where(flags[1 + i] > 0, lower, upper).astype(BF)
        else:
            out[...] = (upper if kind == "up" else lower).astype(BF)


def backward_faces(ways, flags, row, gp, weight, face):
    taps = row.shape[0]
    own, ch = gp.shape
    return pl.pallas_call(
        lambda *refs: faces_kernel(ways, own, taps, *refs),
        in_specs=[SMEM, HBM, HBM, HBM],
        out_specs=[VMEM] * len(ways),
        out_shape=[jax.ShapeDtypeStruct((face, ch), BF)] * len(ways),
        scratch_shapes=backward_scratch(row, gp, 6 * face, taps),
        compiler_params=params(18),
        name="backward_faces",
    )(flags, hold(row), hold(gp), hold(weight))


def own_kernel(first, count, row_hbm, gp_hbm, w_hbm, out_hbm, *scratch):
    backward_body(0, first, count, 384, row_hbm, gp_hbm, w_hbm, None, *scratch)
    copy = pltpu.make_async_copy(scratch[4], out_hbm, scratch[5].at[2])
    copy.start()
    copy.wait()


def backward_own(row, gp, weight, first, count):
    return pl.pallas_call(
        lambda *refs: own_kernel(first, count, *refs),
        in_specs=[HBM, HBM, HBM],
        out_specs=HBM,
        out_shape=pltpu.HBM(gp.shape, F32),
        scratch_shapes=backward_scratch(row, gp, gp.shape[0], count),
        compiler_params=params(14),
        name="backward_own",
    )(hold(row), hold(gp), hold(weight))


def finish_kernel(ways, first, count, flags, rows_ref, row_hbm, gp_hbm, w_hbm, before_hbm, *rest):
    faces, out_ref, scratch = rest[: len(ways)], rest[len(ways)], rest[len(ways) + 1 :]
    backward_body(0, first, count, 384, row_hbm, gp_hbm, w_hbm, before_hbm, *scratch)
    face = rows_ref.shape[2]
    own = out_ref.shape[0]
    places = lax.broadcasted_iota(jnp.int32, (own, face), 0)
    total = scratch[4][...]
    for came, (kind, i) in zip(faces, ways):
        lower, upper = rows_ref[2 * i], rows_ref[2 * i + 1]
        if kind == "pair":
            rows = jnp.where(flags[1 + i] > 0, lower, upper)
        else:
            rows = lower if kind == "up" else upper
        total = total + dot(one_hot(places == rows), came[...])
    out_ref[...] = total.astype(BF)


def finish(ways, flags, rows, row, gp, weight, first, count, before, returned):
    return pl.pallas_call(
        lambda *refs: finish_kernel(ways, first, count, *refs),
        in_specs=[SMEM, VMEM, HBM, HBM, HBM, HBM] + [VMEM] * len(returned),
        out_specs=VMEM,
        out_shape=jax.ShapeDtypeStruct(gp.shape, BF),
        scratch_shapes=backward_scratch(row, gp, gp.shape[0], count),
        compiler_params=params(16),
        name="finish",
    )(flags, rows, hold(row), hold(gp), hold(weight), hold(before), *returned)


def swap(x, axis, bit):
    n = lax.axis_size(axis)
    return lax.ppermute(x, axis, [(j, j ^ (1 << bit)) for j in range(n)])


def side(axis, bit):
    return (lax.axis_index(axis) >> bit) & 1


def place_kernel(size, spots_ref, *refs):
    count = len(refs) - 2
    arrays, out, sem = refs[: count - (count % 2)], refs[-2], refs[-1]
    copies = []
    for a, array in enumerate(arrays):
        blocks = array.shape[0] // size
        for b in range(blocks):
            at = pl.multiple_of(spots_ref[a * blocks + b], 8)
            lane = pl.multiple_of(spots_ref[len(arrays) * blocks + a], 128)
            target = out.at[pl.ds(at, size), pl.ds(lane, array.shape[1])]
            copies.append(pltpu.make_async_copy(array.at[pl.ds(b * size, size), :], target, sem.at[a * blocks + b]))
    for copy in copies:
        copy.start()
    for copy in copies:
        copy.wait()


def place(spots, arrays, size, rows, before):
    blocks = len(arrays) * (arrays[0].shape[0] // size)
    args = list(arrays) + ([] if before is None else [before])
    return pl.pallas_call(
        lambda *refs: place_kernel(size, *refs),
        in_specs=[SMEM] + [ANY] * len(arrays) + [HBM] * (len(args) - len(arrays)),
        out_specs=HBM,
        out_shape=jax.ShapeDtypeStruct((rows, 2 * arrays[0].shape[1]), BF),
        scratch_shapes=[pltpu.SemaphoreType.DMA((blocks,))],
        input_output_aliases={} if before is None else {len(args): 0},
        compiler_params=params(4),
        name="place",
    )(spots, *args)


def reduce_all(keep, give, scaling, beside):
    bits = lambda axis, low: [(axis, b) for b in range(low, lax.axis_size(axis).bit_length() - 1)]
    plane = [bits("gx", 0) + bits("gz", 1), bits("gz", 1) + bits("gx", 0)]
    turns = len(plane[0])
    rows, ch = keep.shape
    came = swap(give, "gz", 0)
    terms = [[(keep, i * (rows // 2)), (came, i * (rows // 2))] for i in range(2)]

    def total(i, extra, size):
        out = None
        for array, start in terms[i]:
            value = lax.dynamic_slice_in_dim(array, start + extra, size, 0).astype(F32)
            out = value if out is None else out + value
        return out

    size = rows // 2
    for turn in range(turns):
        size = size // 2
        mine = [side(*plane[i][turn]) for i in range(2)]
        out = [total(i, (1 - mine[i]) * size, size).astype(BF) for i in range(2)]
        came = beside(out, [swap(out[i], *plane[i][turn]) for i in range(2)])
        for i in range(2):
            terms[i] = [(a, start + mine[i] * size) for a, start in terms[i]] + [(came[i], 0)]
    n = lax.axis_size("gy")
    at = lax.axis_index("gy")
    size = size // n
    slot = lambda s: jnp.concatenate([total(i, ((at + s) % n) * size, size) for i in range(2)], axis=0)
    turn_by = lambda y, s: lax.ppermute(y, "gy", [(j, (j + s) % n) for j in range(n)])
    out = [slot(s).astype(BF) for s in range(1, n)]
    came = beside(out, [turn_by(y, s + 1) for s, y in enumerate(out)])
    final = slot(0)
    for y in came:
        final = final + y.astype(F32)
    mine = (final * scaling).astype(BF)
    came = beside([mine], [turn_by(mine, s) for s in range(1, n)])
    pieces = [jnp.concatenate([y[i * size : (i + 1) * size] for y in [mine] + came], axis=0) for i in range(2)]
    for turn in range(turns - 1, 0, -1):
        came = beside(pieces, [swap(pieces[i], *plane[i][turn]) for i in range(2)])
        pieces = [jnp.concatenate([pieces[i], came[i]], axis=0) for i in range(2)]
    odd = side("gz", 0)
    cross = lambda arrays: [swap(y, "gz", 0) for y in arrays]
    came = beside(pieces, [swap(pieces[i], *plane[i][0]) for i in range(2)])
    twins = cross(pieces)
    sides = [[side(*plane[i][t]) for t in range(turns)] for i in range(2)]
    if size % 8 == 0:
        lanes = jnp.stack([odd, odd, 1 - odd, 1 - odd]) * ch

        def spots(flip):
            out = []
            for i in range(2):
                base = jnp.asarray(i * (rows // 2) + (sides[i][0] ^ flip) * (rows // 4))[None]
                for t in range(1, turns):
                    order = jnp.stack([sides[i][t], 1 - sides[i][t]]) * (rows // (4 << t))
                    base = (base[:, None] + order[None, :]).reshape(-1)
                order = ((at - jnp.arange(n)) % n) * size
                out.append((base[:, None] + order[None, :]).reshape(-1))
            return jnp.concatenate(out + out + [lanes]).astype(jnp.int32)

        half = place(spots(0), pieces + twins, size, rows, None)
        came = lax.optimization_barrier((half, *came))
        half, came = came[0], list(came[1:])
        last = cross(came)
        return place(spots(1), came + last, size, rows, half)
    last = cross(came)

    def ordered(i, first, second):
        x = jnp.concatenate([first, second], axis=0).reshape((2,) * turns + (n, size, ch))
        for t in range(turns):
            x = jnp.where(sides[i][t] == 1, jnp.flip(x, t), x)
        x = jnp.take(x, (at - jnp.arange(n)) % n, axis=turns)
        return x.reshape(rows // 2, ch)

    mine = jnp.concatenate([ordered(i, pieces[i], came[i]) for i in range(2)], axis=0)
    other = jnp.concatenate([ordered(i, twins[i], last[i]) for i in range(2)], axis=0)
    low, high = jnp.where(odd == 1, other, mine), jnp.where(odd == 1, mine, other)
    return jnp.concatenate([low, high], axis=1)


def shards(features, weight, upstream, send_rows, in_rows, out_rows, tap_pair_exists):
    own_features = features[0, 0, 0]
    own, ch = own_features.shape
    single = lambda x: x[0, 0, 0][:, None, :]
    sends = single(send_rows)
    taps = weight.shape[0]
    block = 128
    ways = routes()
    last = [lax.axis_index(a) == lax.axis_size(a) - 1 for a in AXES]
    flags = jnp.stack([side("gz", 0)] + last).astype(jnp.int32)
    faces = exchange(send(ways, flags, sends, own_features), ways)
    col, row = invert(single(in_rows), single(out_rows), single(tap_pair_exists), block)
    activated, gp, keep, give = forward(ways, flags, col, own_features, faces, weight, upstream[0, 0, 0])
    devices = lax.axis_size("gx") * lax.axis_size("gy") * lax.axis_size("gz")
    split = 12
    state = {"turn": 0, "returned": {}}
    early = [j for j, (_, i) in enumerate(ways) if i != 2]
    late = [j for j, (_, i) in enumerate(ways) if i == 2]

    def tied(out, work, came):
        held = lax.optimization_barrier((gp, *out))
        made = work(held[0])
        held = lax.optimization_barrier((*made, *came))
        return held[: len(made)], list(held[len(made) :])

    def beside(out, came):
        turn = state["turn"]
        state["turn"] = turn + 1
        if turn == 0:
            work = lambda g: backward_faces(ways, flags, row, g, weight, sends.shape[2])
            state["back"], came = tied(out, work, came)
        elif turn in (1, 2):
            picks = early if turn == 1 else late
            held = lax.optimization_barrier((*[state["back"][j] for j in picks], *out))
            got = exchange(held[: len(picks)], [ways[j] for j in picks])
            held = lax.optimization_barrier((*got, *came))
            for j, face in zip(picks, held):
                state["returned"][j] = face
            came = list(held[len(picks) :])
        elif turn == 3:
            work = lambda g: [backward_own(row, g, weight, 0, split)]
            (state["grad"],), came = tied(out, work, came)
        elif turn == 5:
            faces = [state["returned"][j] for j in range(len(ways))]
            work = lambda g: [finish(ways, flags, sends, row, g, weight, split, taps - split, state["grad"], faces)]
            (state["done"],), came = tied(out, work, came)
        return came

    grad_weight = reduce_all(keep, give, float(devices * own) ** -0.5, beside).reshape(weight.shape)
    return activated[None, None, None], state["done"][None, None, None], grad_weight


def solution(mesh):
    part = P("gx", "gy", "gz", None, None)
    return jax.shard_map(
        shards,
        mesh=mesh,
        in_specs=(part, P(), part, part, part, part, part),
        out_specs=(part, part, P()),
        check_vma=False,
    )
```

```python
import jax
import jax.numpy as jnp
from jax import lax
from jax.experimental import pallas as pl
from jax.experimental.pallas import tpu as pltpu
from jax.sharding import PartitionSpec as P

BF = jnp.bfloat16
F32 = jnp.float32
NT = (((1,), (1,)), ((), ()))
NN = (((1,), (0,)), ((), ()))
TN = (((0,), (0,)), ((), ()))
AXES = ("gx", "gy", "gz")
MISSING = 2000
VMEM = pl.BlockSpec(memory_space=pltpu.VMEM)
SMEM = pl.BlockSpec(memory_space=pltpu.SMEM)
ANY = pl.BlockSpec(memory_space=pl.ANY)
HBM = pl.BlockSpec(memory_space=pltpu.HBM)


def dot(a, b, dims=NN):
    return lax.dot_general(a, b, dims, preferred_element_type=F32)


def one_hot(mask):
    return jnp.where(mask, jnp.ones((), F32), jnp.zeros((), F32)).astype(BF)


def hold(x):
    return pltpu.with_memory_space_constraint(x, pltpu.HBM)


def params(megabytes):
    return pltpu.CompilerParams(vmem_limit_bytes=megabytes << 20)


def routes():
    out = []
    for i, axis in enumerate(AXES):
        out.append((0, i))
        if lax.axis_size(axis) > 2:
            out.append((1, i))
    return out


def exchange(arrays, ways):
    got = []
    for array, (odd, i) in zip(arrays, ways):
        n = lax.axis_size(AXES[i])
        pairs = [p for j in range(odd, n - 1, 2) for p in ((j, j + 1), (j + 1, j))]
        got.append(lax.ppermute(array, AXES[i], pairs))
    return got


def towards(flags, way, lower, upper):
    odd, i = way
    return jnp.where(flags[1 + i] == odd, upper, lower)


def send_kernel(ways, flags, rows_ref, own_ref, *outs):
    face = rows_ref.shape[2]
    own = own_ref.shape[0]
    places = lax.broadcasted_iota(jnp.int32, (own, face), 0)
    for out, way in zip(outs, ways):
        rows = towards(flags, way, rows_ref[2 * way[1]], rows_ref[2 * way[1] + 1])
        out[...] = dot(one_hot(places == rows), own_ref[...], TN).astype(BF)


def send(ways, flags, rows, own_features):
    shape = jax.ShapeDtypeStruct((rows.shape[2], own_features.shape[1]), BF)
    return pl.pallas_call(
        lambda *refs: send_kernel(ways, *refs),
        in_specs=[SMEM, VMEM, VMEM],
        out_specs=[VMEM] * len(ways),
        out_shape=[shape] * len(ways),
        compiler_params=params(8),
        name="send",
    )(flags, rows, own_features)


def invert_kernel(block, in_hbm, out_hbm, live_hbm, col_ref, row_hbm, tables, row_ref, sems):
    copies = [
        pltpu.make_async_copy(hbm, tables.at[j], sems.at[j])
        for j, hbm in enumerate((in_hbm, out_hbm, live_hbm))
    ]
    for copy in copies:
        copy.start()
    taps, _, own = in_hbm.shape
    lows = lax.broadcasted_iota(jnp.int32, (block, own), 0)
    ranks = lax.broadcasted_iota(jnp.int32, (16, own), 0)
    for copy in copies:
        copy.wait()
    for k in range(taps):
        target = tables[1, k]
        source = jnp.where(tables[2, k] > 0, tables[0, k], MISSING)
        high = target // block
        hot = one_hot(lows == target - high * block)
        big = (source // 16) * 16
        spread = jnp.where(ranks == high, big, jnp.where(ranks - 8 == high, source - big, 0))
        spread = spread.astype(F32).astype(BF)
        col = dot(hot, spread, NT)
        col_ref[k] = col
        row_ref[k] = col.T
    copy = pltpu.make_async_copy(row_ref, row_hbm, sems.at[3])
    copy.start()
    copy.wait()


def invert(in_rows, out_rows, live, block):
    taps, _, own = in_rows.shape
    return pl.pallas_call(
        lambda *refs: invert_kernel(block, *refs),
        in_specs=[HBM, HBM, HBM],
        out_specs=[VMEM, HBM],
        out_shape=(
            jax.ShapeDtypeStruct((taps, block, 16), F32),
            pltpu.HBM((taps, 16, block), F32),
        ),
        scratch_shapes=[
            pltpu.VMEM((3, taps, 1, own), jnp.int32),
            pltpu.VMEM((taps, 16, block), F32),
            pltpu.SemaphoreType.DMA((4,)),
        ],
        compiler_params=params(12),
        name="invert",
    )(hold(in_rows), hold(out_rows), hold(live))


def forward_kernel(ways, step, flags, col_ref, own_hbm, w_hbm, up_hbm, *rest):
    faces = rest[: len(ways)]
    act_hbm, gp_hbm, keep_hbm, give_hbm = rest[len(ways) : len(ways) + 4]
    ext, got, got_t, weights, turned, up, act, gp, keep, give, sems = rest[len(ways) + 4 :]
    taps = col_ref.shape[0]
    own, ch = up.shape
    rows = ext.shape[0]
    half = ch // 2
    parts = own // step
    block = col_ref.shape[1]
    w_copy = pltpu.make_async_copy(w_hbm, weights, sems.at[0])
    up_copy = pltpu.make_async_copy(up_hbm, up, sems.at[1])
    own_copy = pltpu.make_async_copy(own_hbm, ext.at[pl.ds(0, own), :], sems.at[2])
    own_copy.start()
    w_copy.start()
    up_copy.start()
    face = faces[0].shape[0]
    for i in range(len(AXES)):
        mine = [came[...].astype(F32) for came, way in zip(faces, ways) if way[1] == i]
        mine = mine if len(mine) == 2 else mine + [jnp.zeros_like(mine[0])]
        even = flags[1 + i] == 0
        ext[pl.ds(own + 2 * i * face, face), :] = jnp.where(even, mine[1], mine[0]).astype(BF)
        ext[pl.ds(own + (2 * i + 1) * face, face), :] = jnp.where(even, mine[0], mine[1]).astype(BF)
    own_copy.wait()
    lanes = lax.broadcasted_iota(jnp.int32, (step, rows), 1)

    def gather(k, carried):
        at = pl.multiple_of(k * ch, ch)
        for h in range(parts):
            places = [
                col_ref[k, :, b : b + 1] + col_ref[k, :, b + 8 : b + 9]
                for b in range(h * step // block, (h + 1) * step // block)
            ]
            place = jnp.concatenate(places, axis=0).astype(jnp.int32)
            picked = dot(one_hot(lanes == place), ext[...]).astype(BF)
            got[pl.ds(h * step, step), pl.ds(at, ch)] = picked
            got_t[pl.ds(at, ch), pl.ds(h * step, step)] = picked.T
        return carried

    lax.fori_loop(0, taps, gather, 0, unroll=9)
    w_copy.wait()
    up_copy.wait()
    odd = flags[0] > 0
    for h in range(parts):
        part = pl.ds(h * step, step)
        v = dot(got[part, :], weights[...])
        s = jax.nn.sigmoid(v)
        act[part, :] = (v * s).astype(BF)
        g = up[part, :].astype(F32) * (s * (1.0 + v * (1.0 - s)))
        gp[part, :] = g.astype(BF)
        turned[part, :half] = jnp.where(odd, g[:, half:], g[:, :half]).astype(BF)
        turned[part, half:] = jnp.where(odd, g[:, :half], g[:, half:]).astype(BF)
    out_copies = [
        pltpu.make_async_copy(act, act_hbm, sems.at[3]),
        pltpu.make_async_copy(gp, gp_hbm, sems.at[4]),
    ]
    for copy in out_copies:
        copy.start()

    def one(t, carried):
        at = pl.multiple_of(t * ch, ch)
        r = dot(got_t[pl.ds(at, ch), :], turned[...])
        keep[pl.ds(at, ch), :] = r[:, :half]
        give[pl.ds(at, ch), :] = r[:, half:].astype(BF)
        return carried

    bounds = [0, 9, 18, taps] if taps > 18 else [0, taps]
    for j in range(len(bounds) - 1):
        lax.fori_loop(bounds[j], bounds[j + 1], one, 0, unroll=3)
        part = pl.ds(bounds[j] * ch, (bounds[j + 1] - bounds[j]) * ch)
        for source, target, sem in ((give, give_hbm, 5 + j), (keep, keep_hbm, 8 + j)):
            copy = pltpu.make_async_copy(source.at[part, :], target.at[part, :], sems.at[sem])
            copy.start()
            out_copies.append(copy)
    for copy in out_copies:
        copy.wait()


def forward(ways, flags, col, own_features, faces, weight, upstream):
    taps, block, _ = col.shape
    own, ch = own_features.shape
    rows = own + 6 * faces[0].shape[0]
    like = jax.ShapeDtypeStruct
    return pl.pallas_call(
        lambda *refs: forward_kernel(ways, 256, *refs),
        in_specs=[SMEM, VMEM, HBM, HBM, HBM] + [VMEM] * len(faces),
        out_specs=[HBM, HBM, ANY, ANY],
        out_shape=[
            pltpu.HBM((own, ch), BF),
            pltpu.HBM((own, ch), BF),
            like((taps * ch, ch // 2), F32),
            like((taps * ch, ch // 2), BF),
        ],
        scratch_shapes=[
            pltpu.VMEM((rows, ch), BF),
            pltpu.VMEM((own, taps * ch), BF),
            pltpu.VMEM((taps * ch, own), BF),
            pltpu.VMEM((taps * ch, ch), BF),
            pltpu.VMEM((own, ch), BF),
            pltpu.VMEM((own, ch), BF),
            pltpu.VMEM((own, ch), BF),
            pltpu.VMEM((own, ch), BF),
            pltpu.VMEM((taps * ch, ch // 2), F32),
            pltpu.VMEM((taps * ch, ch // 2), BF),
            pltpu.SemaphoreType.DMA((11,)),
        ],
        compiler_params=params(36),
        name="forward",
    )(flags, col, hold(own_features), hold(weight.reshape(taps * ch, ch)), hold(upstream), *faces)


def backward_body(start, first, count, step, row_hbm, gp_hbm, w_hbm, before_hbm, row, gp, got, weights, total, sems):
    size, ch = total.shape
    block = row.shape[2]
    parts = gp.shape[0] // block
    row_copy = pltpu.make_async_copy(row_hbm.at[pl.ds(first, count)], row, sems.at[0])
    gp_copy = pltpu.make_async_copy(gp_hbm, gp, sems.at[1])
    row_copy.start()
    gp_copy.start()
    later = [
        pltpu.make_async_copy(w_hbm.at[first + j], weights.at[:, pl.ds(j * ch, ch)], sems.at[3 + j])
        for j in range(count)
    ]
    if before_hbm is not None:
        later.append(pltpu.make_async_copy(before_hbm, total, sems.at[2]))
    for copy in later:
        copy.start()
    row_copy.wait()
    gp_copy.wait()

    def gather(j, carried):
        at = pl.multiple_of(j * ch, ch)
        for r in range(0, size, step):
            lines = lax.broadcasted_iota(jnp.int32, (step, block), 0) + (start + r)
            hots = []
            for h in range(parts):
                place = (row[j, h : h + 1, :] + row[j, h + 8 : h + 9, :]).astype(jnp.int32)
                hots.append(one_hot(lines == place))
            got[pl.ds(r, step), pl.ds(at, ch)] = dot(jnp.concatenate(hots, axis=1), gp[...]).astype(BF)
        return carried

    lax.fori_loop(0, count, gather, 0, unroll=3)
    for copy in later:
        copy.wait()
    for r in range(0, size, step):
        value = dot(got[pl.ds(r, step), :], weights[...], NT)
        total[pl.ds(r, step), :] = value if before_hbm is None else value + total[pl.ds(r, step), :]


def backward_scratch(row, gp, size, count):
    own, ch = gp.shape
    return [
        pltpu.VMEM((count,) + row.shape[1:], F32),
        pltpu.VMEM((own, ch), BF),
        pltpu.VMEM((size, count * ch), BF),
        pltpu.VMEM((ch, count * ch), BF),
        pltpu.VMEM((size, ch), F32),
        pltpu.SemaphoreType.DMA((3 + count,)),
    ]


def faces_kernel(ways, start, count, flags, row_hbm, gp_hbm, w_hbm, *rest):
    outs, scratch = rest[: len(ways)], rest[len(ways) :]
    total = scratch[4]
    face = outs[0].shape[0]
    backward_body(start, 0, count, 3 * face, row_hbm, gp_hbm, w_hbm, None, *scratch)
    for out, way in zip(outs, ways):
        lower = total[pl.ds(2 * way[1] * face, face), :]
        upper = total[pl.ds((2 * way[1] + 1) * face, face), :]
        out[...] = towards(flags, way, lower, upper).astype(BF)


def backward_faces(ways, flags, row, gp, weight, face):
    taps = row.shape[0]
    own, ch = gp.shape
    return pl.pallas_call(
        lambda *refs: faces_kernel(ways, own, taps, *refs),
        in_specs=[SMEM, HBM, HBM, HBM],
        out_specs=[VMEM] * len(ways),
        out_shape=[jax.ShapeDtypeStruct((face, ch), BF)] * len(ways),
        scratch_shapes=backward_scratch(row, gp, 6 * face, taps),
        compiler_params=params(18),
        name="backward_faces",
    )(flags, hold(row), hold(gp), hold(weight))


def own_kernel(first, count, row_hbm, gp_hbm, w_hbm, out_hbm, *scratch):
    backward_body(0, first, count, 384, row_hbm, gp_hbm, w_hbm, None, *scratch)
    copy = pltpu.make_async_copy(scratch[4], out_hbm, scratch[5].at[2])
    copy.start()
    copy.wait()


def backward_own(row, gp, weight, first, count):
    return pl.pallas_call(
        lambda *refs: own_kernel(first, count, *refs),
        in_specs=[HBM, HBM, HBM],
        out_specs=HBM,
        out_shape=pltpu.HBM(gp.shape, F32),
        scratch_shapes=backward_scratch(row, gp, gp.shape[0], count),
        compiler_params=params(14),
        name="backward_own",
    )(hold(row), hold(gp), hold(weight))


def finish_kernel(ways, first, count, flags, rows_ref, row_hbm, gp_hbm, w_hbm, before_hbm, *rest):
    faces, out_ref, scratch = rest[: len(ways)], rest[len(ways)], rest[len(ways) + 1 :]
    backward_body(0, first, count, 384, row_hbm, gp_hbm, w_hbm, before_hbm, *scratch)
    face = rows_ref.shape[2]
    own = out_ref.shape[0]
    places = lax.broadcasted_iota(jnp.int32, (own, face), 0)
    total = scratch[4][...]
    for came, way in zip(faces, ways):
        rows = towards(flags, way, rows_ref[2 * way[1]], rows_ref[2 * way[1] + 1])
        total = total + dot(one_hot(places == rows), came[...])
    out_ref[...] = total.astype(BF)


def finish(ways, flags, rows, row, gp, weight, first, count, before, returned):
    return pl.pallas_call(
        lambda *refs: finish_kernel(ways, first, count, *refs),
        in_specs=[SMEM, VMEM, HBM, HBM, HBM, HBM] + [VMEM] * len(returned),
        out_specs=VMEM,
        out_shape=jax.ShapeDtypeStruct(gp.shape, BF),
        scratch_shapes=backward_scratch(row, gp, gp.shape[0], count),
        compiler_params=params(16),
        name="finish",
    )(flags, rows, hold(row), hold(gp), hold(weight), hold(before), *returned)


def swap(x, axis, bit):
    n = lax.axis_size(axis)
    return lax.ppermute(x, axis, [(j, j ^ (1 << bit)) for j in range(n)])


def side(axis, bit):
    return (lax.axis_index(axis) >> bit) & 1


def place_kernel(size, spots_ref, *refs):
    count = len(refs) - 2
    arrays, out, sem = refs[: count - (count % 2)], refs[-2], refs[-1]
    copies = []
    for a, array in enumerate(arrays):
        blocks = array.shape[0] // size
        for b in range(blocks):
            at = pl.multiple_of(spots_ref[a * blocks + b], 8)
            lane = pl.multiple_of(spots_ref[len(arrays) * blocks + a], 128)
            target = out.at[pl.ds(at, size), pl.ds(lane, array.shape[1])]
            copies.append(pltpu.make_async_copy(array.at[pl.ds(b * size, size), :], target, sem.at[a * blocks + b]))
    for copy in copies:
        copy.start()
    for copy in copies:
        copy.wait()


def place(spots, arrays, size, rows, before):
    blocks = len(arrays) * (arrays[0].shape[0] // size)
    args = list(arrays) + ([] if before is None else [before])
    return pl.pallas_call(
        lambda *refs: place_kernel(size, *refs),
        in_specs=[SMEM] + [ANY] * len(arrays) + [HBM] * (len(args) - len(arrays)),
        out_specs=HBM,
        out_shape=jax.ShapeDtypeStruct((rows, 2 * arrays[0].shape[1]), BF),
        scratch_shapes=[pltpu.SemaphoreType.DMA((blocks,))],
        input_output_aliases={} if before is None else {len(args): 0},
        compiler_params=params(4),
        name="place",
    )(spots, *args)


def reduce_all(keep, give, scaling, beside):
    bits = lambda axis, low: [(axis, b) for b in range(low, lax.axis_size(axis).bit_length() - 1)]
    plane = [bits("gx", 0) + bits("gz", 1), bits("gz", 1) + bits("gx", 0)]
    turns = len(plane[0])
    rows, ch = keep.shape
    came = swap(give, "gz", 0)
    terms = [[(keep, i * (rows // 2)), (came, i * (rows // 2))] for i in range(2)]

    def total(i, extra, size):
        out = None
        for array, start in terms[i]:
            value = lax.dynamic_slice_in_dim(array, start + extra, size, 0).astype(F32)
            out = value if out is None else out + value
        return out

    size = rows // 2
    for turn in range(turns):
        size = size // 2
        mine = [side(*plane[i][turn]) for i in range(2)]
        out = [total(i, (1 - mine[i]) * size, size).astype(BF) for i in range(2)]
        came = beside(out, [swap(out[i], *plane[i][turn]) for i in range(2)])
        for i in range(2):
            terms[i] = [(a, start + mine[i] * size) for a, start in terms[i]] + [(came[i], 0)]
    n = lax.axis_size("gy")
    at = lax.axis_index("gy")
    size = size // n
    slot = lambda s: jnp.concatenate([total(i, ((at + s) % n) * size, size) for i in range(2)], axis=0)
    turn_by = lambda y, s: lax.ppermute(y, "gy", [(j, (j + s) % n) for j in range(n)])
    out = [slot(s).astype(BF) for s in range(1, n)]
    came = beside(out, [turn_by(y, s + 1) for s, y in enumerate(out)])
    final = slot(0)
    for y in came:
        final = final + y.astype(F32)
    mine = (final * scaling).astype(BF)
    came = beside([mine], [turn_by(mine, s) for s in range(1, n)])
    pieces = [jnp.concatenate([y[i * size : (i + 1) * size] for y in [mine] + came], axis=0) for i in range(2)]
    for turn in range(turns - 1, 0, -1):
        came = beside(pieces, [swap(pieces[i], *plane[i][turn]) for i in range(2)])
        pieces = [jnp.concatenate([pieces[i], came[i]], axis=0) for i in range(2)]
    odd = side("gz", 0)
    cross = lambda arrays: [swap(y, "gz", 0) for y in arrays]
    came = beside(pieces, [swap(pieces[i], *plane[i][0]) for i in range(2)])
    twins = cross(pieces)
    sides = [[side(*plane[i][t]) for t in range(turns)] for i in range(2)]
    if size % 8 == 0:
        lanes = jnp.stack([odd, odd, 1 - odd, 1 - odd]) * ch

        def spots(flip):
            out = []
            for i in range(2):
                base = jnp.asarray(i * (rows // 2) + (sides[i][0] ^ flip) * (rows // 4))[None]
                for t in range(1, turns):
                    order = jnp.stack([sides[i][t], 1 - sides[i][t]]) * (rows // (4 << t))
                    base = (base[:, None] + order[None, :]).reshape(-1)
                order = ((at - jnp.arange(n)) % n) * size
                out.append((base[:, None] + order[None, :]).reshape(-1))
            return jnp.concatenate(out + out + [lanes]).astype(jnp.int32)

        half = place(spots(0), pieces + twins, size, rows, None)
        came = lax.optimization_barrier((half, *came))
        half, came = came[0], list(came[1:])
        last = cross(came)
        return place(spots(1), came + last, size, rows, half)
    last = cross(came)

    def ordered(i, first, second):
        x = jnp.concatenate([first, second], axis=0).reshape((2,) * turns + (n, size, ch))
        for t in range(turns):
            x = jnp.where(sides[i][t] == 1, jnp.flip(x, t), x)
        x = jnp.take(x, (at - jnp.arange(n)) % n, axis=turns)
        return x.reshape(rows // 2, ch)

    mine = jnp.concatenate([ordered(i, pieces[i], came[i]) for i in range(2)], axis=0)
    other = jnp.concatenate([ordered(i, twins[i], last[i]) for i in range(2)], axis=0)
    low, high = jnp.where(odd == 1, other, mine), jnp.where(odd == 1, mine, other)
    return jnp.concatenate([low, high], axis=1)


def shards(features, weight, upstream, send_rows, in_rows, out_rows, tap_pair_exists):
    own_features = features[0, 0, 0]
    own, ch = own_features.shape
    single = lambda x: x[0, 0, 0][:, None, :]
    sends = single(send_rows)
    taps = weight.shape[0]
    block = 128
    ways = routes()
    flags = jnp.stack([side("gz", 0)] + [lax.axis_index(a) & 1 for a in AXES]).astype(jnp.int32)
    faces = exchange(send(ways, flags, sends, own_features), ways)
    col, row = invert(single(in_rows), single(out_rows), single(tap_pair_exists), block)
    activated, gp, keep, give = forward(ways, flags, col, own_features, faces, weight, upstream[0, 0, 0])
    devices = lax.axis_size("gx") * lax.axis_size("gy") * lax.axis_size("gz")
    split = 12
    state = {"turn": 0, "returned": {}}
    late = [j for j, way in enumerate(ways) if way in ((0, 0), (1, 2))]
    early = [j for j in range(len(ways)) if j not in late]

    def tied(out, work, came):
        held = lax.optimization_barrier((gp, *out))
        made = work(held[0])
        held = lax.optimization_barrier((*made, *came))
        return held[: len(made)], list(held[len(made) :])

    def beside(out, came):
        turn = state["turn"]
        state["turn"] = turn + 1
        if turn == 0:
            work = lambda g: backward_faces(ways, flags, row, g, weight, sends.shape[2])
            state["back"], came = tied(out, work, came)
        elif turn in (1, 2):
            picks = early if turn == 1 else late
            held = lax.optimization_barrier((*[state["back"][j] for j in picks], *out))
            got = exchange(held[: len(picks)], [ways[j] for j in picks])
            held = lax.optimization_barrier((*got, *came))
            for j, face in zip(picks, held):
                state["returned"][j] = face
            came = list(held[len(picks) :])
        elif turn == 3:
            work = lambda g: [backward_own(row, g, weight, 0, split)]
            (state["grad"],), came = tied(out, work, came)
        elif turn == 5:
            faces = [state["returned"][j] for j in range(len(ways))]
            work = lambda g: [finish(ways, flags, sends, row, g, weight, split, taps - split, state["grad"], faces)]
            (state["done"],), came = tied(out, work, came)
        return came

    grad_weight = reduce_all(keep, give, float(devices * own) ** -0.5, beside).reshape(weight.shape)
    return activated[None, None, None], state["done"][None, None, None], grad_weight


def solution(mesh):
    part = P("gx", "gy", "gz", None, None)
    return jax.shard_map(
        shards,
        mesh=mesh,
        in_specs=(part, P(), part, part, part, part, part),
        out_specs=(part, part, P()),
        check_vma=False,
    )
```

```python
import jax
import jax.numpy as jnp
from jax import lax
from jax.experimental import pallas as pl
from jax.experimental.pallas import tpu as pltpu
from jax.sharding import PartitionSpec as P

BF = jnp.bfloat16
F32 = jnp.float32
NT = (((1,), (1,)), ((), ()))
NN = (((1,), (0,)), ((), ()))
TN = (((0,), (0,)), ((), ()))
AXES = ("gx", "gy", "gz")
MISSING = 2000
VMEM = pl.BlockSpec(memory_space=pltpu.VMEM)
SMEM = pl.BlockSpec(memory_space=pltpu.SMEM)
ANY = pl.BlockSpec(memory_space=pl.ANY)
HBM = pl.BlockSpec(memory_space=pltpu.HBM)


def dot(a, b, dims=NN):
    return lax.dot_general(a, b, dims, preferred_element_type=F32)


def one_hot(mask):
    return jnp.where(mask, jnp.ones((), F32), jnp.zeros((), F32)).astype(BF)


def hold(x):
    return pltpu.with_memory_space_constraint(x, pltpu.HBM)


def params(megabytes):
    return pltpu.CompilerParams(vmem_limit_bytes=megabytes << 20)


def routes():
    out = []
    for i, axis in enumerate(AXES):
        out.append((0, i))
        if lax.axis_size(axis) > 2:
            out.append((1, i))
    return out


def slots():
    out, count = [], 0
    for axis in AXES:
        size = 1 if lax.axis_size(axis) == 2 else 2
        out.append(tuple(range(count, count + size)))
        count += size
    return out, count


def exchange(arrays, ways):
    got = []
    for array, (odd, i) in zip(arrays, ways):
        n = lax.axis_size(AXES[i])
        pairs = [p for j in range(odd, n - 1, 2) for p in ((j, j + 1), (j + 1, j))]
        got.append(lax.ppermute(array, AXES[i], pairs))
    return got


def towards(flags, way, lower, upper):
    odd, i = way
    return jnp.where(flags[1 + i] == odd, upper, lower)


def send_kernel(ways, flags, rows_hbm, own_hbm, *rest):
    outs, (rows_ref, own_ref, sems) = rest[: len(ways)], rest[len(ways) :]
    copies = [
        pltpu.make_async_copy(own_hbm, own_ref, sems.at[0]),
        pltpu.make_async_copy(rows_hbm, rows_ref, sems.at[1]),
    ]
    for copy in copies:
        copy.start()
    for copy in copies:
        copy.wait()
    face = rows_ref.shape[2]
    own = own_ref.shape[0]
    places = lax.broadcasted_iota(jnp.int32, (own, face), 0)
    for out, way in zip(outs, ways):
        rows = towards(flags, way, rows_ref[2 * way[1]], rows_ref[2 * way[1] + 1])
        out[...] = dot(one_hot(places == rows), own_ref[...], TN).astype(BF)


def send(ways, flags, rows, own_features):
    shape = jax.ShapeDtypeStruct((rows.shape[2], own_features.shape[1]), BF)
    return pl.pallas_call(
        lambda *refs: send_kernel(ways, *refs),
        in_specs=[SMEM, HBM, HBM],
        out_specs=[VMEM] * len(ways),
        out_shape=[shape] * len(ways),
        scratch_shapes=[
            pltpu.VMEM(rows.shape, jnp.int32),
            pltpu.VMEM(own_features.shape, BF),
            pltpu.SemaphoreType.DMA((2,)),
        ],
        compiler_params=params(8),
        name="send",
    )(flags, hold(rows), hold(own_features))


def invert_kernel(block, face, pairs, flags, in_hbm, out_hbm, live_hbm, col_ref, row_hbm, tables, row_ref, sems):
    copies = [
        pltpu.make_async_copy(hbm, tables.at[j], sems.at[j])
        for j, hbm in enumerate((in_hbm, out_hbm, live_hbm))
    ]
    for copy in copies:
        copy.start()
    taps, _, own = in_hbm.shape
    lows = lax.broadcasted_iota(jnp.int32, (block, own), 0)
    ranks = lax.broadcasted_iota(jnp.int32, (16, own), 0)
    for copy in copies:
        copy.wait()
    for k in range(taps):
        target = tables[1, k]
        source = tables[0, k]
        live = tables[2, k] > 0
        for i in pairs:
            dead = own + (2 * i + flags[1 + i]) * face
            beyond = source >= dead + face
            live = jnp.logical_and(live, jnp.logical_or(beyond, source < dead))
            source = jnp.where(beyond, source - face, source)
        source = jnp.where(live, source, MISSING)
        high = target // block
        hot = one_hot(lows == target - high * block)
        big = (source // 16) * 16
        spread = jnp.where(ranks == high, big, jnp.where(ranks - 8 == high, source - big, 0))
        spread = spread.astype(F32).astype(BF)
        col = dot(hot, spread, NT)
        col_ref[k] = col
        row_ref[k] = col.T
    copy = pltpu.make_async_copy(row_ref, row_hbm, sems.at[3])
    copy.start()
    copy.wait()


def invert(flags, in_rows, out_rows, live, face, block):
    pairs = [i for i in reversed(range(len(AXES))) if lax.axis_size(AXES[i]) == 2]
    taps, _, own = in_rows.shape
    return pl.pallas_call(
        lambda *refs: invert_kernel(block, face, pairs, *refs),
        in_specs=[SMEM, HBM, HBM, HBM],
        out_specs=[VMEM, HBM],
        out_shape=(
            jax.ShapeDtypeStruct((taps, block, 16), F32),
            pltpu.HBM((taps, 16, block), F32),
        ),
        scratch_shapes=[
            pltpu.VMEM((3, taps, 1, own), jnp.int32),
            pltpu.VMEM((taps, 16, block), F32),
            pltpu.SemaphoreType.DMA((4,)),
        ],
        compiler_params=params(12),
        name="invert",
    )(flags, hold(in_rows), hold(out_rows), hold(live))


def forward_kernel(ways, where, step, flags, col_ref, own_hbm, w_hbm, up_hbm, *rest):
    faces = rest[: len(ways)]
    act_hbm, gp_hbm, keep_hbm, *give_hbm = rest[len(ways) : len(ways) + 5]
    ext, got, got_t, weights, turned, up, act, gp, keep, give, sems = rest[len(ways) + 5 :]
    taps = col_ref.shape[0]
    own, ch = up.shape
    rows = ext.shape[0]
    half = ch // 2
    parts = own // step
    block = col_ref.shape[1]
    w_copy = pltpu.make_async_copy(w_hbm, weights, sems.at[0])
    up_copy = pltpu.make_async_copy(up_hbm, up, sems.at[1])
    own_copy = pltpu.make_async_copy(own_hbm, ext.at[pl.ds(0, own), :], sems.at[2])
    own_copy.start()
    w_copy.start()
    up_copy.start()
    face = faces[0].shape[0]
    for i, places in enumerate(where):
        mine = [came[...] for came, way in zip(faces, ways) if way[1] == i]
        if len(places) == 2:
            mine = [value.astype(F32) for value in mine]
            even = flags[1 + i] == 0
            mine = [jnp.where(even, mine[1], mine[0]).astype(BF), jnp.where(even, mine[0], mine[1]).astype(BF)]
        for place, value in zip(places, mine):
            ext[pl.ds(own + place * face, face), :] = value
    own_copy.wait()
    lanes = lax.broadcasted_iota(jnp.int32, (step, rows), 1)

    def gather(k, carried):
        at = pl.multiple_of(k * ch, ch)
        for h in range(parts):
            places = [
                col_ref[k, :, b : b + 1] + col_ref[k, :, b + 8 : b + 9]
                for b in range(h * step // block, (h + 1) * step // block)
            ]
            place = jnp.concatenate(places, axis=0).astype(jnp.int32)
            picked = dot(one_hot(lanes == place), ext[...]).astype(BF)
            got[pl.ds(h * step, step), pl.ds(at, ch)] = picked
            got_t[pl.ds(at, ch), pl.ds(h * step, step)] = picked.T
        return carried

    lax.fori_loop(0, taps, gather, 0, unroll=9)
    w_copy.wait()
    up_copy.wait()
    odd = flags[0] > 0
    for h in range(parts):
        part = pl.ds(h * step, step)
        v = dot(got[part, :], weights[...])
        s = jax.nn.sigmoid(v)
        act[part, :] = (v * s).astype(BF)
        g = up[part, :].astype(F32) * (s * (1.0 + v * (1.0 - s)))
        gp[part, :] = g.astype(BF)
        turned[part, :half] = jnp.where(odd, g[:, half:], g[:, :half]).astype(BF)
        turned[part, half:] = jnp.where(odd, g[:, :half], g[:, half:]).astype(BF)
    out_copies = [
        pltpu.make_async_copy(act, act_hbm, sems.at[3]),
        pltpu.make_async_copy(gp, gp_hbm, sems.at[4]),
    ]
    for copy in out_copies:
        copy.start()

    def one(t, carried):
        at = pl.multiple_of(t * ch, ch)
        r = dot(got_t[pl.ds(at, ch), :], turned[...])
        keep[pl.ds(at, ch), :] = r[:, :half]
        give[pl.ds(at, ch), :] = r[:, half:].astype(BF)
        return carried

    middle = taps * ch // 2
    bounds = [0, (taps + 1) // 2, taps]
    for j in range(2):
        lax.fori_loop(bounds[j], bounds[j + 1], one, 0, unroll=2)
        part = pl.ds(j * middle, middle)
        for source, target, sem in ((give, give_hbm[j], 5 + j), (keep, keep_hbm.at[part, :], 7 + j)):
            copy = pltpu.make_async_copy(source.at[part, :], target, sems.at[sem])
            copy.start()
            out_copies.append(copy)
    for copy in out_copies:
        copy.wait()


def forward(ways, flags, col, own_features, faces, weight, upstream):
    taps, block, _ = col.shape
    own, ch = own_features.shape
    where, faced = slots()
    rows = own + faced * faces[0].shape[0]
    like = jax.ShapeDtypeStruct
    return pl.pallas_call(
        lambda *refs: forward_kernel(ways, where, 256, *refs),
        in_specs=[SMEM, VMEM, HBM, HBM, HBM] + [VMEM] * len(faces),
        out_specs=[HBM, HBM, ANY, ANY, ANY],
        out_shape=[
            pltpu.HBM((own, ch), BF),
            pltpu.HBM((own, ch), BF),
            like((taps * ch, ch // 2), F32),
            like((taps * ch // 2, ch // 2), BF),
            like((taps * ch // 2, ch // 2), BF),
        ],
        scratch_shapes=[
            pltpu.VMEM((rows, ch), BF),
            pltpu.VMEM((own, taps * ch), BF),
            pltpu.VMEM((taps * ch, own), BF),
            pltpu.VMEM((taps * ch, ch), BF),
            pltpu.VMEM((own, ch), BF),
            pltpu.VMEM((own, ch), BF),
            pltpu.VMEM((own, ch), BF),
            pltpu.VMEM((own, ch), BF),
            pltpu.VMEM((taps * ch, ch // 2), F32),
            pltpu.VMEM((taps * ch, ch // 2), BF),
            pltpu.SemaphoreType.DMA((11,)),
        ],
        compiler_params=params(36),
        name="forward",
    )(flags, col, hold(own_features), hold(weight.reshape(taps * ch, ch)), hold(upstream), *faces)


def backward_body(start, first, count, step, row_hbm, gp_hbm, w_hbm, before_hbm, row, gp, got, weights, total, sems):
    size, ch = total.shape
    block = row.shape[2]
    parts = gp.shape[0] // block
    row_copy = pltpu.make_async_copy(row_hbm.at[pl.ds(first, count)], row, sems.at[0])
    gp_copy = pltpu.make_async_copy(gp_hbm, gp, sems.at[1])
    row_copy.start()
    gp_copy.start()
    later = [
        pltpu.make_async_copy(w_hbm.at[first + j], weights.at[:, pl.ds(j * ch, ch)], sems.at[3 + j])
        for j in range(count)
    ]
    if before_hbm is not None:
        later.append(pltpu.make_async_copy(before_hbm, total, sems.at[2]))
    for copy in later:
        copy.start()
    row_copy.wait()
    gp_copy.wait()

    def gather(j, carried):
        at = pl.multiple_of(j * ch, ch)
        for r in range(0, size, step):
            lines = lax.broadcasted_iota(jnp.int32, (step, block), 0) + (start + r)
            hots = []
            for h in range(parts):
                place = (row[j, h : h + 1, :] + row[j, h + 8 : h + 9, :]).astype(jnp.int32)
                hots.append(one_hot(lines == place))
            got[pl.ds(r, step), pl.ds(at, ch)] = dot(jnp.concatenate(hots, axis=1), gp[...]).astype(BF)
        return carried

    lax.fori_loop(0, count, gather, 0, unroll=3)
    for copy in later:
        copy.wait()
    for r in range(0, size, step):
        value = dot(got[pl.ds(r, step), :], weights[...], NT)
        total[pl.ds(r, step), :] = value if before_hbm is None else value + total[pl.ds(r, step), :]


def backward_scratch(row, gp, size, count):
    own, ch = gp.shape
    return [
        pltpu.VMEM((count,) + row.shape[1:], F32),
        pltpu.VMEM((own, ch), BF),
        pltpu.VMEM((size, count * ch), BF),
        pltpu.VMEM((ch, count * ch), BF),
        pltpu.VMEM((size, ch), F32),
        pltpu.SemaphoreType.DMA((3 + count,)),
    ]


def faces_kernel(ways, where, start, count, flags, row_hbm, gp_hbm, w_hbm, *rest):
    outs, staged, sems, scratch = rest[: len(ways)], rest[len(ways)], rest[len(ways) + 1], rest[len(ways) + 2 :]
    total = scratch[4]
    face = outs[0].shape[0]
    backward_body(start, 0, count, total.shape[0] // 2, row_hbm, gp_hbm, w_hbm, None, *scratch)
    copies = []
    for j, way in enumerate(ways):
        values = [total[pl.ds(place * face, face), :] for place in where[way[1]]]
        value = towards(flags, way, *values) if len(values) == 2 else values[0]
        staged[j] = value.astype(BF)
        copies.append(pltpu.make_async_copy(staged.at[j], outs[j], sems.at[j]))
        copies[-1].start()
    for copy in copies:
        copy.wait()


def backward_faces(ways, flags, row, gp, weight, face):
    taps = row.shape[0]
    own, ch = gp.shape
    where, faced = slots()
    return pl.pallas_call(
        lambda *refs: faces_kernel(ways, where, own, taps, *refs),
        in_specs=[SMEM, HBM, HBM, HBM],
        out_specs=[HBM] * len(ways),
        out_shape=[pltpu.HBM((face, ch), BF)] * len(ways),
        scratch_shapes=[pltpu.VMEM((len(ways), face, ch), BF), pltpu.SemaphoreType.DMA((len(ways),))]
        + backward_scratch(row, gp, faced * face, taps),
        compiler_params=params(18),
        name="backward_faces",
    )(flags, hold(row), hold(gp), hold(weight))


def own_kernel(first, count, row_hbm, gp_hbm, w_hbm, *rest):
    *before, out_hbm = rest[:-6]
    scratch = rest[-6:]
    backward_body(0, first, count, 384, row_hbm, gp_hbm, w_hbm, before[0] if before else None, *scratch)
    copy = pltpu.make_async_copy(scratch[4], out_hbm, scratch[5].at[2])
    copy.start()
    copy.wait()


def backward_own(row, gp, weight, first, count, before):
    args = [row, gp, weight] + before
    return pl.pallas_call(
        lambda *refs: own_kernel(first, count, *refs),
        in_specs=[HBM] * len(args),
        out_specs=HBM,
        out_shape=pltpu.HBM(gp.shape, F32),
        scratch_shapes=backward_scratch(row, gp, gp.shape[0], count),
        compiler_params=params(14),
        name="backward_own",
    )(*[hold(x) for x in args])


def finish_kernel(ways, first, count, flags, rows_hbm, row_hbm, gp_hbm, w_hbm, before_hbm, *rest):
    faces_hbm, out_ref, rows_ref, faces, sems = rest[: len(ways)], *rest[len(ways) : len(ways) + 4]
    scratch = rest[len(ways) + 4 :]
    copies = [pltpu.make_async_copy(rows_hbm, rows_ref, sems.at[len(ways)])]
    for j in range(len(ways)):
        copies.append(pltpu.make_async_copy(faces_hbm[j], faces.at[j], sems.at[j]))
    for copy in copies:
        copy.start()
    backward_body(0, first, count, 384, row_hbm, gp_hbm, w_hbm, before_hbm, *scratch)
    face = rows_ref.shape[2]
    own = out_ref.shape[0]
    places = lax.broadcasted_iota(jnp.int32, (own, face), 0)
    total = scratch[4][...]
    for copy in copies:
        copy.wait()
    for j, way in enumerate(ways):
        rows = towards(flags, way, rows_ref[2 * way[1]], rows_ref[2 * way[1] + 1])
        total = total + dot(one_hot(places == rows), faces[j])
    out_ref[...] = total.astype(BF)


def finish(ways, flags, rows, row, gp, weight, first, count, before, returned):
    return pl.pallas_call(
        lambda *refs: finish_kernel(ways, first, count, *refs),
        in_specs=[SMEM] + [HBM] * (5 + len(returned)),
        out_specs=VMEM,
        out_shape=jax.ShapeDtypeStruct(gp.shape, BF),
        scratch_shapes=[
            pltpu.VMEM(rows.shape, jnp.int32),
            pltpu.VMEM((len(ways),) + returned[0].shape, BF),
            pltpu.SemaphoreType.DMA((len(ways) + 1,)),
        ]
        + backward_scratch(row, gp, gp.shape[0], count),
        compiler_params=params(16),
        name="finish",
    )(flags, *[hold(x) for x in [rows, row, gp, weight, before] + returned])


def swap(x, axis, bit):
    n = lax.axis_size(axis)
    return lax.ppermute(x, axis, [(j, j ^ (1 << bit)) for j in range(n)])


def side(axis, bit):
    return (lax.axis_index(axis) >> bit) & 1


def place_kernel(size, spots_ref, *refs):
    count = len(refs) - 2
    arrays, out, sem = refs[: count - (count % 2)], refs[-2], refs[-1]
    copies = []
    for a, array in enumerate(arrays):
        blocks = array.shape[0] // size
        for b in range(blocks):
            at = pl.multiple_of(spots_ref[a * blocks + b], 8)
            lane = pl.multiple_of(spots_ref[len(arrays) * blocks + a], 128)
            target = out.at[pl.ds(at, size), pl.ds(lane, array.shape[1])]
            copies.append(pltpu.make_async_copy(array.at[pl.ds(b * size, size), :], target, sem.at[a * blocks + b]))
    for copy in copies:
        copy.start()
    for copy in copies:
        copy.wait()


def place(spots, arrays, size, rows, before):
    blocks = len(arrays) * (arrays[0].shape[0] // size)
    args = list(arrays) + ([] if before is None else [before])
    return pl.pallas_call(
        lambda *refs: place_kernel(size, *refs),
        in_specs=[SMEM] + [ANY] * len(arrays) + [HBM] * (len(args) - len(arrays)),
        out_specs=HBM,
        out_shape=jax.ShapeDtypeStruct((rows, 2 * arrays[0].shape[1]), BF),
        scratch_shapes=[pltpu.SemaphoreType.DMA((blocks,))],
        input_output_aliases={} if before is None else {len(args): 0},
        compiler_params=params(4),
        name="place",
    )(spots, *args)


def reduce_all(keep, give, scaling, beside):
    bits = lambda axis, low: [(axis, b) for b in range(low, lax.axis_size(axis).bit_length() - 1)]
    plane = [bits("gx", 0) + bits("gz", 1), bits("gz", 1) + bits("gx", 0)]
    turns = len(plane[0])
    rows, ch = keep.shape
    terms = [[(keep, i * (rows // 2)), (swap(give[i], "gz", 0), 0)] for i in range(2)]

    def total(i, extra, size):
        out = None
        for array, start in terms[i]:
            value = lax.dynamic_slice_in_dim(array, start + extra, size, 0).astype(F32)
            out = value if out is None else out + value
        return out

    size = rows // 2
    for turn in range(turns):
        size = size // 2
        mine = [side(*plane[i][turn]) for i in range(2)]
        out = [total(0, (1 - mine[0]) * size, size).astype(BF)]
        held = lax.optimization_barrier((out[0], terms[1][-1][0]))
        out, terms[1][-1] = [held[0]], (held[1], terms[1][-1][1])
        out.append(total(1, (1 - mine[1]) * size, size).astype(BF))
        came = beside(out, [swap(out[i], *plane[i][turn]) for i in range(2)])
        for i in range(2):
            terms[i] = [(a, start + mine[i] * size) for a, start in terms[i]] + [(came[i], 0)]
    n = lax.axis_size("gy")
    at = lax.axis_index("gy")
    size = size // n
    slot = lambda s: jnp.concatenate([total(i, ((at + s) % n) * size, size) for i in range(2)], axis=0)
    turn_by = lambda y, s: lax.ppermute(y, "gy", [(j, (j + s) % n) for j in range(n)])
    out = [slot(s).astype(BF) for s in range(1, n)]
    came = beside(out, [turn_by(y, s + 1) for s, y in enumerate(out)])
    final = slot(0)
    for y in came:
        final = final + y.astype(F32)
    mine = (final * scaling).astype(BF)
    came = beside([mine], [turn_by(mine, s) for s in range(1, n)])
    pieces = [jnp.concatenate([y[i * size : (i + 1) * size] for y in [mine] + came], axis=0) for i in range(2)]
    for turn in range(turns - 1, 0, -1):
        came = beside(pieces, [swap(pieces[i], *plane[i][turn]) for i in range(2)])
        pieces = [jnp.concatenate([pieces[i], came[i]], axis=0) for i in range(2)]
    odd = side("gz", 0)
    cross = lambda arrays: [swap(y, "gz", 0) for y in arrays]
    came = beside(pieces, [swap(pieces[i], *plane[i][0]) for i in range(2)])
    twins = cross(pieces)
    sides = [[side(*plane[i][t]) for t in range(turns)] for i in range(2)]
    if size % 8 == 0:
        lanes = jnp.stack([odd, odd, 1 - odd, 1 - odd]) * ch

        def spots(flip):
            out = []
            for i in range(2):
                base = jnp.asarray(i * (rows // 2) + (sides[i][0] ^ flip) * (rows // 4))[None]
                for t in range(1, turns):
                    order = jnp.stack([sides[i][t], 1 - sides[i][t]]) * (rows // (4 << t))
                    base = (base[:, None] + order[None, :]).reshape(-1)
                order = ((at - jnp.arange(n)) % n) * size
                out.append((base[:, None] + order[None, :]).reshape(-1))
            return jnp.concatenate(out + out + [lanes]).astype(jnp.int32)

        half = place(spots(0), pieces + twins, size, rows, None)
        came = lax.optimization_barrier((half, *came))
        half, came = came[0], list(came[1:])
        last = cross(came)
        return place(spots(1), came + last, size, rows, half)
    last = cross(came)

    def ordered(i, first, second):
        x = jnp.concatenate([first, second], axis=0).reshape((2,) * turns + (n, size, ch))
        for t in range(turns):
            x = jnp.where(sides[i][t] == 1, jnp.flip(x, t), x)
        x = jnp.take(x, (at - jnp.arange(n)) % n, axis=turns)
        return x.reshape(rows // 2, ch)

    mine = jnp.concatenate([ordered(i, pieces[i], came[i]) for i in range(2)], axis=0)
    other = jnp.concatenate([ordered(i, twins[i], last[i]) for i in range(2)], axis=0)
    low, high = jnp.where(odd == 1, other, mine), jnp.where(odd == 1, mine, other)
    return jnp.concatenate([low, high], axis=1)


def shards(features, weight, upstream, send_rows, in_rows, out_rows, tap_pair_exists):
    own_features = features[0, 0, 0]
    own, ch = own_features.shape
    single = lambda x: x[0, 0, 0][:, None, :]
    sends = single(send_rows)
    taps = weight.shape[0]
    block = 128
    ways = routes()
    flags = jnp.stack([side("gz", 0)] + [lax.axis_index(a) & 1 for a in AXES]).astype(jnp.int32)
    faces = exchange(send(ways, flags, sends, own_features), ways)
    col, row = invert(
        flags, single(in_rows), single(out_rows), single(tap_pair_exists), sends.shape[2], block
    )
    activated, gp, keep, *give = forward(ways, flags, col, own_features, faces, weight, upstream[0, 0, 0])
    devices = lax.axis_size("gx") * lax.axis_size("gy") * lax.axis_size("gz")
    split = (0, 6, 18)
    state = {"turn": 0, "returned": {}, "grad": []}
    late = [j for j, way in enumerate(ways) if way in ((0, 0), (1, 2))]
    early = [j for j in range(len(ways)) if j not in late]

    def tied(out, work, came):
        held = lax.optimization_barrier((gp, *out))
        made = work(held[0])
        held = lax.optimization_barrier((*made, *came))
        return held[: len(made)], list(held[len(made) :])

    def beside(out, came):
        turn = state["turn"]
        state["turn"] = turn + 1
        if turn == 0:
            work = lambda g: backward_faces(ways, flags, row, g, weight, sends.shape[2])
            state["back"], came = tied(out, work, came)
        elif turn in (1, 2):
            picks = early if turn == 1 else late
            held = lax.optimization_barrier((*[state["back"][j] for j in picks], *out))
            got = exchange(held[: len(picks)], [ways[j] for j in picks])
            held = lax.optimization_barrier((*got, *came))
            for j, face in zip(picks, held):
                state["returned"][j] = face
            came = list(held[len(picks) :])
        if turn in (2, 3):
            first, after = split[turn - 2 : turn]
            work = lambda g: [backward_own(row, g, weight, first, after - first, state["grad"])]
            made, came = tied(out, work, came)
            state["grad"] = [made[0]]
        if turn == 5:
            faces = [state["returned"][j] for j in range(len(ways))]
            first = split[-1]
            work = lambda g: [finish(ways, flags, sends, row, g, weight, first, taps - first, state["grad"][0], faces)]
            (state["done"],), came = tied(out, work, came)
        return came

    grad_weight = reduce_all(keep, give, float(devices * own) ** -0.5, beside).reshape(weight.shape)
    return activated[None, None, None], state["done"][None, None, None], grad_weight


def solution(mesh):
    part = P("gx", "gy", "gz", None, None)
    return jax.shard_map(
        shards,
        mesh=mesh,
        in_specs=(part, P(), part, part, part, part, part),
        out_specs=(part, part, P()),
        check_vma=False,
    )
```

```python
import jax
import jax.numpy as jnp
from jax import lax
from jax.experimental import pallas as pl
from jax.experimental.pallas import tpu as pltpu
from jax.sharding import PartitionSpec as P

BF = jnp.bfloat16
F32 = jnp.float32
NT = (((1,), (1,)), ((), ()))
NN = (((1,), (0,)), ((), ()))
TN = (((0,), (0,)), ((), ()))
AXES = ("gx", "gy", "gz")
MISSING = 2000
VMEM = pl.BlockSpec(memory_space=pltpu.VMEM)
SMEM = pl.BlockSpec(memory_space=pltpu.SMEM)
ANY = pl.BlockSpec(memory_space=pl.ANY)
HBM = pl.BlockSpec(memory_space=pltpu.HBM)


def dot(a, b, dims=NN):
    return lax.dot_general(a, b, dims, preferred_element_type=F32)


def one_hot(mask):
    return jnp.where(mask, jnp.ones((), F32), jnp.zeros((), F32)).astype(BF)


def hold(x):
    return pltpu.with_memory_space_constraint(x, pltpu.HBM)


def params(megabytes):
    return pltpu.CompilerParams(vmem_limit_bytes=megabytes << 20)


def routes():
    out = []
    for i, axis in enumerate(AXES):
        out.append((0, i))
        if lax.axis_size(axis) > 2:
            out.append((1, i))
    return out


def slots():
    out, count = [], 0
    for axis in AXES:
        size = 1 if lax.axis_size(axis) == 2 else 2
        out.append(tuple(range(count, count + size)))
        count += size
    return out, count


def exchange(arrays, ways):
    got = []
    for array, (odd, i) in zip(arrays, ways):
        n = lax.axis_size(AXES[i])
        pairs = [p for j in range(odd, n - 1, 2) for p in ((j, j + 1), (j + 1, j))]
        got.append(lax.ppermute(array, AXES[i], pairs))
    return got


def towards(flags, way, lower, upper):
    odd, i = way
    return jnp.where(flags[1 + i] == odd, upper, lower)


def send_kernel(ways, flags, rows_hbm, own_hbm, *rest):
    outs, (rows_ref, own_ref, sems) = rest[: len(ways)], rest[len(ways) :]
    copies = [
        pltpu.make_async_copy(own_hbm, own_ref, sems.at[0]),
        pltpu.make_async_copy(rows_hbm, rows_ref, sems.at[1]),
    ]
    for copy in copies:
        copy.start()
    for copy in copies:
        copy.wait()
    face = rows_ref.shape[2]
    own = own_ref.shape[0]
    places = lax.broadcasted_iota(jnp.int32, (own, face), 0)
    for out, way in zip(outs, ways):
        rows = towards(flags, way, rows_ref[2 * way[1]], rows_ref[2 * way[1] + 1])
        out[...] = dot(one_hot(places == rows), own_ref[...], TN).astype(BF)


def send(ways, flags, rows, own_features):
    shape = jax.ShapeDtypeStruct((rows.shape[2], own_features.shape[1]), BF)
    return pl.pallas_call(
        lambda *refs: send_kernel(ways, *refs),
        in_specs=[SMEM, HBM, HBM],
        out_specs=[VMEM] * len(ways),
        out_shape=[shape] * len(ways),
        scratch_shapes=[
            pltpu.VMEM(rows.shape, jnp.int32),
            pltpu.VMEM(own_features.shape, BF),
            pltpu.SemaphoreType.DMA((2,)),
        ],
        compiler_params=params(8),
        name="send",
    )(flags, hold(rows), hold(own_features))


def invert_kernel(block, face, pairs, flags, in_hbm, out_hbm, live_hbm, col_ref, row_hbm, tables, row_ref, sems):
    copies = [
        pltpu.make_async_copy(hbm, tables.at[j], sems.at[j])
        for j, hbm in enumerate((in_hbm, out_hbm, live_hbm))
    ]
    for copy in copies:
        copy.start()
    taps, _, own = in_hbm.shape
    lows = lax.broadcasted_iota(jnp.int32, (block, own), 0)
    ranks = lax.broadcasted_iota(jnp.int32, (16, own), 0)
    for copy in copies:
        copy.wait()
    for k in range(taps):
        target = tables[1, k]
        source = tables[0, k]
        live = tables[2, k] > 0
        for i in pairs:
            dead = own + (2 * i + flags[1 + i]) * face
            beyond = source >= dead + face
            live = jnp.logical_and(live, jnp.logical_or(beyond, source < dead))
            source = jnp.where(beyond, source - face, source)
        source = jnp.where(live, source, MISSING)
        high = target // block
        hot = one_hot(lows == target - high * block)
        big = (source // 16) * 16
        spread = jnp.where(ranks == high, big, jnp.where(ranks - 8 == high, source - big, 0))
        spread = spread.astype(F32).astype(BF)
        col = dot(hot, spread, NT)
        col_ref[k] = col
        row_ref[k] = col.T
    copy = pltpu.make_async_copy(row_ref, row_hbm, sems.at[3])
    copy.start()
    copy.wait()


def invert(flags, in_rows, out_rows, live, face, block):
    pairs = [i for i in reversed(range(len(AXES))) if lax.axis_size(AXES[i]) == 2]
    taps, _, own = in_rows.shape
    return pl.pallas_call(
        lambda *refs: invert_kernel(block, face, pairs, *refs),
        in_specs=[SMEM, HBM, HBM, HBM],
        out_specs=[VMEM, HBM],
        out_shape=(
            jax.ShapeDtypeStruct((taps, block, 16), F32),
            pltpu.HBM((taps, 16, block), F32),
        ),
        scratch_shapes=[
            pltpu.VMEM((3, taps, 1, own), jnp.int32),
            pltpu.VMEM((taps, 16, block), F32),
            pltpu.SemaphoreType.DMA((4,)),
        ],
        compiler_params=params(12),
        name="invert",
    )(flags, hold(in_rows), hold(out_rows), hold(live))


def forward_kernel(ways, where, step, flags, col_ref, own_hbm, w_hbm, up_hbm, *rest):
    faces = rest[: len(ways)]
    act_hbm, gp_hbm, keep_hbm, *give_hbm = rest[len(ways) : len(ways) + 5]
    ext, got, got_t, weights, turned, up, act, gp, keep, give, sems = rest[len(ways) + 5 :]
    taps = col_ref.shape[0]
    own, ch = up.shape
    rows = ext.shape[0]
    half = ch // 2
    parts = own // step
    block = col_ref.shape[1]
    w_copy = pltpu.make_async_copy(w_hbm, weights, sems.at[0])
    up_copy = pltpu.make_async_copy(up_hbm, up, sems.at[1])
    own_copy = pltpu.make_async_copy(own_hbm, ext.at[pl.ds(0, own), :], sems.at[2])
    own_copy.start()
    w_copy.start()
    up_copy.start()
    face = faces[0].shape[0]
    for i, places in enumerate(where):
        mine = [came[...] for came, way in zip(faces, ways) if way[1] == i]
        if len(places) == 2:
            mine = [value.astype(F32) for value in mine]
            even = flags[1 + i] == 0
            mine = [jnp.where(even, mine[1], mine[0]).astype(BF), jnp.where(even, mine[0], mine[1]).astype(BF)]
        for place, value in zip(places, mine):
            ext[pl.ds(own + place * face, face), :] = value
    own_copy.wait()
    lanes = lax.broadcasted_iota(jnp.int32, (step, rows), 1)

    def gather(k, carried):
        at = pl.multiple_of(k * ch, ch)
        for h in range(parts):
            places = [
                col_ref[k, :, b : b + 1] + col_ref[k, :, b + 8 : b + 9]
                for b in range(h * step // block, (h + 1) * step // block)
            ]
            place = jnp.concatenate(places, axis=0).astype(jnp.int32)
            picked = dot(one_hot(lanes == place), ext[...]).astype(BF)
            got[pl.ds(h * step, step), pl.ds(at, ch)] = picked
            got_t[pl.ds(at, ch), pl.ds(h * step, step)] = picked.T
        return carried

    lax.fori_loop(0, taps, gather, 0, unroll=9)
    w_copy.wait()
    up_copy.wait()
    odd = flags[0] > 0
    for h in range(parts):
        part = pl.ds(h * step, step)
        v = dot(got[part, :], weights[...])
        s = jax.nn.sigmoid(v)
        act[part, :] = (v * s).astype(BF)
        g = up[part, :].astype(F32) * (s * (1.0 + v * (1.0 - s)))
        gp[part, :] = g.astype(BF)
        turned[part, :half] = jnp.where(odd, g[:, half:], g[:, :half]).astype(BF)
        turned[part, half:] = jnp.where(odd, g[:, :half], g[:, half:]).astype(BF)
    out_copies = [
        pltpu.make_async_copy(act, act_hbm, sems.at[3]),
        pltpu.make_async_copy(gp, gp_hbm, sems.at[4]),
    ]
    for copy in out_copies:
        copy.start()

    def one(t, carried):
        at = pl.multiple_of(t * ch, ch)
        r = dot(got_t[pl.ds(at, ch), :], turned[...])
        keep[pl.ds(at, ch), :] = r[:, :half]
        give[pl.ds(at, ch), :] = r[:, half:].astype(BF)
        return carried

    middle = taps * ch // 2
    bounds = [0, (taps + 1) // 2, taps]
    for j in range(2):
        lax.fori_loop(bounds[j], bounds[j + 1], one, 0, unroll=7 if (bounds[j + 1] - bounds[j]) % 7 == 0 else True)
        part = pl.ds(j * middle, middle)
        for source, target, sem in ((give, give_hbm[j], 5 + j), (keep, keep_hbm.at[part, :], 7 + j)):
            copy = pltpu.make_async_copy(source.at[part, :], target, sems.at[sem])
            copy.start()
            out_copies.append(copy)
    for copy in out_copies:
        copy.wait()


def forward(ways, flags, col, own_features, faces, weight, upstream):
    taps, block, _ = col.shape
    own, ch = own_features.shape
    where, faced = slots()
    rows = own + faced * faces[0].shape[0]
    like = jax.ShapeDtypeStruct
    return pl.pallas_call(
        lambda *refs: forward_kernel(ways, where, 256, *refs),
        in_specs=[SMEM, VMEM, HBM, HBM, HBM] + [VMEM] * len(faces),
        out_specs=[HBM, HBM, ANY, ANY, ANY],
        out_shape=[
            pltpu.HBM((own, ch), BF),
            pltpu.HBM((own, ch), BF),
            like((taps * ch, ch // 2), F32),
            like((taps * ch // 2, ch // 2), BF),
            like((taps * ch // 2, ch // 2), BF),
        ],
        scratch_shapes=[
            pltpu.VMEM((rows, ch), BF),
            pltpu.VMEM((own, taps * ch), BF),
            pltpu.VMEM((taps * ch, own), BF),
            pltpu.VMEM((taps * ch, ch), BF),
            pltpu.VMEM((own, ch), BF),
            pltpu.VMEM((own, ch), BF),
            pltpu.VMEM((own, ch), BF),
            pltpu.VMEM((own, ch), BF),
            pltpu.VMEM((taps * ch, ch // 2), F32),
            pltpu.VMEM((taps * ch, ch // 2), BF),
            pltpu.SemaphoreType.DMA((11,)),
        ],
        compiler_params=params(36),
        name="forward",
    )(flags, col, hold(own_features), hold(weight.reshape(taps * ch, ch)), hold(upstream), *faces)


def backward_body(start, first, count, step, row_hbm, gp_hbm, w_hbm, before_hbm, row, gp, got, weights, total, sems):
    size, ch = total.shape
    block = row.shape[2]
    parts = gp.shape[0] // block
    row_copy = pltpu.make_async_copy(row_hbm.at[pl.ds(first, count)], row, sems.at[0])
    gp_copy = pltpu.make_async_copy(gp_hbm, gp, sems.at[1])
    row_copy.start()
    gp_copy.start()
    later = [
        pltpu.make_async_copy(w_hbm.at[first + j], weights.at[:, pl.ds(j * ch, ch)], sems.at[3 + j])
        for j in range(count)
    ]
    if before_hbm is not None:
        later.append(pltpu.make_async_copy(before_hbm, total, sems.at[2]))
    for copy in later:
        copy.start()
    row_copy.wait()
    gp_copy.wait()

    def gather(j, carried):
        at = pl.multiple_of(j * ch, ch)
        for r in range(0, size, step):
            lines = lax.broadcasted_iota(jnp.int32, (step, block), 0) + (start + r)
            hots = []
            for h in range(parts):
                place = (row[j, h : h + 1, :] + row[j, h + 8 : h + 9, :]).astype(jnp.int32)
                hots.append(one_hot(lines == place))
            got[pl.ds(r, step), pl.ds(at, ch)] = dot(jnp.concatenate(hots, axis=1), gp[...]).astype(BF)
        return carried

    lax.fori_loop(0, count, gather, 0, unroll=next(u for u in (9, 6, 3, 1) if count % u == 0))
    for copy in later:
        copy.wait()
    for r in range(0, size, step):
        value = dot(got[pl.ds(r, step), :], weights[...], NT)
        total[pl.ds(r, step), :] = value if before_hbm is None else value + total[pl.ds(r, step), :]


def backward_scratch(row, gp, size, count):
    own, ch = gp.shape
    return [
        pltpu.VMEM((count,) + row.shape[1:], F32),
        pltpu.VMEM((own, ch), BF),
        pltpu.VMEM((size, count * ch), BF),
        pltpu.VMEM((ch, count * ch), BF),
        pltpu.VMEM((size, ch), F32),
        pltpu.SemaphoreType.DMA((3 + count,)),
    ]


def faces_kernel(ways, where, start, count, flags, row_hbm, gp_hbm, w_hbm, *rest):
    outs, staged, sems, scratch = rest[: len(ways)], rest[len(ways)], rest[len(ways) + 1], rest[len(ways) + 2 :]
    total = scratch[4]
    face = outs[0].shape[0]
    backward_body(start, 0, count, total.shape[0] // 2, row_hbm, gp_hbm, w_hbm, None, *scratch)
    copies = []
    for j, way in enumerate(ways):
        values = [total[pl.ds(place * face, face), :] for place in where[way[1]]]
        value = towards(flags, way, *values) if len(values) == 2 else values[0]
        staged[j] = value.astype(BF)
        copies.append(pltpu.make_async_copy(staged.at[j], outs[j], sems.at[j]))
        copies[-1].start()
    for copy in copies:
        copy.wait()


def backward_faces(ways, flags, row, gp, weight, face):
    taps = row.shape[0]
    own, ch = gp.shape
    where, faced = slots()
    return pl.pallas_call(
        lambda *refs: faces_kernel(ways, where, own, taps, *refs),
        in_specs=[SMEM, HBM, HBM, HBM],
        out_specs=[HBM] * len(ways),
        out_shape=[pltpu.HBM((face, ch), BF)] * len(ways),
        scratch_shapes=[pltpu.VMEM((len(ways), face, ch), BF), pltpu.SemaphoreType.DMA((len(ways),))]
        + backward_scratch(row, gp, faced * face, taps),
        compiler_params=params(18),
        name="backward_faces",
    )(flags, hold(row), hold(gp), hold(weight))


def own_kernel(first, count, row_hbm, gp_hbm, w_hbm, *rest):
    *before, out_hbm = rest[:-6]
    scratch = rest[-6:]
    backward_body(0, first, count, 384, row_hbm, gp_hbm, w_hbm, before[0] if before else None, *scratch)
    copy = pltpu.make_async_copy(scratch[4], out_hbm, scratch[5].at[2])
    copy.start()
    copy.wait()


def backward_own(row, gp, weight, first, count, before):
    args = [row, gp, weight] + before
    return pl.pallas_call(
        lambda *refs: own_kernel(first, count, *refs),
        in_specs=[HBM] * len(args),
        out_specs=HBM,
        out_shape=pltpu.HBM(gp.shape, F32),
        scratch_shapes=backward_scratch(row, gp, gp.shape[0], count),
        compiler_params=params(14),
        name="backward_own",
    )(*[hold(x) for x in args])


def finish_kernel(ways, first, count, flags, rows_hbm, row_hbm, gp_hbm, w_hbm, before_hbm, *rest):
    faces_hbm, out_ref, rows_ref, faces, sems = rest[: len(ways)], *rest[len(ways) : len(ways) + 4]
    scratch = rest[len(ways) + 4 :]
    copies = [pltpu.make_async_copy(rows_hbm, rows_ref, sems.at[len(ways)])]
    for j in range(len(ways)):
        copies.append(pltpu.make_async_copy(faces_hbm[j], faces.at[j], sems.at[j]))
    for copy in copies:
        copy.start()
    backward_body(0, first, count, 384, row_hbm, gp_hbm, w_hbm, before_hbm, *scratch)
    face = rows_ref.shape[2]
    own = out_ref.shape[0]
    places = lax.broadcasted_iota(jnp.int32, (own, face), 0)
    total = scratch[4][...]
    for copy in copies:
        copy.wait()
    for j, way in enumerate(ways):
        rows = towards(flags, way, rows_ref[2 * way[1]], rows_ref[2 * way[1] + 1])
        total = total + dot(one_hot(places == rows), faces[j])
    out_ref[...] = total.astype(BF)


def finish(ways, flags, rows, row, gp, weight, first, count, before, returned):
    return pl.pallas_call(
        lambda *refs: finish_kernel(ways, first, count, *refs),
        in_specs=[SMEM] + [HBM] * (5 + len(returned)),
        out_specs=VMEM,
        out_shape=jax.ShapeDtypeStruct(gp.shape, BF),
        scratch_shapes=[
            pltpu.VMEM(rows.shape, jnp.int32),
            pltpu.VMEM((len(ways),) + returned[0].shape, BF),
            pltpu.SemaphoreType.DMA((len(ways) + 1,)),
        ]
        + backward_scratch(row, gp, gp.shape[0], count),
        compiler_params=params(16),
        name="finish",
    )(flags, *[hold(x) for x in [rows, row, gp, weight, before] + returned])


def swap(x, axis, bit):
    n = lax.axis_size(axis)
    return lax.ppermute(x, axis, [(j, j ^ (1 << bit)) for j in range(n)])


def side(axis, bit):
    return (lax.axis_index(axis) >> bit) & 1


def place_kernel(size, spots_ref, *refs):
    count = len(refs) - 2
    arrays, out, sem = refs[: count - (count % 2)], refs[-2], refs[-1]
    copies = []
    for a, array in enumerate(arrays):
        blocks = array.shape[0] // size
        for b in range(blocks):
            at = pl.multiple_of(spots_ref[a * blocks + b], 8)
            lane = pl.multiple_of(spots_ref[len(arrays) * blocks + a], 128)
            target = out.at[pl.ds(at, size), pl.ds(lane, array.shape[1])]
            copies.append(pltpu.make_async_copy(array.at[pl.ds(b * size, size), :], target, sem.at[a * blocks + b]))
    for copy in copies:
        copy.start()
    for copy in copies:
        copy.wait()


def place(spots, arrays, size, rows, before):
    blocks = len(arrays) * (arrays[0].shape[0] // size)
    args = list(arrays) + ([] if before is None else [before])
    return pl.pallas_call(
        lambda *refs: place_kernel(size, *refs),
        in_specs=[SMEM] + [ANY] * len(arrays) + [HBM] * (len(args) - len(arrays)),
        out_specs=HBM,
        out_shape=jax.ShapeDtypeStruct((rows, 2 * arrays[0].shape[1]), BF),
        scratch_shapes=[pltpu.SemaphoreType.DMA((blocks,))],
        input_output_aliases={} if before is None else {len(args): 0},
        compiler_params=params(4),
        name="place",
    )(spots, *args)


def reduce_all(keep, give, scaling, beside):
    bits = lambda axis, low: [(axis, b) for b in range(low, lax.axis_size(axis).bit_length() - 1)]
    plane = [bits("gx", 0) + bits("gz", 1), bits("gz", 1) + bits("gx", 0)]
    turns = len(plane[0])
    rows, ch = keep.shape
    terms = [[(keep, i * (rows // 2)), (swap(give[i], "gz", 0), 0)] for i in range(2)]

    def total(i, extra, size):
        out = None
        for array, start in terms[i]:
            value = lax.dynamic_slice_in_dim(array, start + extra, size, 0).astype(F32)
            out = value if out is None else out + value
        return out

    size = rows // 2
    for turn in range(turns):
        size = size // 2
        mine = [side(*plane[i][turn]) for i in range(2)]
        out = [total(i, (1 - mine[i]) * size, size).astype(BF) for i in range(2)]
        came = beside(out, [swap(out[i], *plane[i][turn]) for i in range(2)])
        for i in range(2):
            terms[i] = [(a, start + mine[i] * size) for a, start in terms[i]] + [(came[i], 0)]
    n = lax.axis_size("gy")
    at = lax.axis_index("gy")
    size = size // n
    slot = lambda s: jnp.concatenate([total(i, ((at + s) % n) * size, size) for i in range(2)], axis=0)
    turn_by = lambda y, s: lax.ppermute(y, "gy", [(j, (j + s) % n) for j in range(n)])
    out = [slot(s).astype(BF) for s in range(1, n)]
    came = beside(out, [turn_by(y, s + 1) for s, y in enumerate(out)])
    final = slot(0)
    for y in came:
        final = final + y.astype(F32)
    mine = (final * scaling).astype(BF)
    came = beside([mine], [turn_by(mine, s) for s in range(1, n)])
    pieces = [jnp.concatenate([y[i * size : (i + 1) * size] for y in [mine] + came], axis=0) for i in range(2)]
    for turn in range(turns - 1, 0, -1):
        came = beside(pieces, [swap(pieces[i], *plane[i][turn]) for i in range(2)])
        pieces = [jnp.concatenate([pieces[i], came[i]], axis=0) for i in range(2)]
    odd = side("gz", 0)
    cross = lambda arrays: [swap(y, "gz", 0) for y in arrays]
    came = beside(pieces, [swap(pieces[i], *plane[i][0]) for i in range(2)])
    twins = cross(pieces)
    sides = [[side(*plane[i][t]) for t in range(turns)] for i in range(2)]
    if size % 8 == 0:
        lanes = jnp.stack([odd, odd, 1 - odd, 1 - odd]) * ch

        def spots(flip):
            out = []
            for i in range(2):
                base = jnp.asarray(i * (rows // 2) + (sides[i][0] ^ flip) * (rows // 4))[None]
                for t in range(1, turns):
                    order = jnp.stack([sides[i][t], 1 - sides[i][t]]) * (rows // (4 << t))
                    base = (base[:, None] + order[None, :]).reshape(-1)
                order = ((at - jnp.arange(n)) % n) * size
                out.append((base[:, None] + order[None, :]).reshape(-1))
            return jnp.concatenate(out + out + [lanes]).astype(jnp.int32)

        half = place(spots(0), pieces + twins, size, rows, None)
        last = cross(came)
        return place(spots(1), came + last, size, rows, half)
    last = cross(came)

    def ordered(i, first, second):
        x = jnp.concatenate([first, second], axis=0).reshape((2,) * turns + (n, size, ch))
        for t in range(turns):
            x = jnp.where(sides[i][t] == 1, jnp.flip(x, t), x)
        x = jnp.take(x, (at - jnp.arange(n)) % n, axis=turns)
        return x.reshape(rows // 2, ch)

    mine = jnp.concatenate([ordered(i, pieces[i], came[i]) for i in range(2)], axis=0)
    other = jnp.concatenate([ordered(i, twins[i], last[i]) for i in range(2)], axis=0)
    low, high = jnp.where(odd == 1, other, mine), jnp.where(odd == 1, mine, other)
    return jnp.concatenate([low, high], axis=1)


def shards(features, weight, upstream, send_rows, in_rows, out_rows, tap_pair_exists):
    own_features = features[0, 0, 0]
    own, ch = own_features.shape
    single = lambda x: x[0, 0, 0][:, None, :]
    sends = single(send_rows)
    taps = weight.shape[0]
    block = 128
    ways = routes()
    flags = jnp.stack([side("gz", 0)] + [lax.axis_index(a) & 1 for a in AXES]).astype(jnp.int32)
    faces = exchange(send(ways, flags, sends, own_features), ways)
    col, row = invert(
        flags, single(in_rows), single(out_rows), single(tap_pair_exists), sends.shape[2], block
    )
    activated, gp, keep, *give = forward(ways, flags, col, own_features, faces, weight, upstream[0, 0, 0])
    devices = lax.axis_size("gx") * lax.axis_size("gy") * lax.axis_size("gz")
    split = (0, 3, 15)
    state = {"turn": 0, "returned": {}, "grad": []}
    late = [j for j, way in enumerate(ways) if way in ((0, 0), (1, 2))]
    early = [j for j in range(len(ways)) if j not in late]

    def tied(out, work, came):
        held = lax.optimization_barrier((gp, *out))
        made = work(held[0])
        held = lax.optimization_barrier((*made, *came))
        return held[: len(made)], list(held[len(made) :])

    def beside(out, came):
        turn = state["turn"]
        state["turn"] = turn + 1
        if turn == 0:
            work = lambda g: backward_faces(ways, flags, row, g, weight, sends.shape[2])
            state["back"], came = tied(out, work, came)
        elif turn in (1, 2):
            picks = early if turn == 1 else late
            held = lax.optimization_barrier((*[state["back"][j] for j in picks], *out))
            got = exchange(held[: len(picks)], [ways[j] for j in picks])
            held = lax.optimization_barrier((*got, *came))
            for j, face in zip(picks, held):
                state["returned"][j] = face
            came = list(held[len(picks) :])
        if turn in (2, 3):
            first, after = split[turn - 2 : turn]
            work = lambda g: [backward_own(row, g, weight, first, after - first, state["grad"])]
            made, came = tied(out, work, came)
            state["grad"] = [made[0]]
        if turn == 5:
            faces = [state["returned"][j] for j in range(len(ways))]
            first = split[-1]
            work = lambda g: [finish(ways, flags, sends, row, g, weight, first, taps - first, state["grad"][0], faces)]
            (state["done"],), came = tied(out, work, came)
        return came

    grad_weight = reduce_all(keep, give, float(devices * own) ** -0.5, beside).reshape(weight.shape)
    return activated[None, None, None], state["done"][None, None, None], grad_weight


def solution(mesh):
    part = P("gx", "gy", "gz", None, None)
    return jax.shard_map(
        shards,
        mesh=mesh,
        in_specs=(part, P(), part, part, part, part, part),
        out_specs=(part, part, P()),
        check_vma=False,
    )
```

```python
import jax
import jax.numpy as jnp
from jax import lax
from jax.experimental import pallas as pl
from jax.experimental.pallas import tpu as pltpu
from jax.sharding import PartitionSpec as P

BF = jnp.bfloat16
F32 = jnp.float32
NT = (((1,), (1,)), ((), ()))
NN = (((1,), (0,)), ((), ()))
TN = (((0,), (0,)), ((), ()))
AXES = ("gx", "gy", "gz")
MISSING = 2000
VMEM = pl.BlockSpec(memory_space=pltpu.VMEM)
SMEM = pl.BlockSpec(memory_space=pltpu.SMEM)
ANY = pl.BlockSpec(memory_space=pl.ANY)
HBM = pl.BlockSpec(memory_space=pltpu.HBM)


def dot(a, b, dims=NN):
    return lax.dot_general(a, b, dims, preferred_element_type=F32)


def one_hot(mask):
    return jnp.where(mask, jnp.ones((), F32), jnp.zeros((), F32)).astype(BF)


def hold(x):
    return pltpu.with_memory_space_constraint(x, pltpu.HBM)


def params(megabytes):
    return pltpu.CompilerParams(vmem_limit_bytes=megabytes << 20)


def routes():
    out = []
    for i, axis in enumerate(AXES):
        out.append((0, i))
        if lax.axis_size(axis) > 2:
            out.append((1, i))
    return out


def slots():
    out, count = [], 0
    for axis in AXES:
        size = 1 if lax.axis_size(axis) == 2 else 2
        out.append(tuple(range(count, count + size)))
        count += size
    return out, count


def exchange(arrays, ways):
    got = []
    for array, (odd, i) in zip(arrays, ways):
        n = lax.axis_size(AXES[i])
        pairs = [p for j in range(odd, n - 1, 2) for p in ((j, j + 1), (j + 1, j))]
        got.append(lax.ppermute(array, AXES[i], pairs))
    return got


def towards(flags, way, lower, upper):
    odd, i = way
    return jnp.where(flags[1 + i] == odd, upper, lower)


def send_kernel(ways, flags, rows_hbm, own_hbm, *rest):
    outs, (rows_ref, own_ref, sems) = rest[: len(ways)], rest[len(ways) :]
    copies = [
        pltpu.make_async_copy(own_hbm, own_ref, sems.at[0]),
        pltpu.make_async_copy(rows_hbm, rows_ref, sems.at[1]),
    ]
    for copy in copies:
        copy.start()
    for copy in copies:
        copy.wait()
    face = rows_ref.shape[2]
    own = own_ref.shape[0]
    places = lax.broadcasted_iota(jnp.int32, (own, face), 0)
    for out, way in zip(outs, ways):
        rows = towards(flags, way, rows_ref[2 * way[1]], rows_ref[2 * way[1] + 1])
        out[...] = dot(one_hot(places == rows), own_ref[...], TN).astype(BF)


def send(ways, flags, rows, own_features):
    shape = jax.ShapeDtypeStruct((rows.shape[2], own_features.shape[1]), BF)
    return pl.pallas_call(
        lambda *refs: send_kernel(ways, *refs),
        in_specs=[SMEM, HBM, HBM],
        out_specs=[VMEM] * len(ways),
        out_shape=[shape] * len(ways),
        scratch_shapes=[
            pltpu.VMEM(rows.shape, jnp.int32),
            pltpu.VMEM(own_features.shape, BF),
            pltpu.SemaphoreType.DMA((2,)),
        ],
        compiler_params=params(8),
        name="send",
    )(flags, hold(rows), hold(own_features))


def invert_kernel(block, face, pairs, flags, in_ref, out_ref, live_ref, col_ref, row_hbm, row_ref, sem):
    taps, _, own = in_ref.shape
    lows = lax.broadcasted_iota(jnp.int32, (block, own), 0)
    ranks = lax.broadcasted_iota(jnp.int32, (16, own), 0)
    for k in range(taps):
        target = out_ref[k]
        source = in_ref[k]
        live = live_ref[k] > 0
        for i in pairs:
            dead = own + (2 * i + flags[1 + i]) * face
            beyond = source >= dead + face
            live = jnp.logical_and(live, jnp.logical_or(beyond, source < dead))
            source = jnp.where(beyond, source - face, source)
        source = jnp.where(live, source, MISSING)
        high = target // block
        hot = one_hot(lows == target - high * block)
        big = (source // 16) * 16
        spread = jnp.where(ranks == high, big, jnp.where(ranks - 8 == high, source - big, 0))
        spread = spread.astype(F32).astype(BF)
        col = dot(hot, spread, NT)
        col_ref[k] = col
        row_ref[k] = col.T
    copy = pltpu.make_async_copy(row_ref, row_hbm, sem)
    copy.start()
    copy.wait()


def invert(flags, in_rows, out_rows, live, face, block):
    pairs = [i for i in reversed(range(len(AXES))) if lax.axis_size(AXES[i]) == 2]
    taps, _, own = in_rows.shape
    return pl.pallas_call(
        lambda *refs: invert_kernel(block, face, pairs, *refs),
        in_specs=[SMEM, VMEM, VMEM, VMEM],
        out_specs=[VMEM, HBM],
        out_shape=(
            jax.ShapeDtypeStruct((taps, block, 16), F32),
            pltpu.HBM((taps, 16, block), F32),
        ),
        scratch_shapes=[
            pltpu.VMEM((taps, 16, block), F32),
            pltpu.SemaphoreType.DMA,
        ],
        compiler_params=params(12),
        name="invert",
    )(flags, in_rows, out_rows, live)


def forward_kernel(ways, where, step, flags, col_ref, own_hbm, w_hbm, up_hbm, *rest):
    faces = rest[: len(ways)]
    act_hbm, gp_hbm, keep_hbm, *give_hbm = rest[len(ways) : len(ways) + 5]
    ext, got, got_t, weights, turned, up, act, gp, keep, give, sems = rest[len(ways) + 5 :]
    taps = col_ref.shape[0]
    own, ch = up.shape
    rows = ext.shape[0]
    half = ch // 2
    parts = own // step
    block = col_ref.shape[1]
    w_copy = pltpu.make_async_copy(w_hbm, weights, sems.at[0])
    up_copy = pltpu.make_async_copy(up_hbm, up, sems.at[1])
    own_copy = pltpu.make_async_copy(own_hbm, ext.at[pl.ds(0, own), :], sems.at[2])
    own_copy.start()
    w_copy.start()
    up_copy.start()
    face = faces[0].shape[0]
    for i, places in enumerate(where):
        mine = [came[...] for came, way in zip(faces, ways) if way[1] == i]
        if len(places) == 2:
            mine = [value.astype(F32) for value in mine]
            even = flags[1 + i] == 0
            mine = [jnp.where(even, mine[1], mine[0]).astype(BF), jnp.where(even, mine[0], mine[1]).astype(BF)]
        for place, value in zip(places, mine):
            ext[pl.ds(own + place * face, face), :] = value
    own_copy.wait()
    lanes = lax.broadcasted_iota(jnp.int32, (step, rows), 1)

    def gather(k, carried):
        at = pl.multiple_of(k * ch, ch)
        for h in range(parts):
            places = [
                col_ref[k, :, b : b + 1] + col_ref[k, :, b + 8 : b + 9]
                for b in range(h * step // block, (h + 1) * step // block)
            ]
            place = jnp.concatenate(places, axis=0).astype(jnp.int32)
            picked = dot(one_hot(lanes == place), ext[...]).astype(BF)
            got[pl.ds(h * step, step), pl.ds(at, ch)] = picked
            got_t[pl.ds(at, ch), pl.ds(h * step, step)] = picked.T
        return carried

    lax.fori_loop(0, taps, gather, 0, unroll=9)
    w_copy.wait()
    up_copy.wait()
    odd = flags[0] > 0
    for h in range(parts):
        part = pl.ds(h * step, step)
        v = dot(got[part, :], weights[...])
        s = jax.nn.sigmoid(v)
        act[part, :] = (v * s).astype(BF)
        g = up[part, :].astype(F32) * (s * (1.0 + v * (1.0 - s)))
        gp[part, :] = g.astype(BF)
        turned[part, :half] = jnp.where(odd, g[:, half:], g[:, :half]).astype(BF)
        turned[part, half:] = jnp.where(odd, g[:, :half], g[:, half:]).astype(BF)
    out_copies = [
        pltpu.make_async_copy(act, act_hbm, sems.at[3]),
        pltpu.make_async_copy(gp, gp_hbm, sems.at[4]),
    ]
    for copy in out_copies:
        copy.start()

    def one(t, carried):
        at = pl.multiple_of(t * ch, ch)
        r = dot(got_t[pl.ds(at, ch), :], turned[...])
        keep[pl.ds(at, ch), :] = r[:, :half]
        give[pl.ds(at, ch), :] = r[:, half:].astype(BF)
        return carried

    middle = taps * ch // 2
    bounds = [0, (taps + 1) // 2, taps]
    for j in range(2):
        lax.fori_loop(bounds[j], bounds[j + 1], one, 0, unroll=7 if (bounds[j + 1] - bounds[j]) % 7 == 0 else True)
        part = pl.ds(j * middle, middle)
        for source, target, sem in ((give, give_hbm[j], 5 + j), (keep, keep_hbm.at[part, :], 7 + j)):
            copy = pltpu.make_async_copy(source.at[part, :], target, sems.at[sem])
            copy.start()
            out_copies.append(copy)
    for copy in out_copies:
        copy.wait()


def forward(ways, flags, col, own_features, faces, weight, upstream):
    taps, block, _ = col.shape
    own, ch = own_features.shape
    where, faced = slots()
    rows = own + faced * faces[0].shape[0]
    like = jax.ShapeDtypeStruct
    return pl.pallas_call(
        lambda *refs: forward_kernel(ways, where, 256, *refs),
        in_specs=[SMEM, VMEM, HBM, HBM, HBM] + [VMEM] * len(faces),
        out_specs=[HBM, HBM, ANY, ANY, ANY],
        out_shape=[
            pltpu.HBM((own, ch), BF),
            pltpu.HBM((own, ch), BF),
            like((taps * ch, ch // 2), F32),
            like((taps * ch // 2, ch // 2), BF),
            like((taps * ch // 2, ch // 2), BF),
        ],
        scratch_shapes=[
            pltpu.VMEM((rows, ch), BF),
            pltpu.VMEM((own, taps * ch), BF),
            pltpu.VMEM((taps * ch, own), BF),
            pltpu.VMEM((taps * ch, ch), BF),
            pltpu.VMEM((own, ch), BF),
            pltpu.VMEM((own, ch), BF),
            pltpu.VMEM((own, ch), BF),
            pltpu.VMEM((own, ch), BF),
            pltpu.VMEM((taps * ch, ch // 2), F32),
            pltpu.VMEM((taps * ch, ch // 2), BF),
            pltpu.SemaphoreType.DMA((11,)),
        ],
        compiler_params=params(36),
        name="forward",
    )(flags, col, hold(own_features), hold(weight.reshape(taps * ch, ch)), hold(upstream), *faces)


def backward_body(start, first, count, step, row_hbm, gp_hbm, w_hbm, before_hbm, row, gp, got, weights, total, sems):
    size, ch = total.shape
    block = row.shape[2]
    parts = gp.shape[0] // block
    row_copy = pltpu.make_async_copy(row_hbm.at[pl.ds(first, count)], row, sems.at[0])
    gp_copy = pltpu.make_async_copy(gp_hbm, gp, sems.at[1])
    row_copy.start()
    gp_copy.start()
    later = [
        pltpu.make_async_copy(w_hbm.at[first + j], weights.at[:, pl.ds(j * ch, ch)], sems.at[3 + j])
        for j in range(count)
    ]
    if before_hbm is not None:
        later.append(pltpu.make_async_copy(before_hbm, total, sems.at[2]))
    for copy in later:
        copy.start()
    row_copy.wait()
    gp_copy.wait()

    def gather(j, carried):
        at = pl.multiple_of(j * ch, ch)
        for r in range(0, size, step):
            lines = lax.broadcasted_iota(jnp.int32, (step, block), 0) + (start + r)
            hots = []
            for h in range(parts):
                place = (row[j, h : h + 1, :] + row[j, h + 8 : h + 9, :]).astype(jnp.int32)
                hots.append(one_hot(lines == place))
            got[pl.ds(r, step), pl.ds(at, ch)] = dot(jnp.concatenate(hots, axis=1), gp[...]).astype(BF)
        return carried

    lax.fori_loop(0, count, gather, 0, unroll=next(u for u in (9, 6, 5, 3, 1) if count % u == 0))
    for copy in later:
        copy.wait()
    for r in range(0, size, step):
        value = dot(got[pl.ds(r, step), :], weights[...], NT)
        total[pl.ds(r, step), :] = value if before_hbm is None else value + total[pl.ds(r, step), :]


def backward_scratch(row, gp, size, count):
    own, ch = gp.shape
    return [
        pltpu.VMEM((count,) + row.shape[1:], F32),
        pltpu.VMEM((own, ch), BF),
        pltpu.VMEM((size, count * ch), BF),
        pltpu.VMEM((ch, count * ch), BF),
        pltpu.VMEM((size, ch), F32),
        pltpu.SemaphoreType.DMA((3 + count,)),
    ]


def faces_kernel(ways, where, start, count, flags, row_hbm, gp_hbm, w_hbm, *rest):
    outs, staged, sems, scratch = rest[: len(ways)], rest[len(ways)], rest[len(ways) + 1], rest[len(ways) + 2 :]
    total = scratch[4]
    face = outs[0].shape[0]
    backward_body(start, 0, count, total.shape[0] // 2, row_hbm, gp_hbm, w_hbm, None, *scratch)
    copies = []
    for j, way in enumerate(ways):
        values = [total[pl.ds(place * face, face), :] for place in where[way[1]]]
        value = towards(flags, way, *values) if len(values) == 2 else values[0]
        staged[j] = value.astype(BF)
        copies.append(pltpu.make_async_copy(staged.at[j], outs[j], sems.at[j]))
        copies[-1].start()
    for copy in copies:
        copy.wait()


def backward_faces(ways, flags, row, gp, weight, face):
    taps = row.shape[0]
    own, ch = gp.shape
    where, faced = slots()
    return pl.pallas_call(
        lambda *refs: faces_kernel(ways, where, own, taps, *refs),
        in_specs=[SMEM, HBM, HBM, HBM],
        out_specs=[HBM] * len(ways),
        out_shape=[pltpu.HBM((face, ch), BF)] * len(ways),
        scratch_shapes=[pltpu.VMEM((len(ways), face, ch), BF), pltpu.SemaphoreType.DMA((len(ways),))]
        + backward_scratch(row, gp, faced * face, taps),
        compiler_params=params(18),
        name="backward_faces",
    )(flags, hold(row), hold(gp), hold(weight))


def own_kernel(first, count, row_hbm, gp_hbm, w_hbm, *rest):
    *before, out_hbm = rest[:-6]
    scratch = rest[-6:]
    backward_body(0, first, count, 384, row_hbm, gp_hbm, w_hbm, before[0] if before else None, *scratch)
    copy = pltpu.make_async_copy(scratch[4], out_hbm, scratch[5].at[2])
    copy.start()
    copy.wait()


def backward_own(row, gp, weight, first, count, before):
    args = [row, gp, weight] + before
    return pl.pallas_call(
        lambda *refs: own_kernel(first, count, *refs),
        in_specs=[HBM] * len(args),
        out_specs=HBM,
        out_shape=pltpu.HBM(gp.shape, F32),
        scratch_shapes=backward_scratch(row, gp, gp.shape[0], count),
        compiler_params=params(14),
        name="backward_own",
    )(*[hold(x) for x in args])


def finish_kernel(ways, first, count, flags, rows_hbm, row_hbm, gp_hbm, w_hbm, before_hbm, *rest):
    faces_hbm, out_ref, rows_ref, faces, sems = rest[: len(ways)], *rest[len(ways) : len(ways) + 4]
    scratch = rest[len(ways) + 4 :]
    copies = [pltpu.make_async_copy(rows_hbm, rows_ref, sems.at[len(ways)])]
    for j in range(len(ways)):
        copies.append(pltpu.make_async_copy(faces_hbm[j], faces.at[j], sems.at[j]))
    for copy in copies:
        copy.start()
    backward_body(0, first, count, 384, row_hbm, gp_hbm, w_hbm, before_hbm, *scratch)
    face = rows_ref.shape[2]
    own = out_ref.shape[0]
    places = lax.broadcasted_iota(jnp.int32, (own, face), 0)
    total = scratch[4][...]
    for copy in copies:
        copy.wait()
    for j, way in enumerate(ways):
        rows = towards(flags, way, rows_ref[2 * way[1]], rows_ref[2 * way[1] + 1])
        total = total + dot(one_hot(places == rows), faces[j])
    out_ref[...] = total.astype(BF)


def finish(ways, flags, rows, row, gp, weight, first, count, before, returned):
    return pl.pallas_call(
        lambda *refs: finish_kernel(ways, first, count, *refs),
        in_specs=[SMEM] + [HBM] * (5 + len(returned)),
        out_specs=VMEM,
        out_shape=jax.ShapeDtypeStruct(gp.shape, BF),
        scratch_shapes=[
            pltpu.VMEM(rows.shape, jnp.int32),
            pltpu.VMEM((len(ways),) + returned[0].shape, BF),
            pltpu.SemaphoreType.DMA((len(ways) + 1,)),
        ]
        + backward_scratch(row, gp, gp.shape[0], count),
        compiler_params=params(16),
        name="finish",
    )(flags, *[hold(x) for x in [rows, row, gp, weight, before] + returned])


def swap(x, axis, bit):
    n = lax.axis_size(axis)
    return lax.ppermute(x, axis, [(j, j ^ (1 << bit)) for j in range(n)])


def side(axis, bit):
    return (lax.axis_index(axis) >> bit) & 1


def place_kernel(size, turns, n, flip, spots, *refs):
    arrays, out, sem = refs[:4], refs[-2], refs[-1]
    half, ch = out.shape[0] // 2, out.shape[1] // 2
    at, odd = spots[2 * turns], spots[2 * turns + 1]
    copies = []
    for a, array in enumerate(arrays):
        i, twin = a % 2, a // 2
        side_of = lambda t, r: jnp.bitwise_xor(spots[i * turns + t], r)
        lane = pl.multiple_of((odd if twin == 0 else 1 - odd) * ch, 128)
        for b in range(array.shape[0] // size):
            s, rest = b % n, b // n
            row = i * half + side_of(0, flip) * (half // 2)
            for t in range(turns - 1, 0, -1):
                row = row + side_of(t, rest % 2) * (half >> (t + 1))
                rest = rest // 2
            row = row + jnp.where(at >= s, at - s, at - s + n) * size
            target = out.at[pl.ds(pl.multiple_of(row, 8), size), pl.ds(lane, ch)]
            copies.append(pltpu.make_async_copy(array.at[pl.ds(b * size, size), :], target, sem.at[len(copies)]))
            copies[-1].start()
    for copy in copies:
        copy.wait()


def place(spots, arrays, size, turns, rows, flip, before):
    blocks = len(arrays) * (arrays[0].shape[0] // size)
    n = lax.axis_size("gy")
    args = list(arrays) + ([] if before is None else [before])
    return pl.pallas_call(
        lambda *refs: place_kernel(size, turns, n, flip, *refs),
        in_specs=[SMEM] + [ANY] * len(arrays) + [HBM] * (len(args) - len(arrays)),
        out_specs=HBM,
        out_shape=jax.ShapeDtypeStruct((rows, 2 * arrays[0].shape[1]), BF),
        scratch_shapes=[pltpu.SemaphoreType.DMA((blocks,))],
        input_output_aliases={} if before is None else {len(args): 0},
        compiler_params=params(4),
        name="place",
    )(spots, *args)


def reduce_all(keep, give, scaling, beside):
    bits = lambda axis, low: [(axis, b) for b in range(low, lax.axis_size(axis).bit_length() - 1)]
    plane = [bits("gx", 0) + bits("gz", 1), bits("gz", 1) + bits("gx", 0)]
    turns = len(plane[0])
    rows, ch = keep.shape
    sides = [[side(*plane[i][t]) for t in range(turns)] for i in range(2)]
    terms = [[(keep, i * (rows // 2)), (swap(give[i], "gz", 0), 0)] for i in range(2)]

    def total(i, extra, size):
        out = None
        for array, start in terms[i]:
            value = lax.dynamic_slice_in_dim(array, start + extra, size, 0).astype(F32)
            out = value if out is None else out + value
        return out

    size = rows // 2
    for turn in range(turns):
        size = size // 2
        mine = [side(*plane[i][turn]) for i in range(2)]
        out = [total(i, (1 - mine[i]) * size, size).astype(BF) for i in range(2)]
        came = beside(out, [swap(out[i], *plane[i][turn]) for i in range(2)])
        for i in range(2):
            terms[i] = [(a, start + mine[i] * size) for a, start in terms[i]] + [(came[i], 0)]
    n = lax.axis_size("gy")
    at = lax.axis_index("gy")
    size = size // n
    slot = lambda s: jnp.concatenate([total(i, ((at + s) % n) * size, size) for i in range(2)], axis=0)
    turn_by = lambda y, s: lax.ppermute(y, "gy", [(j, (j + s) % n) for j in range(n)])
    out = [slot(s).astype(BF) for s in range(1, n)]
    came = beside(out, [turn_by(y, s + 1) for s, y in enumerate(out)])
    final = slot(0)
    for y in came:
        final = final + y.astype(F32)
    mine = (final * scaling).astype(BF)
    came = beside([mine], [turn_by(mine, s) for s in range(1, n)])
    pieces = [jnp.concatenate([y[i * size : (i + 1) * size] for y in [mine] + came], axis=0) for i in range(2)]
    for turn in range(turns - 1, 0, -1):
        came = beside(pieces, [swap(pieces[i], *plane[i][turn]) for i in range(2)])
        pieces = [jnp.concatenate([pieces[i], came[i]], axis=0) for i in range(2)]
    odd = side("gz", 0)
    cross = lambda arrays: [swap(y, "gz", 0) for y in arrays]
    came = beside(pieces, [swap(pieces[i], *plane[i][0]) for i in range(2)])
    twins = cross(pieces)
    if size % 8 == 0:
        spots = jnp.stack(sides[0] + sides[1] + [at, odd]).astype(jnp.int32)
        half = place(spots, pieces + twins, size, turns, rows, 0, None)
        last = cross(came)
        return place(spots, came + last, size, turns, rows, 1, half)
    last = cross(came)

    def ordered(i, first, second):
        x = jnp.concatenate([first, second], axis=0).reshape((2,) * turns + (n, size, ch))
        for t in range(turns):
            x = jnp.where(sides[i][t] == 1, jnp.flip(x, t), x)
        x = jnp.take(x, (at - jnp.arange(n)) % n, axis=turns)
        return x.reshape(rows // 2, ch)

    mine = jnp.concatenate([ordered(i, pieces[i], came[i]) for i in range(2)], axis=0)
    other = jnp.concatenate([ordered(i, twins[i], last[i]) for i in range(2)], axis=0)
    low, high = jnp.where(odd == 1, other, mine), jnp.where(odd == 1, mine, other)
    return jnp.concatenate([low, high], axis=1)


def shards(features, weight, upstream, send_rows, in_rows, out_rows, tap_pair_exists):
    own_features = features[0, 0, 0]
    own, ch = own_features.shape
    single = lambda x: x[0, 0, 0][:, None, :]
    sends = single(send_rows)
    taps = weight.shape[0]
    block = 128
    ways = routes()
    flags = jnp.stack([side("gz", 0)] + [lax.axis_index(a) & 1 for a in AXES]).astype(jnp.int32)
    faces = exchange(send(ways, flags, sends, own_features), ways)
    col, row = invert(
        flags, single(in_rows), single(out_rows), single(tap_pair_exists), sends.shape[2], block
    )
    activated, gp, keep, *give = forward(ways, flags, col, own_features, faces, weight, upstream[0, 0, 0])
    devices = lax.axis_size("gx") * lax.axis_size("gy") * lax.axis_size("gz")
    split = (0, 3, 18)
    state = {"turn": 0, "returned": {}, "grad": []}
    late = [j for j, way in enumerate(ways) if way in ((0, 0), (1, 2))]
    early = [j for j in range(len(ways)) if j not in late]

    def tied(out, work, came):
        held = lax.optimization_barrier((gp, *out))
        made = work(held[0])
        held = lax.optimization_barrier((*made, *came))
        return held[: len(made)], list(held[len(made) :])

    def beside(out, came):
        turn = state["turn"]
        state["turn"] = turn + 1
        if turn == 0:
            work = lambda g: backward_faces(ways, flags, row, g, weight, sends.shape[2])
            state["back"], came = tied(out, work, came)
        elif turn in (1, 2):
            picks = early if turn == 1 else late
            held = lax.optimization_barrier((*[state["back"][j] for j in picks], *out))
            got = exchange(held[: len(picks)], [ways[j] for j in picks])
            held = lax.optimization_barrier((*got, *came))
            for j, face in zip(picks, held):
                state["returned"][j] = face
            came = list(held[len(picks) :])
        if turn in (2, 3):
            first, after = split[turn - 2 : turn]
            work = lambda g: [backward_own(row, g, weight, first, after - first, state["grad"])]
            made, came = tied(out, work, came)
            state["grad"] = [made[0]]
        if turn == 5:
            faces = [state["returned"][j] for j in range(len(ways))]
            first = split[-1]
            work = lambda g: [finish(ways, flags, sends, row, g, weight, first, taps - first, state["grad"][0], faces)]
            (state["done"],), came = tied(out, work, came)
        return came

    grad_weight = reduce_all(keep, give, float(devices * own) ** -0.5, beside).reshape(weight.shape)
    return activated[None, None, None], state["done"][None, None, None], grad_weight


def solution(mesh):
    part = P("gx", "gy", "gz", None, None)
    return jax.shard_map(
        shards,
        mesh=mesh,
        in_specs=(part, P(), part, part, part, part, part),
        out_specs=(part, part, P()),
        check_vma=False,
    )
```

```python
import jax
import jax.numpy as jnp
from jax import lax
from jax.experimental import pallas as pl
from jax.experimental.pallas import tpu as pltpu
from jax.sharding import PartitionSpec as P

BF = jnp.bfloat16
F32 = jnp.float32
NT = (((1,), (1,)), ((), ()))
NN = (((1,), (0,)), ((), ()))
TN = (((0,), (0,)), ((), ()))
AXES = ("gx", "gy", "gz")
MISSING = 2000
VMEM = pl.BlockSpec(memory_space=pltpu.VMEM)
SMEM = pl.BlockSpec(memory_space=pltpu.SMEM)
ANY = pl.BlockSpec(memory_space=pl.ANY)
HBM = pl.BlockSpec(memory_space=pltpu.HBM)


def dot(a, b, dims=NN):
    return lax.dot_general(a, b, dims, preferred_element_type=F32)


def one_hot(mask):
    return jnp.where(mask, jnp.ones((), F32), jnp.zeros((), F32)).astype(BF)


def hold(x):
    return pltpu.with_memory_space_constraint(x, pltpu.HBM)


def params(megabytes):
    return pltpu.CompilerParams(vmem_limit_bytes=megabytes << 20)


def routes():
    out = []
    for i, axis in enumerate(AXES):
        out.append((0, i))
        if lax.axis_size(axis) > 2:
            out.append((1, i))
    return out


def slots():
    out, count = [], 0
    for axis in AXES:
        size = 1 if lax.axis_size(axis) == 2 else 2
        out.append(tuple(range(count, count + size)))
        count += size
    return out, count


def exchange(arrays, ways):
    got = []
    for array, (odd, i) in zip(arrays, ways):
        n = lax.axis_size(AXES[i])
        pairs = [p for j in range(odd, n - 1, 2) for p in ((j, j + 1), (j + 1, j))]
        got.append(lax.ppermute(array, AXES[i], pairs))
    return got


def towards(flags, way, lower, upper):
    odd, i = way
    return jnp.where(flags[1 + i] == odd, upper, lower)


def send_kernel(ways, flags, rows_hbm, own_hbm, *rest):
    outs, (rows_ref, own_ref, sems) = rest[: len(ways)], rest[len(ways) :]
    copies = [
        pltpu.make_async_copy(own_hbm, own_ref, sems.at[0]),
        pltpu.make_async_copy(rows_hbm, rows_ref, sems.at[1]),
    ]
    for copy in copies:
        copy.start()
    for copy in copies:
        copy.wait()
    face = rows_ref.shape[2]
    own = own_ref.shape[0]
    places = lax.broadcasted_iota(jnp.int32, (own, face), 0)
    for out, way in zip(outs, ways):
        rows = towards(flags, way, rows_ref[2 * way[1]], rows_ref[2 * way[1] + 1])
        out[...] = dot(one_hot(places == rows), own_ref[...], TN).astype(BF)


def send(ways, flags, rows, own_features):
    shape = jax.ShapeDtypeStruct((rows.shape[2], own_features.shape[1]), BF)
    return pl.pallas_call(
        lambda *refs: send_kernel(ways, *refs),
        in_specs=[SMEM, HBM, HBM],
        out_specs=[VMEM] * len(ways),
        out_shape=[shape] * len(ways),
        scratch_shapes=[
            pltpu.VMEM(rows.shape, jnp.int32),
            pltpu.VMEM(own_features.shape, BF),
            pltpu.SemaphoreType.DMA((2,)),
        ],
        compiler_params=params(8),
        name="send",
    )(flags, hold(rows), hold(own_features))


def invert_kernel(block, face, pairs, flags, in_hbm, out_hbm, live_hbm, col_ref, row_hbm, tables, row_ref, sems):
    copies = [
        pltpu.make_async_copy(hbm, tables.at[j], sems.at[j])
        for j, hbm in enumerate((in_hbm, out_hbm, live_hbm))
    ]
    for copy in copies:
        copy.start()
    taps, _, own = in_hbm.shape
    lows = lax.broadcasted_iota(jnp.int32, (block, own), 0)
    ranks = lax.broadcasted_iota(jnp.int32, (16, own), 0)
    for copy in copies:
        copy.wait()
    for k in range(taps):
        target = tables[1, k]
        source = tables[0, k]
        live = tables[2, k] > 0
        for i in pairs:
            dead = own + (2 * i + flags[1 + i]) * face
            beyond = source >= dead + face
            live = jnp.logical_and(live, jnp.logical_or(beyond, source < dead))
            source = jnp.where(beyond, source - face, source)
        source = jnp.where(live, source, MISSING)
        high = target // block
        hot = one_hot(lows == target - high * block)
        big = (source // 16) * 16
        spread = jnp.where(ranks == high, big, jnp.where(ranks - 8 == high, source - big, 0))
        spread = spread.astype(F32).astype(BF)
        col = dot(hot, spread, NT)
        col_ref[k] = col
        row_ref[k] = col.T
    copy = pltpu.make_async_copy(row_ref, row_hbm, sems.at[3])
    copy.start()
    copy.wait()


def invert(flags, in_rows, out_rows, live, face, block):
    pairs = [i for i in reversed(range(len(AXES))) if lax.axis_size(AXES[i]) == 2]
    taps, _, own = in_rows.shape
    return pl.pallas_call(
        lambda *refs: invert_kernel(block, face, pairs, *refs),
        in_specs=[SMEM, HBM, HBM, HBM],
        out_specs=[VMEM, HBM],
        out_shape=(
            jax.ShapeDtypeStruct((taps, block, 16), F32),
            pltpu.HBM((taps, 16, block), F32),
        ),
        scratch_shapes=[
            pltpu.VMEM((3, taps, 1, own), jnp.int32),
            pltpu.VMEM((taps, 16, block), F32),
            pltpu.SemaphoreType.DMA((4,)),
        ],
        compiler_params=params(12),
        name="invert",
    )(flags, hold(in_rows), hold(out_rows), hold(live))


def forward_kernel(ways, where, step, flags, col_ref, own_hbm, w_hbm, up_hbm, *rest):
    faces = rest[: len(ways)]
    act_hbm, gp_hbm, keep_hbm, *give_hbm = rest[len(ways) : len(ways) + 5]
    ext, got, got_t, weights, turned, up, act, gp, keep, give, sems = rest[len(ways) + 5 :]
    taps = col_ref.shape[0]
    own, ch = up.shape
    rows = ext.shape[0]
    half = ch // 2
    parts = own // step
    block = col_ref.shape[1]
    w_copy = pltpu.make_async_copy(w_hbm, weights, sems.at[0])
    up_copy = pltpu.make_async_copy(up_hbm, up, sems.at[1])
    own_copy = pltpu.make_async_copy(own_hbm, ext.at[pl.ds(0, own), :], sems.at[2])
    own_copy.start()
    w_copy.start()
    up_copy.start()
    face = faces[0].shape[0]
    for i, places in enumerate(where):
        mine = [came[...] for came, way in zip(faces, ways) if way[1] == i]
        if len(places) == 2:
            mine = [value.astype(F32) for value in mine]
            even = flags[1 + i] == 0
            mine = [jnp.where(even, mine[1], mine[0]).astype(BF), jnp.where(even, mine[0], mine[1]).astype(BF)]
        for place, value in zip(places, mine):
            ext[pl.ds(own + place * face, face), :] = value
    own_copy.wait()
    lanes = lax.broadcasted_iota(jnp.int32, (step, rows), 1)

    def gather(k, carried):
        at = pl.multiple_of(k * ch, ch)
        for h in range(parts):
            places = [
                col_ref[k, :, b : b + 1] + col_ref[k, :, b + 8 : b + 9]
                for b in range(h * step // block, (h + 1) * step // block)
            ]
            place = jnp.concatenate(places, axis=0).astype(jnp.int32)
            picked = dot(one_hot(lanes == place), ext[...]).astype(BF)
            got[pl.ds(h * step, step), pl.ds(at, ch)] = picked
            got_t[pl.ds(at, ch), pl.ds(h * step, step)] = picked.T
        return carried

    lax.fori_loop(0, taps, gather, 0, unroll=9)
    w_copy.wait()
    up_copy.wait()
    odd = flags[0] > 0
    for h in range(parts):
        part = pl.ds(h * step, step)
        v = dot(got[part, :], weights[...])
        s = jax.nn.sigmoid(v)
        act[part, :] = (v * s).astype(BF)
        g = up[part, :].astype(F32) * (s * (1.0 + v * (1.0 - s)))
        gp[part, :] = g.astype(BF)
        turned[part, :half] = jnp.where(odd, g[:, half:], g[:, :half]).astype(BF)
        turned[part, half:] = jnp.where(odd, g[:, :half], g[:, half:]).astype(BF)
    out_copies = [
        pltpu.make_async_copy(act, act_hbm, sems.at[3]),
        pltpu.make_async_copy(gp, gp_hbm, sems.at[4]),
    ]
    for copy in out_copies:
        copy.start()

    def one(t, carried):
        at = pl.multiple_of(t * ch, ch)
        r = dot(got_t[pl.ds(at, ch), :], turned[...])
        keep[pl.ds(at, ch), :] = r[:, :half]
        give[pl.ds(at, ch), :] = r[:, half:].astype(BF)
        return carried

    middle = taps * ch // 2
    bounds = [0, (taps + 1) // 2, taps]
    for j in range(2):
        lax.fori_loop(bounds[j], bounds[j + 1], one, 0, unroll=7 if (bounds[j + 1] - bounds[j]) % 7 == 0 else True)
        part = pl.ds(j * middle, middle)
        for source, target, sem in ((give, give_hbm[j], 5 + j), (keep, keep_hbm.at[part, :], 7 + j)):
            copy = pltpu.make_async_copy(source.at[part, :], target, sems.at[sem])
            copy.start()
            out_copies.append(copy)
    for copy in out_copies:
        copy.wait()


def forward(ways, flags, col, own_features, faces, weight, upstream):
    taps, block, _ = col.shape
    own, ch = own_features.shape
    where, faced = slots()
    rows = own + faced * faces[0].shape[0]
    like = jax.ShapeDtypeStruct
    return pl.pallas_call(
        lambda *refs: forward_kernel(ways, where, 256, *refs),
        in_specs=[SMEM, VMEM, HBM, HBM, HBM] + [VMEM] * len(faces),
        out_specs=[HBM, HBM, ANY, ANY, ANY],
        out_shape=[
            pltpu.HBM((own, ch), BF),
            pltpu.HBM((own, ch), BF),
            like((taps * ch, ch // 2), F32),
            like((taps * ch // 2, ch // 2), BF),
            like((taps * ch // 2, ch // 2), BF),
        ],
        scratch_shapes=[
            pltpu.VMEM((rows, ch), BF),
            pltpu.VMEM((own, taps * ch), BF),
            pltpu.VMEM((taps * ch, own), BF),
            pltpu.VMEM((taps * ch, ch), BF),
            pltpu.VMEM((own, ch), BF),
            pltpu.VMEM((own, ch), BF),
            pltpu.VMEM((own, ch), BF),
            pltpu.VMEM((own, ch), BF),
            pltpu.VMEM((taps * ch, ch // 2), F32),
            pltpu.VMEM((taps * ch, ch // 2), BF),
            pltpu.SemaphoreType.DMA((11,)),
        ],
        compiler_params=params(36),
        name="forward",
    )(flags, col, hold(own_features), hold(weight.reshape(taps * ch, ch)), hold(upstream), *faces)


def backward_body(start, first, count, step, row_hbm, gp_hbm, w_hbm, before_hbm, row, gp, got, weights, total, sems):
    size, ch = total.shape
    block = row.shape[2]
    parts = gp.shape[0] // block
    row_copy = pltpu.make_async_copy(row_hbm.at[pl.ds(first, count)], row, sems.at[0])
    gp_copy = pltpu.make_async_copy(gp_hbm, gp, sems.at[1])
    row_copy.start()
    gp_copy.start()
    later = [
        pltpu.make_async_copy(w_hbm.at[first + j], weights.at[:, pl.ds(j * ch, ch)], sems.at[3 + j])
        for j in range(count)
    ]
    if before_hbm is not None:
        later.append(pltpu.make_async_copy(before_hbm, total, sems.at[2]))
    for copy in later:
        copy.start()
    row_copy.wait()
    gp_copy.wait()

    def gather(j, carried):
        at = pl.multiple_of(j * ch, ch)
        for r in range(0, size, step):
            lines = lax.broadcasted_iota(jnp.int32, (step, block), 0) + (start + r)
            hots = []
            for h in range(parts):
                place = (row[j, h : h + 1, :] + row[j, h + 8 : h + 9, :]).astype(jnp.int32)
                hots.append(one_hot(lines == place))
            got[pl.ds(r, step), pl.ds(at, ch)] = dot(jnp.concatenate(hots, axis=1), gp[...]).astype(BF)
        return carried

    lax.fori_loop(0, count, gather, 0, unroll=next(u for u in (9, 6, 5, 3, 1) if count % u == 0))
    for copy in later:
        copy.wait()
    for r in range(0, size, step):
        value = dot(got[pl.ds(r, step), :], weights[...], NT)
        total[pl.ds(r, step), :] = value if before_hbm is None else value + total[pl.ds(r, step), :]


def backward_scratch(row, gp, size, count):
    own, ch = gp.shape
    return [
        pltpu.VMEM((count,) + row.shape[1:], F32),
        pltpu.VMEM((own, ch), BF),
        pltpu.VMEM((size, count * ch), BF),
        pltpu.VMEM((ch, count * ch), BF),
        pltpu.VMEM((size, ch), F32),
        pltpu.SemaphoreType.DMA((3 + count,)),
    ]


def faces_kernel(ways, where, start, count, flags, row_hbm, gp_hbm, w_hbm, *rest):
    outs, staged, sems, scratch = rest[: len(ways)], rest[len(ways)], rest[len(ways) + 1], rest[len(ways) + 2 :]
    total = scratch[4]
    face = outs[0].shape[0]
    backward_body(start, 0, count, total.shape[0] // 2, row_hbm, gp_hbm, w_hbm, None, *scratch)
    copies = []
    for j, way in enumerate(ways):
        values = [total[pl.ds(place * face, face), :] for place in where[way[1]]]
        value = towards(flags, way, *values) if len(values) == 2 else values[0]
        staged[j] = value.astype(BF)
        copies.append(pltpu.make_async_copy(staged.at[j], outs[j], sems.at[j]))
        copies[-1].start()
    for copy in copies:
        copy.wait()


def backward_faces(ways, flags, row, gp, weight, face):
    taps = row.shape[0]
    own, ch = gp.shape
    where, faced = slots()
    return pl.pallas_call(
        lambda *refs: faces_kernel(ways, where, own, taps, *refs),
        in_specs=[SMEM, HBM, HBM, HBM],
        out_specs=[HBM] * len(ways),
        out_shape=[pltpu.HBM((face, ch), BF)] * len(ways),
        scratch_shapes=[pltpu.VMEM((len(ways), face, ch), BF), pltpu.SemaphoreType.DMA((len(ways),))]
        + backward_scratch(row, gp, faced * face, taps),
        compiler_params=params(18),
        name="backward_faces",
    )(flags, hold(row), hold(gp), hold(weight))


def own_kernel(first, count, row_hbm, gp_hbm, w_hbm, *rest):
    *before, out_hbm = rest[:-6]
    scratch = rest[-6:]
    backward_body(0, first, count, 384, row_hbm, gp_hbm, w_hbm, before[0] if before else None, *scratch)
    copy = pltpu.make_async_copy(scratch[4], out_hbm, scratch[5].at[2])
    copy.start()
    copy.wait()


def backward_own(row, gp, weight, first, count, before):
    args = [row, gp, weight] + before
    return pl.pallas_call(
        lambda *refs: own_kernel(first, count, *refs),
        in_specs=[HBM] * len(args),
        out_specs=HBM,
        out_shape=pltpu.HBM(gp.shape, F32),
        scratch_shapes=backward_scratch(row, gp, gp.shape[0], count),
        compiler_params=params(14),
        name="backward_own",
    )(*[hold(x) for x in args])


def finish_kernel(ways, first, count, flags, rows_hbm, row_hbm, gp_hbm, w_hbm, before_hbm, *rest):
    faces_hbm, out_ref, rows_ref, faces, sems = rest[: len(ways)], *rest[len(ways) : len(ways) + 4]
    scratch = rest[len(ways) + 4 :]
    copies = [pltpu.make_async_copy(rows_hbm, rows_ref, sems.at[len(ways)])]
    for j in range(len(ways)):
        copies.append(pltpu.make_async_copy(faces_hbm[j], faces.at[j], sems.at[j]))
    for copy in copies:
        copy.start()
    backward_body(0, first, count, 384, row_hbm, gp_hbm, w_hbm, before_hbm, *scratch)
    face = rows_ref.shape[2]
    own = out_ref.shape[0]
    places = lax.broadcasted_iota(jnp.int32, (own, face), 0)
    total = scratch[4][...]
    for copy in copies:
        copy.wait()
    for j, way in enumerate(ways):
        rows = towards(flags, way, rows_ref[2 * way[1]], rows_ref[2 * way[1] + 1])
        total = total + dot(one_hot(places == rows), faces[j])
    out_ref[...] = total.astype(BF)


def finish(ways, flags, rows, row, gp, weight, first, count, before, returned):
    return pl.pallas_call(
        lambda *refs: finish_kernel(ways, first, count, *refs),
        in_specs=[SMEM] + [HBM] * (5 + len(returned)),
        out_specs=VMEM,
        out_shape=jax.ShapeDtypeStruct(gp.shape, BF),
        scratch_shapes=[
            pltpu.VMEM(rows.shape, jnp.int32),
            pltpu.VMEM((len(ways),) + returned[0].shape, BF),
            pltpu.SemaphoreType.DMA((len(ways) + 1,)),
        ]
        + backward_scratch(row, gp, gp.shape[0], count),
        compiler_params=params(16),
        name="finish",
    )(flags, *[hold(x) for x in [rows, row, gp, weight, before] + returned])


def swap(x, axis, bit):
    n = lax.axis_size(axis)
    return lax.ppermute(x, axis, [(j, j ^ (1 << bit)) for j in range(n)])


def side(axis, bit):
    return (lax.axis_index(axis) >> bit) & 1


def place_kernel(size, turns, n, flip, spots, *refs):
    arrays, out, sem = refs[:4], refs[-2], refs[-1]
    half, ch = out.shape[0] // 2, out.shape[1] // 2
    at, odd = spots[2 * turns], spots[2 * turns + 1]
    copies = []
    for a, array in enumerate(arrays):
        i, twin = a % 2, a // 2
        side_of = lambda t, r: jnp.bitwise_xor(spots[i * turns + t], r)
        lane = pl.multiple_of((odd if twin == 0 else 1 - odd) * ch, 128)
        for b in range(array.shape[0] // size):
            s, rest = b % n, b // n
            row = i * half + side_of(0, flip) * (half // 2)
            for t in range(turns - 1, 0, -1):
                row = row + side_of(t, rest % 2) * (half >> (t + 1))
                rest = rest // 2
            row = row + jnp.where(at >= s, at - s, at - s + n) * size
            target = out.at[pl.ds(pl.multiple_of(row, 8), size), pl.ds(lane, ch)]
            copies.append(pltpu.make_async_copy(array.at[pl.ds(b * size, size), :], target, sem.at[len(copies)]))
            copies[-1].start()
    for copy in copies:
        copy.wait()


def place(spots, arrays, size, turns, rows, flip, before):
    blocks = len(arrays) * (arrays[0].shape[0] // size)
    n = lax.axis_size("gy")
    args = list(arrays) + ([] if before is None else [before])
    return pl.pallas_call(
        lambda *refs: place_kernel(size, turns, n, flip, *refs),
        in_specs=[SMEM] + [ANY] * len(arrays) + [HBM] * (len(args) - len(arrays)),
        out_specs=HBM,
        out_shape=jax.ShapeDtypeStruct((rows, 2 * arrays[0].shape[1]), BF),
        scratch_shapes=[pltpu.SemaphoreType.DMA((blocks,))],
        input_output_aliases={} if before is None else {len(args): 0},
        compiler_params=params(4),
        name="place",
    )(spots, *args)


def reduce_all(keep, give, scaling, beside):
    bits = lambda axis, low: [(axis, b) for b in range(low, lax.axis_size(axis).bit_length() - 1)]
    plane = [bits("gx", 0) + bits("gz", 1), bits("gz", 1) + bits("gx", 0)]
    turns = len(plane[0])
    rows, ch = keep.shape
    sides = [[side(*plane[i][t]) for t in range(turns)] for i in range(2)]
    terms = [[(keep, i * (rows // 2)), (swap(give[i], "gz", 0), 0)] for i in range(2)]

    def total(i, extra, size):
        out = None
        for array, start in terms[i]:
            value = lax.dynamic_slice_in_dim(array, start + extra, size, 0).astype(F32)
            out = value if out is None else out + value
        return out

    size = rows // 2
    for turn in range(turns):
        size = size // 2
        mine = [side(*plane[i][turn]) for i in range(2)]
        out = [total(i, (1 - mine[i]) * size, size).astype(BF) for i in range(2)]
        came = beside(out, [swap(out[i], *plane[i][turn]) for i in range(2)])
        for i in range(2):
            terms[i] = [(a, start + mine[i] * size) for a, start in terms[i]] + [(came[i], 0)]
    n = lax.axis_size("gy")
    at = lax.axis_index("gy")
    size = size // n
    slot = lambda s: jnp.concatenate([total(i, ((at + s) % n) * size, size) for i in range(2)], axis=0)
    turn_by = lambda y, s: lax.ppermute(y, "gy", [(j, (j + s) % n) for j in range(n)])
    out = [slot(s).astype(BF) for s in range(1, n)]
    came = beside(out, [turn_by(y, s + 1) for s, y in enumerate(out)])
    final = slot(0)
    for y in came:
        final = final + y.astype(F32)
    mine = (final * scaling).astype(BF)
    came = beside([mine], [turn_by(mine, s) for s in range(1, n)])
    pieces = [jnp.concatenate([y[i * size : (i + 1) * size] for y in [mine] + came], axis=0) for i in range(2)]
    for turn in range(turns - 1, 0, -1):
        came = beside(pieces, [swap(pieces[i], *plane[i][turn]) for i in range(2)])
        pieces = [jnp.concatenate([pieces[i], came[i]], axis=0) for i in range(2)]
    odd = side("gz", 0)
    cross = lambda arrays: [swap(y, "gz", 0) for y in arrays]
    came = beside(pieces, [swap(pieces[i], *plane[i][0]) for i in range(2)])
    twins = cross(pieces)
    if size % 8 == 0:
        spots = jnp.stack(sides[0] + sides[1] + [at, odd]).astype(jnp.int32)
        half = place(spots, pieces + twins, size, turns, rows, 0, None)
        last = cross(came)
        return place(spots, came + last, size, turns, rows, 1, half)
    last = cross(came)

    def ordered(i, first, second):
        x = jnp.concatenate([first, second], axis=0).reshape((2,) * turns + (n, size, ch))
        for t in range(turns):
            x = jnp.where(sides[i][t] == 1, jnp.flip(x, t), x)
        x = jnp.take(x, (at - jnp.arange(n)) % n, axis=turns)
        return x.reshape(rows // 2, ch)

    mine = jnp.concatenate([ordered(i, pieces[i], came[i]) for i in range(2)], axis=0)
    other = jnp.concatenate([ordered(i, twins[i], last[i]) for i in range(2)], axis=0)
    low, high = jnp.where(odd == 1, other, mine), jnp.where(odd == 1, mine, other)
    return jnp.concatenate([low, high], axis=1)


def shards(features, weight, upstream, send_rows, in_rows, out_rows, tap_pair_exists):
    own_features = features[0, 0, 0]
    own, ch = own_features.shape
    single = lambda x: x[0, 0, 0][:, None, :]
    sends = single(send_rows)
    taps = weight.shape[0]
    block = 128
    ways = routes()
    flags = jnp.stack([side("gz", 0)] + [lax.axis_index(a) & 1 for a in AXES]).astype(jnp.int32)
    faces = exchange(send(ways, flags, sends, own_features), ways)
    col, row = invert(
        flags, single(in_rows), single(out_rows), single(tap_pair_exists), sends.shape[2], block
    )
    activated, gp, keep, *give = forward(ways, flags, col, own_features, faces, weight, upstream[0, 0, 0])
    devices = lax.axis_size("gx") * lax.axis_size("gy") * lax.axis_size("gz")
    split = (0, 15, 18)
    state = {"turn": 0, "returned": {}, "grad": []}
    late = [j for j, way in enumerate(ways) if way in ((0, 0), (1, 2))]
    early = [j for j in range(len(ways)) if j not in late]

    def tied(out, work, came):
        held = lax.optimization_barrier((gp, *out))
        made = work(held[0])
        held = lax.optimization_barrier((*made, *came))
        return held[: len(made)], list(held[len(made) :])

    def beside(out, came):
        turn = state["turn"]
        state["turn"] = turn + 1
        if turn == 0:
            work = lambda g: backward_faces(ways, flags, row, g, weight, sends.shape[2])
            state["back"], came = tied(out, work, came)
        elif turn in (1, 2):
            picks = early if turn == 1 else late
            held = lax.optimization_barrier((*[state["back"][j] for j in picks], *out))
            got = exchange(held[: len(picks)], [ways[j] for j in picks])
            held = lax.optimization_barrier((*got, *came))
            for j, face in zip(picks, held):
                state["returned"][j] = face
            came = list(held[len(picks) :])
        if turn in (3, 4):
            first, after = split[turn - 3 : turn - 1]
            work = lambda g: [backward_own(row, g, weight, first, after - first, state["grad"])]
            made, came = tied(out, work, came)
            state["grad"] = [made[0]]
        if turn == 5:
            faces = [state["returned"][j] for j in range(len(ways))]
            first = split[-1]
            work = lambda g: [finish(ways, flags, sends, row, g, weight, first, taps - first, state["grad"][0], faces)]
            (state["done"],), came = tied(out, work, came)
        return came

    grad_weight = reduce_all(keep, give, float(devices * own) ** -0.5, beside).reshape(weight.shape)
    return activated[None, None, None], state["done"][None, None, None], grad_weight


def solution(mesh):
    part = P("gx", "gy", "gz", None, None)
    return jax.shard_map(
        shards,
        mesh=mesh,
        in_specs=(part, P(), part, part, part, part, part),
        out_specs=(part, part, P()),
        check_vma=False,
    )
```

```python
import jax
import jax.numpy as jnp
from jax import lax
from jax.experimental import pallas as pl
from jax.experimental.pallas import tpu as pltpu
from jax.sharding import PartitionSpec as P

BF = jnp.bfloat16
F32 = jnp.float32
NT = (((1,), (1,)), ((), ()))
NN = (((1,), (0,)), ((), ()))
TN = (((0,), (0,)), ((), ()))
AXES = ("gx", "gy", "gz")
MISSING = 2000
VMEM = pl.BlockSpec(memory_space=pltpu.VMEM)
SMEM = pl.BlockSpec(memory_space=pltpu.SMEM)
ANY = pl.BlockSpec(memory_space=pl.ANY)
HBM = pl.BlockSpec(memory_space=pltpu.HBM)


def dot(a, b, dims=NN):
    return lax.dot_general(a, b, dims, preferred_element_type=F32)


def one_hot(mask):
    return jnp.where(mask, jnp.ones((), F32), jnp.zeros((), F32)).astype(BF)


def hold(x):
    return pltpu.with_memory_space_constraint(x, pltpu.HBM)


def params(megabytes):
    return pltpu.CompilerParams(vmem_limit_bytes=megabytes << 20)


def routes():
    out = []
    for i, axis in enumerate(AXES):
        out.append((0, i))
        if lax.axis_size(axis) > 2:
            out.append((1, i))
    return out


def slots():
    out, count = [], 0
    for axis in AXES:
        size = 1 if lax.axis_size(axis) == 2 else 2
        out.append(tuple(range(count, count + size)))
        count += size
    return out, count


def exchange(arrays, ways):
    got = []
    for array, (odd, i) in zip(arrays, ways):
        n = lax.axis_size(AXES[i])
        pairs = [p for j in range(odd, n - 1, 2) for p in ((j, j + 1), (j + 1, j))]
        got.append(lax.ppermute(array, AXES[i], pairs))
    return got


def towards(flags, way, lower, upper):
    odd, i = way
    return jnp.where(flags[1 + i] == odd, upper, lower)


def send_kernel(ways, flags, rows_hbm, own_hbm, *rest):
    outs, (rows_ref, own_ref, sems) = rest[: len(ways)], rest[len(ways) :]
    copies = [
        pltpu.make_async_copy(own_hbm, own_ref, sems.at[0]),
        pltpu.make_async_copy(rows_hbm, rows_ref, sems.at[1]),
    ]
    for copy in copies:
        copy.start()
    for copy in copies:
        copy.wait()
    face = rows_ref.shape[2]
    own = own_ref.shape[0]
    places = lax.broadcasted_iota(jnp.int32, (own, face), 0)
    for out, way in zip(outs, ways):
        rows = towards(flags, way, rows_ref[2 * way[1]], rows_ref[2 * way[1] + 1])
        out[...] = dot(one_hot(places == rows), own_ref[...], TN).astype(BF)


def send(ways, flags, rows, own_features):
    shape = jax.ShapeDtypeStruct((rows.shape[2], own_features.shape[1]), BF)
    return pl.pallas_call(
        lambda *refs: send_kernel(ways, *refs),
        in_specs=[SMEM, HBM, HBM],
        out_specs=[VMEM] * len(ways),
        out_shape=[shape] * len(ways),
        scratch_shapes=[
            pltpu.VMEM(rows.shape, jnp.int32),
            pltpu.VMEM(own_features.shape, BF),
            pltpu.SemaphoreType.DMA((2,)),
        ],
        compiler_params=params(8),
        name="send",
    )(flags, hold(rows), hold(own_features))


def invert_kernel(block, face, pairs, flags, in_hbm, out_hbm, live_hbm, col_ref, row_hbm, tables, row_ref, sems):
    copies = [
        pltpu.make_async_copy(hbm, tables.at[j], sems.at[j])
        for j, hbm in enumerate((in_hbm, out_hbm, live_hbm))
    ]
    for copy in copies:
        copy.start()
    taps, _, own = in_hbm.shape
    lows = lax.broadcasted_iota(jnp.int32, (block, own), 0)
    ranks = lax.broadcasted_iota(jnp.int32, (16, own), 0)
    for copy in copies:
        copy.wait()
    for k in range(taps):
        target = tables[1, k]
        source = tables[0, k]
        live = tables[2, k] > 0
        for i in pairs:
            dead = own + (2 * i + flags[1 + i]) * face
            beyond = source >= dead + face
            live = jnp.logical_and(live, jnp.logical_or(beyond, source < dead))
            source = jnp.where(beyond, source - face, source)
        source = jnp.where(live, source, MISSING)
        high = target // block
        hot = one_hot(lows == target - high * block)
        big = (source // 16) * 16
        spread = jnp.where(ranks == high, big, jnp.where(ranks - 8 == high, source - big, 0))
        spread = spread.astype(F32).astype(BF)
        col = dot(hot, spread, NT)
        col_ref[k] = col
        row_ref[k] = col.T
    copy = pltpu.make_async_copy(row_ref, row_hbm, sems.at[3])
    copy.start()
    copy.wait()


def invert(flags, in_rows, out_rows, live, face, block):
    pairs = [i for i in reversed(range(len(AXES))) if lax.axis_size(AXES[i]) == 2]
    taps, _, own = in_rows.shape
    return pl.pallas_call(
        lambda *refs: invert_kernel(block, face, pairs, *refs),
        in_specs=[SMEM, HBM, HBM, HBM],
        out_specs=[VMEM, HBM],
        out_shape=(
            jax.ShapeDtypeStruct((taps, block, 16), F32),
            pltpu.HBM((taps, 16, block), F32),
        ),
        scratch_shapes=[
            pltpu.VMEM((3, taps, 1, own), jnp.int32),
            pltpu.VMEM((taps, 16, block), F32),
            pltpu.SemaphoreType.DMA((4,)),
        ],
        compiler_params=params(12),
        name="invert",
    )(flags, hold(in_rows), hold(out_rows), hold(live))


def forward_kernel(ways, where, step, flags, col_ref, own_hbm, w_hbm, up_hbm, *rest):
    faces = rest[: len(ways)]
    act_hbm, gp_hbm, keep_hbm, *give_hbm = rest[len(ways) : len(ways) + 5]
    ext, got, got_t, weights, turned, up, act, gp, keep, give, sems = rest[len(ways) + 5 :]
    taps = col_ref.shape[0]
    own, ch = up.shape
    rows = ext.shape[0]
    half = ch // 2
    parts = own // step
    block = col_ref.shape[1]
    w_copy = pltpu.make_async_copy(w_hbm, weights, sems.at[0])
    up_copy = pltpu.make_async_copy(up_hbm, up, sems.at[1])
    own_copy = pltpu.make_async_copy(own_hbm, ext.at[pl.ds(0, own), :], sems.at[2])
    own_copy.start()
    w_copy.start()
    up_copy.start()
    face = faces[0].shape[0]
    for i, places in enumerate(where):
        mine = [came[...] for came, way in zip(faces, ways) if way[1] == i]
        if len(places) == 2:
            mine = [value.astype(F32) for value in mine]
            even = flags[1 + i] == 0
            mine = [jnp.where(even, mine[1], mine[0]).astype(BF), jnp.where(even, mine[0], mine[1]).astype(BF)]
        for place, value in zip(places, mine):
            ext[pl.ds(own + place * face, face), :] = value
    own_copy.wait()
    lanes = lax.broadcasted_iota(jnp.int32, (step, rows), 1)

    def gather(k, carried):
        at = pl.multiple_of(k * ch, ch)
        for h in range(parts):
            places = [
                col_ref[k, :, b : b + 1] + col_ref[k, :, b + 8 : b + 9]
                for b in range(h * step // block, (h + 1) * step // block)
            ]
            place = jnp.concatenate(places, axis=0).astype(jnp.int32)
            picked = dot(one_hot(lanes == place), ext[...]).astype(BF)
            got[pl.ds(h * step, step), pl.ds(at, ch)] = picked
            got_t[pl.ds(at, ch), pl.ds(h * step, step)] = picked.T
        return carried

    lax.fori_loop(0, taps, gather, 0, unroll=9)
    w_copy.wait()
    up_copy.wait()
    odd = flags[0] > 0
    for h in range(parts):
        part = pl.ds(h * step, step)
        v = dot(got[part, :], weights[...])
        s = jax.nn.sigmoid(v)
        act[part, :] = (v * s).astype(BF)
        g = up[part, :].astype(F32) * (s * (1.0 + v * (1.0 - s)))
        gp[part, :] = g.astype(BF)
        turned[part, :half] = jnp.where(odd, g[:, half:], g[:, :half]).astype(BF)
        turned[part, half:] = jnp.where(odd, g[:, :half], g[:, half:]).astype(BF)
    out_copies = [
        pltpu.make_async_copy(act, act_hbm, sems.at[3]),
        pltpu.make_async_copy(gp, gp_hbm, sems.at[4]),
    ]
    for copy in out_copies:
        copy.start()

    def one(t, carried):
        at = pl.multiple_of(t * ch, ch)
        r = dot(got_t[pl.ds(at, ch), :], turned[...])
        keep[pl.ds(at, ch), :] = r[:, :half]
        give[pl.ds(at, ch), :] = r[:, half:].astype(BF)
        return carried

    middle = taps * ch // 2
    bounds = [0, (taps + 1) // 2, taps]
    for j in range(2):
        lax.fori_loop(bounds[j], bounds[j + 1], one, 0, unroll=7 if (bounds[j + 1] - bounds[j]) % 7 == 0 else True)
        part = pl.ds(j * middle, middle)
        for source, target, sem in ((give, give_hbm[j], 5 + j), (keep, keep_hbm.at[part, :], 7 + j)):
            copy = pltpu.make_async_copy(source.at[part, :], target, sems.at[sem])
            copy.start()
            out_copies.append(copy)
    for copy in out_copies:
        copy.wait()


def forward(ways, flags, col, own_features, faces, weight, upstream):
    taps, block, _ = col.shape
    own, ch = own_features.shape
    where, faced = slots()
    rows = own + faced * faces[0].shape[0]
    like = jax.ShapeDtypeStruct
    return pl.pallas_call(
        lambda *refs: forward_kernel(ways, where, 256, *refs),
        in_specs=[SMEM, VMEM, HBM, HBM, HBM] + [VMEM] * len(faces),
        out_specs=[HBM, HBM, ANY, ANY, ANY],
        out_shape=[
            pltpu.HBM((own, ch), BF),
            pltpu.HBM((own, ch), BF),
            like((taps * ch, ch // 2), F32),
            like((taps * ch // 2, ch // 2), BF),
            like((taps * ch // 2, ch // 2), BF),
        ],
        scratch_shapes=[
            pltpu.VMEM((rows, ch), BF),
            pltpu.VMEM((own, taps * ch), BF),
            pltpu.VMEM((taps * ch, own), BF),
            pltpu.VMEM((taps * ch, ch), BF),
            pltpu.VMEM((own, ch), BF),
            pltpu.VMEM((own, ch), BF),
            pltpu.VMEM((own, ch), BF),
            pltpu.VMEM((own, ch), BF),
            pltpu.VMEM((taps * ch, ch // 2), F32),
            pltpu.VMEM((taps * ch, ch // 2), BF),
            pltpu.SemaphoreType.DMA((11,)),
        ],
        compiler_params=params(36),
        name="forward",
    )(flags, col, hold(own_features), hold(weight.reshape(taps * ch, ch)), hold(upstream), *faces)


def backward_body(start, first, count, step, row_hbm, gp_hbm, w_hbm, before_hbm, row, gp, got, weights, total, sems):
    size, ch = total.shape
    block = row.shape[2]
    parts = gp.shape[0] // block
    row_copy = pltpu.make_async_copy(row_hbm.at[pl.ds(first, count)], row, sems.at[0])
    gp_copy = pltpu.make_async_copy(gp_hbm, gp, sems.at[1])
    row_copy.start()
    gp_copy.start()
    later = [
        pltpu.make_async_copy(w_hbm.at[first + j], weights.at[:, pl.ds(j * ch, ch)], sems.at[3 + j])
        for j in range(count)
    ]
    if before_hbm is not None:
        later.append(pltpu.make_async_copy(before_hbm, total, sems.at[2]))
    for copy in later:
        copy.start()
    row_copy.wait()
    gp_copy.wait()

    def gather(j, carried):
        at = pl.multiple_of(j * ch, ch)
        for r in range(0, size, step):
            lines = lax.broadcasted_iota(jnp.int32, (step, block), 0) + (start + r)
            hots = []
            for h in range(parts):
                place = (row[j, h : h + 1, :] + row[j, h + 8 : h + 9, :]).astype(jnp.int32)
                hots.append(one_hot(lines == place))
            got[pl.ds(r, step), pl.ds(at, ch)] = dot(jnp.concatenate(hots, axis=1), gp[...]).astype(BF)
        return carried

    lax.fori_loop(0, count, gather, 0, unroll=next(u for u in (9, 6, 5, 3, 1) if count % u == 0))
    for copy in later:
        copy.wait()
    for r in range(0, size, step):
        value = dot(got[pl.ds(r, step), :], weights[...], NT)
        total[pl.ds(r, step), :] = value if before_hbm is None else value + total[pl.ds(r, step), :]


def backward_scratch(row, gp, size, count):
    own, ch = gp.shape
    return [
        pltpu.VMEM((count,) + row.shape[1:], F32),
        pltpu.VMEM((own, ch), BF),
        pltpu.VMEM((size, count * ch), BF),
        pltpu.VMEM((ch, count * ch), BF),
        pltpu.VMEM((size, ch), F32),
        pltpu.SemaphoreType.DMA((3 + count,)),
    ]


def faces_kernel(ways, where, start, count, flags, row_hbm, gp_hbm, w_hbm, *rest):
    outs, staged, sems, scratch = rest[: len(ways)], rest[len(ways)], rest[len(ways) + 1], rest[len(ways) + 2 :]
    total = scratch[4]
    face = outs[0].shape[0]
    backward_body(start, 0, count, total.shape[0] // 2, row_hbm, gp_hbm, w_hbm, None, *scratch)
    copies = []
    for j, way in enumerate(ways):
        values = [total[pl.ds(place * face, face), :] for place in where[way[1]]]
        value = towards(flags, way, *values) if len(values) == 2 else values[0]
        staged[j] = value.astype(BF)
        copies.append(pltpu.make_async_copy(staged.at[j], outs[j], sems.at[j]))
        copies[-1].start()
    for copy in copies:
        copy.wait()


def backward_faces(ways, flags, row, gp, weight, face):
    taps = row.shape[0]
    own, ch = gp.shape
    where, faced = slots()
    return pl.pallas_call(
        lambda *refs: faces_kernel(ways, where, own, taps, *refs),
        in_specs=[SMEM, HBM, HBM, HBM],
        out_specs=[HBM] * len(ways),
        out_shape=[pltpu.HBM((face, ch), BF)] * len(ways),
        scratch_shapes=[pltpu.VMEM((len(ways), face, ch), BF), pltpu.SemaphoreType.DMA((len(ways),))]
        + backward_scratch(row, gp, faced * face, taps),
        compiler_params=params(18),
        name="backward_faces",
    )(flags, hold(row), hold(gp), hold(weight))


def own_kernel(first, count, row_hbm, gp_hbm, w_hbm, *rest):
    *before, out_hbm = rest[:-6]
    scratch = rest[-6:]
    backward_body(0, first, count, 384, row_hbm, gp_hbm, w_hbm, before[0] if before else None, *scratch)
    copy = pltpu.make_async_copy(scratch[4], out_hbm, scratch[5].at[2])
    copy.start()
    copy.wait()


def backward_own(row, gp, weight, first, count, before):
    args = [row, gp, weight] + before
    return pl.pallas_call(
        lambda *refs: own_kernel(first, count, *refs),
        in_specs=[HBM] * len(args),
        out_specs=HBM,
        out_shape=pltpu.HBM(gp.shape, F32),
        scratch_shapes=backward_scratch(row, gp, gp.shape[0], count),
        compiler_params=params(14),
        name="backward_own",
    )(*[hold(x) for x in args])


def finish_kernel(ways, first, count, flags, rows_hbm, row_hbm, gp_hbm, w_hbm, before_hbm, *rest):
    faces_hbm, out_ref, rows_ref, faces, sems = rest[: len(ways)], *rest[len(ways) : len(ways) + 4]
    scratch = rest[len(ways) + 4 :]
    copies = [pltpu.make_async_copy(rows_hbm, rows_ref, sems.at[len(ways)])]
    for j in range(len(ways)):
        copies.append(pltpu.make_async_copy(faces_hbm[j], faces.at[j], sems.at[j]))
    for copy in copies:
        copy.start()
    backward_body(0, first, count, 384, row_hbm, gp_hbm, w_hbm, before_hbm, *scratch)
    face = rows_ref.shape[2]
    own = out_ref.shape[0]
    places = lax.broadcasted_iota(jnp.int32, (own, face), 0)
    total = scratch[4][...]
    for copy in copies:
        copy.wait()
    for j, way in enumerate(ways):
        rows = towards(flags, way, rows_ref[2 * way[1]], rows_ref[2 * way[1] + 1])
        total = total + dot(one_hot(places == rows), faces[j])
    out_ref[...] = total.astype(BF)


def finish(ways, flags, rows, row, gp, weight, first, count, before, returned):
    return pl.pallas_call(
        lambda *refs: finish_kernel(ways, first, count, *refs),
        in_specs=[SMEM] + [HBM] * (5 + len(returned)),
        out_specs=VMEM,
        out_shape=jax.ShapeDtypeStruct(gp.shape, BF),
        scratch_shapes=[
            pltpu.VMEM(rows.shape, jnp.int32),
            pltpu.VMEM((len(ways),) + returned[0].shape, BF),
            pltpu.SemaphoreType.DMA((len(ways) + 1,)),
        ]
        + backward_scratch(row, gp, gp.shape[0], count),
        compiler_params=params(16),
        name="finish",
    )(flags, *[hold(x) for x in [rows, row, gp, weight, before] + returned])


def swap(x, axis, bit):
    n = lax.axis_size(axis)
    return lax.ppermute(x, axis, [(j, j ^ (1 << bit)) for j in range(n)])


def side(axis, bit):
    return (lax.axis_index(axis) >> bit) & 1


def place_kernel(size, turns, n, flip, spots, *refs):
    arrays, out, sem = refs[:4], refs[-2], refs[-1]
    half, ch = out.shape[0] // 2, out.shape[1] // 2
    at, odd = spots[2 * turns], spots[2 * turns + 1]
    copies = []
    for a, array in enumerate(arrays):
        i, twin = a % 2, a // 2
        side_of = lambda t, r: jnp.bitwise_xor(spots[i * turns + t], r)
        lane = pl.multiple_of((odd if twin == 0 else 1 - odd) * ch, 128)
        for b in range(array.shape[0] // size):
            s, rest = b % n, b // n
            row = i * half + side_of(0, flip) * (half // 2)
            for t in range(turns - 1, 0, -1):
                row = row + side_of(t, rest % 2) * (half >> (t + 1))
                rest = rest // 2
            row = row + jnp.where(at >= s, at - s, at - s + n) * size
            target = out.at[pl.ds(pl.multiple_of(row, 8), size), pl.ds(lane, ch)]
            copies.append(pltpu.make_async_copy(array.at[pl.ds(b * size, size), :], target, sem.at[len(copies)]))
            copies[-1].start()
    for copy in copies:
        copy.wait()


def place(spots, arrays, size, turns, rows, flip, before):
    blocks = len(arrays) * (arrays[0].shape[0] // size)
    n = lax.axis_size("gy")
    args = list(arrays) + ([] if before is None else [before])
    return pl.pallas_call(
        lambda *refs: place_kernel(size, turns, n, flip, *refs),
        in_specs=[SMEM] + [ANY] * len(arrays) + [HBM] * (len(args) - len(arrays)),
        out_specs=HBM,
        out_shape=jax.ShapeDtypeStruct((rows, 2 * arrays[0].shape[1]), BF),
        scratch_shapes=[pltpu.SemaphoreType.DMA((blocks,))],
        input_output_aliases={} if before is None else {len(args): 0},
        compiler_params=params(4),
        name="place",
    )(spots, *args)


def reduce_all(keep, give, scaling, beside):
    bits = lambda axis, low: [(axis, b) for b in range(low, lax.axis_size(axis).bit_length() - 1)]
    plane = [bits("gx", 0) + bits("gz", 1), bits("gz", 1) + bits("gx", 0)]
    turns = len(plane[0])
    rows, ch = keep.shape
    sides = [[side(*plane[i][t]) for t in range(turns)] for i in range(2)]
    terms = [[(keep, i * (rows // 2)), (swap(give[i], "gz", 0), 0)] for i in range(2)]

    def total(i, extra, size):
        out = None
        for array, start in terms[i]:
            value = lax.dynamic_slice_in_dim(array, start + extra, size, 0).astype(F32)
            out = value if out is None else out + value
        return out

    size = rows // 2
    for turn in range(turns):
        size = size // 2
        mine = [side(*plane[i][turn]) for i in range(2)]
        out = [total(i, (1 - mine[i]) * size, size).astype(BF) for i in range(2)]
        came = beside(out, [swap(out[i], *plane[i][turn]) for i in range(2)])
        for i in range(2):
            terms[i] = [(a, start + mine[i] * size) for a, start in terms[i]] + [(came[i], 0)]
    n = lax.axis_size("gy")
    at = lax.axis_index("gy")
    size = size // n
    slot = lambda s: jnp.concatenate([total(i, ((at + s) % n) * size, size) for i in range(2)], axis=0)
    turn_by = lambda y, s: lax.ppermute(y, "gy", [(j, (j + s) % n) for j in range(n)])
    out = [slot(s).astype(BF) for s in range(1, n)]
    came = beside(out, [turn_by(y, s + 1) for s, y in enumerate(out)])
    final = slot(0)
    for y in came:
        final = final + y.astype(F32)
    mine = (final * scaling).astype(BF)
    came = beside([mine], [turn_by(mine, s) for s in range(1, n)])
    pieces = [jnp.concatenate([y[i * size : (i + 1) * size] for y in [mine] + came], axis=0) for i in range(2)]
    for turn in range(turns - 1, 0, -1):
        came = beside(pieces, [swap(pieces[i], *plane[i][turn]) for i in range(2)])
        pieces = [jnp.concatenate([pieces[i], came[i]], axis=0) for i in range(2)]
    odd = side("gz", 0)
    cross = lambda arrays: [swap(y, "gz", 0) for y in arrays]
    came = beside(pieces, [swap(pieces[i], *plane[i][0]) for i in range(2)])
    twins = cross(pieces)
    if size % 8 == 0:
        spots = jnp.stack(sides[0] + sides[1] + [at, odd]).astype(jnp.int32)
        half = place(spots, pieces + twins, size, turns, rows, 0, None)
        last = cross(came)
        return place(spots, came + last, size, turns, rows, 1, half)
    last = cross(came)

    def ordered(i, first, second):
        x = jnp.concatenate([first, second], axis=0).reshape((2,) * turns + (n, size, ch))
        for t in range(turns):
            x = jnp.where(sides[i][t] == 1, jnp.flip(x, t), x)
        x = jnp.take(x, (at - jnp.arange(n)) % n, axis=turns)
        return x.reshape(rows // 2, ch)

    mine = jnp.concatenate([ordered(i, pieces[i], came[i]) for i in range(2)], axis=0)
    other = jnp.concatenate([ordered(i, twins[i], last[i]) for i in range(2)], axis=0)
    low, high = jnp.where(odd == 1, other, mine), jnp.where(odd == 1, mine, other)
    return jnp.concatenate([low, high], axis=1)


def shards(features, weight, upstream, send_rows, in_rows, out_rows, tap_pair_exists):
    own_features = features[0, 0, 0]
    own, ch = own_features.shape
    single = lambda x: x[0, 0, 0][:, None, :]
    sends = single(send_rows)
    taps = weight.shape[0]
    block = 128
    ways = routes()
    flags = jnp.stack([side("gz", 0)] + [lax.axis_index(a) & 1 for a in AXES]).astype(jnp.int32)
    faces = exchange(send(ways, flags, sends, own_features), ways)
    col, row = invert(
        flags, single(in_rows), single(out_rows), single(tap_pair_exists), sends.shape[2], block
    )
    activated, gp, keep, *give = forward(ways, flags, col, own_features, faces, weight, upstream[0, 0, 0])
    devices = lax.axis_size("gx") * lax.axis_size("gy") * lax.axis_size("gz")
    state = {"turn": 0, "returned": {}, "grad": []}
    when = {(0, 0): 2, (1, 2): 2, (0, 2): 3, (0, 1): 4, (1, 1): 4}
    back_at = {turn: [j for j, way in enumerate(ways) if when.get(way, 4) == turn] for turn in (2, 3, 4)}
    own_at = {1: (0, 3), 2: (3, 6), 3: (6, 18)}

    def tied(out, work, came):
        held = lax.optimization_barrier((gp, *out))
        made = work(held[0])
        held = lax.optimization_barrier((*made, *came))
        return held[: len(made)], list(held[len(made) :])

    def beside(out, came):
        turn = state["turn"]
        state["turn"] = turn + 1
        if turn == 0:
            work = lambda g: backward_faces(ways, flags, row, g, weight, sends.shape[2])
            state["back"], came = tied(out, work, came)
        if back_at.get(turn):
            picks = back_at[turn]
            held = lax.optimization_barrier((*[state["back"][j] for j in picks], *out))
            got = exchange(held[: len(picks)], [ways[j] for j in picks])
            held = lax.optimization_barrier((*got, *came))
            for j, face in zip(picks, held):
                state["returned"][j] = face
            came = list(held[len(picks) :])
        if turn in own_at:
            first, after = own_at[turn]
            work = lambda g: [backward_own(row, g, weight, first, after - first, state["grad"])]
            made, came = tied(out, work, came)
            state["grad"] = [made[0]]
        if turn == 5:
            faces = [state["returned"][j] for j in range(len(ways))]
            first = own_at[3][1]
            work = lambda g: [finish(ways, flags, sends, row, g, weight, first, taps - first, state["grad"][0], faces)]
            (state["done"],), came = tied(out, work, came)
        return came

    grad_weight = reduce_all(keep, give, float(devices * own) ** -0.5, beside).reshape(weight.shape)
    return activated[None, None, None], state["done"][None, None, None], grad_weight


def solution(mesh):
    part = P("gx", "gy", "gz", None, None)
    return jax.shard_map(
        shards,
        mesh=mesh,
        in_specs=(part, P(), part, part, part, part, part),
        out_specs=(part, part, P()),
        check_vma=False,
    )
```

```python
import jax
import jax.numpy as jnp
from jax import lax
from jax.experimental import pallas as pl
from jax.experimental.pallas import tpu as pltpu
from jax.sharding import PartitionSpec as P

BF = jnp.bfloat16
F32 = jnp.float32
NT = (((1,), (1,)), ((), ()))
NN = (((1,), (0,)), ((), ()))
TN = (((0,), (0,)), ((), ()))
AXES = ("gx", "gy", "gz")
MISSING = 2000
VMEM = pl.BlockSpec(memory_space=pltpu.VMEM)
SMEM = pl.BlockSpec(memory_space=pltpu.SMEM)
ANY = pl.BlockSpec(memory_space=pl.ANY)
HBM = pl.BlockSpec(memory_space=pltpu.HBM)


def dot(a, b, dims=NN):
    return lax.dot_general(a, b, dims, preferred_element_type=F32)


def one_hot(mask):
    return jnp.where(mask, jnp.ones((), F32), jnp.zeros((), F32)).astype(BF)


def hold(x):
    return pltpu.with_memory_space_constraint(x, pltpu.HBM)


def params(megabytes):
    return pltpu.CompilerParams(vmem_limit_bytes=megabytes << 20)


def routes():
    out = []
    for i, axis in enumerate(AXES):
        out.append((0, i))
        if lax.axis_size(axis) > 2:
            out.append((1, i))
    return out


def slots():
    out, count = [], 0
    for axis in AXES:
        size = 1 if lax.axis_size(axis) == 2 else 2
        out.append(tuple(range(count, count + size)))
        count += size
    return out, count


def exchange(arrays, ways):
    got = []
    for array, (odd, i) in zip(arrays, ways):
        n = lax.axis_size(AXES[i])
        pairs = [p for j in range(odd, n - 1, 2) for p in ((j, j + 1), (j + 1, j))]
        got.append(lax.ppermute(array, AXES[i], pairs))
    return got


def towards(flags, way, lower, upper):
    odd, i = way
    return jnp.where(flags[1 + i] == odd, upper, lower)


def send_kernel(ways, flags, rows_hbm, own_hbm, *rest):
    outs, (rows_ref, own_ref, sems) = rest[: len(ways)], rest[len(ways) :]
    copies = [
        pltpu.make_async_copy(own_hbm, own_ref, sems.at[0]),
        pltpu.make_async_copy(rows_hbm, rows_ref, sems.at[1]),
    ]
    for copy in copies:
        copy.start()
    for copy in copies:
        copy.wait()
    face = rows_ref.shape[2]
    own = own_ref.shape[0]
    places = lax.broadcasted_iota(jnp.int32, (own, face), 0)
    for out, way in zip(outs, ways):
        rows = towards(flags, way, rows_ref[2 * way[1]], rows_ref[2 * way[1] + 1])
        out[...] = dot(one_hot(places == rows), own_ref[...], TN).astype(BF)


def send(ways, flags, rows, own_features):
    shape = jax.ShapeDtypeStruct((rows.shape[2], own_features.shape[1]), BF)
    return pl.pallas_call(
        lambda *refs: send_kernel(ways, *refs),
        in_specs=[SMEM, HBM, HBM],
        out_specs=[VMEM] * len(ways),
        out_shape=[shape] * len(ways),
        scratch_shapes=[
            pltpu.VMEM(rows.shape, jnp.int32),
            pltpu.VMEM(own_features.shape, BF),
            pltpu.SemaphoreType.DMA((2,)),
        ],
        compiler_params=params(8),
        name="send",
    )(flags, hold(rows), hold(own_features))


def invert_kernel(block, face, pairs, flags, in_hbm, out_hbm, live_hbm, col_ref, row_hbm, tables, row_ref, sems):
    copies = [
        pltpu.make_async_copy(hbm, tables.at[j], sems.at[j])
        for j, hbm in enumerate((in_hbm, out_hbm, live_hbm))
    ]
    for copy in copies:
        copy.start()
    taps, _, own = in_hbm.shape
    lows = lax.broadcasted_iota(jnp.int32, (block, own), 0)
    ranks = lax.broadcasted_iota(jnp.int32, (16, own), 0)
    for copy in copies:
        copy.wait()
    for k in range(taps):
        target = tables[1, k]
        source = tables[0, k]
        live = tables[2, k] > 0
        for i in pairs:
            dead = own + (2 * i + flags[1 + i]) * face
            beyond = source >= dead + face
            live = jnp.logical_and(live, jnp.logical_or(beyond, source < dead))
            source = jnp.where(beyond, source - face, source)
        source = jnp.where(live, source, MISSING)
        high = target // block
        hot = one_hot(lows == target - high * block)
        big = (source // 16) * 16
        spread = jnp.where(ranks == high, big, jnp.where(ranks - 8 == high, source - big, 0))
        spread = spread.astype(F32).astype(BF)
        col = dot(hot, spread, NT)
        col_ref[k] = col
        row_ref[k] = col.T
    copy = pltpu.make_async_copy(row_ref, row_hbm, sems.at[3])
    copy.start()
    copy.wait()


def invert(flags, in_rows, out_rows, live, face, block):
    pairs = [i for i in reversed(range(len(AXES))) if lax.axis_size(AXES[i]) == 2]
    taps, _, own = in_rows.shape
    return pl.pallas_call(
        lambda *refs: invert_kernel(block, face, pairs, *refs),
        in_specs=[SMEM, HBM, HBM, HBM],
        out_specs=[VMEM, HBM],
        out_shape=(
            jax.ShapeDtypeStruct((taps, block, 16), F32),
            pltpu.HBM((taps, 16, block), F32),
        ),
        scratch_shapes=[
            pltpu.VMEM((3, taps, 1, own), jnp.int32),
            pltpu.VMEM((taps, 16, block), F32),
            pltpu.SemaphoreType.DMA((4,)),
        ],
        compiler_params=params(12),
        name="invert",
    )(flags, hold(in_rows), hold(out_rows), hold(live))


def forward_kernel(ways, where, step, flags, col_ref, own_hbm, w_hbm, up_hbm, *rest):
    faces = rest[: len(ways)]
    act_hbm, gp_hbm, keep_hbm, *give_hbm = rest[len(ways) : len(ways) + 5]
    ext, got, got_t, weights, turned, up, act, gp, keep, give, sems = rest[len(ways) + 5 :]
    taps = col_ref.shape[0]
    own, ch = up.shape
    rows = ext.shape[0]
    half = ch // 2
    parts = own // step
    block = col_ref.shape[1]
    w_copy = pltpu.make_async_copy(w_hbm, weights, sems.at[0])
    up_copy = pltpu.make_async_copy(up_hbm, up, sems.at[1])
    own_copy = pltpu.make_async_copy(own_hbm, ext.at[pl.ds(0, own), :], sems.at[2])
    own_copy.start()
    w_copy.start()
    up_copy.start()
    face = faces[0].shape[0]
    for i, places in enumerate(where):
        mine = [came[...] for came, way in zip(faces, ways) if way[1] == i]
        if len(places) == 2:
            mine = [value.astype(F32) for value in mine]
            even = flags[1 + i] == 0
            mine = [jnp.where(even, mine[1], mine[0]).astype(BF), jnp.where(even, mine[0], mine[1]).astype(BF)]
        for place, value in zip(places, mine):
            ext[pl.ds(own + place * face, face), :] = value
    own_copy.wait()
    lanes = lax.broadcasted_iota(jnp.int32, (step, 128), 1)

    def gather(k, carried):
        at = pl.multiple_of(k * ch, ch)
        for h in range(parts):
            places = [
                col_ref[k, :, b : b + 1] + col_ref[k, :, b + 8 : b + 9]
                for b in range(h * step // block, (h + 1) * step // block)
            ]
            place = jnp.concatenate(places, axis=0).astype(jnp.int32)
            place = jnp.broadcast_to(place, (step, 128)).astype(jnp.int16)
            hots = []
            for r in range(0, rows, 128):
                hot = jnp.where((lanes + r).astype(jnp.int16) == place, jnp.ones((), BF), jnp.zeros((), BF))
                hots.append(hot[:, : min(128, rows - r)])
            picked = dot(jnp.concatenate(hots, axis=1), ext[...]).astype(BF)
            got[pl.ds(h * step, step), pl.ds(at, ch)] = picked
            got_t[pl.ds(at, ch), pl.ds(h * step, step)] = picked.T
        return carried

    lax.fori_loop(0, taps, gather, 0, unroll=9)
    w_copy.wait()
    up_copy.wait()
    odd = flags[0] > 0
    for h in range(parts):
        part = pl.ds(h * step, step)
        v = dot(got[part, :], weights[...])
        s = jax.nn.sigmoid(v)
        act[part, :] = (v * s).astype(BF)
        g = up[part, :].astype(F32) * (s * (1.0 + v * (1.0 - s)))
        gp[part, :] = g.astype(BF)
        turned[part, :half] = jnp.where(odd, g[:, half:], g[:, :half]).astype(BF)
        turned[part, half:] = jnp.where(odd, g[:, :half], g[:, half:]).astype(BF)
    out_copies = [
        pltpu.make_async_copy(act, act_hbm, sems.at[3]),
        pltpu.make_async_copy(gp, gp_hbm, sems.at[4]),
    ]
    for copy in out_copies:
        copy.start()

    def one(t, carried):
        at = pl.multiple_of(t * ch, ch)
        r = dot(got_t[pl.ds(at, ch), :], turned[...])
        keep[pl.ds(at, ch), :] = r[:, :half]
        give[pl.ds(at, ch), :] = r[:, half:].astype(BF)
        return carried

    middle = taps * ch // 2
    bounds = [0, (taps + 1) // 2, taps]
    for j in range(2):
        lax.fori_loop(bounds[j], bounds[j + 1], one, 0, unroll=7 if (bounds[j + 1] - bounds[j]) % 7 == 0 else True)
        part = pl.ds(j * middle, middle)
        for source, target, sem in ((give, give_hbm[j], 5 + j), (keep, keep_hbm.at[part, :], 7 + j)):
            copy = pltpu.make_async_copy(source.at[part, :], target, sems.at[sem])
            copy.start()
            out_copies.append(copy)
    for copy in out_copies:
        copy.wait()


def forward(ways, flags, col, own_features, faces, weight, upstream):
    taps, block, _ = col.shape
    own, ch = own_features.shape
    where, faced = slots()
    rows = own + faced * faces[0].shape[0]
    like = jax.ShapeDtypeStruct
    return pl.pallas_call(
        lambda *refs: forward_kernel(ways, where, 256, *refs),
        in_specs=[SMEM, VMEM, HBM, HBM, HBM] + [VMEM] * len(faces),
        out_specs=[HBM, HBM, ANY, ANY, ANY],
        out_shape=[
            pltpu.HBM((own, ch), BF),
            pltpu.HBM((own, ch), BF),
            like((taps * ch, ch // 2), F32),
            like((taps * ch // 2, ch // 2), BF),
            like((taps * ch // 2, ch // 2), BF),
        ],
        scratch_shapes=[
            pltpu.VMEM((rows, ch), BF),
            pltpu.VMEM((own, taps * ch), BF),
            pltpu.VMEM((taps * ch, own), BF),
            pltpu.VMEM((taps * ch, ch), BF),
            pltpu.VMEM((own, ch), BF),
            pltpu.VMEM((own, ch), BF),
            pltpu.VMEM((own, ch), BF),
            pltpu.VMEM((own, ch), BF),
            pltpu.VMEM((taps * ch, ch // 2), F32),
            pltpu.VMEM((taps * ch, ch // 2), BF),
            pltpu.SemaphoreType.DMA((11,)),
        ],
        compiler_params=params(36),
        name="forward",
    )(flags, col, hold(own_features), hold(weight.reshape(taps * ch, ch)), hold(upstream), *faces)


def backward_body(start, first, count, step, row_hbm, gp_hbm, w_hbm, before_hbm, row, gp, got, weights, total, sems):
    size, ch = total.shape
    block = row.shape[2]
    parts = gp.shape[0] // block
    row_copy = pltpu.make_async_copy(row_hbm.at[pl.ds(first, count)], row, sems.at[0])
    gp_copy = pltpu.make_async_copy(gp_hbm, gp, sems.at[1])
    row_copy.start()
    gp_copy.start()
    later = [
        pltpu.make_async_copy(w_hbm.at[first + j], weights.at[:, pl.ds(j * ch, ch)], sems.at[3 + j])
        for j in range(count)
    ]
    if before_hbm is not None:
        later.append(pltpu.make_async_copy(before_hbm, total, sems.at[2]))
    for copy in later:
        copy.start()
    row_copy.wait()
    gp_copy.wait()

    def gather(j, carried):
        at = pl.multiple_of(j * ch, ch)
        for r in range(0, size, step):
            lines = lax.broadcasted_iota(jnp.int32, (step, block), 0) + (start + r)
            hots = []
            for h in range(parts):
                place = (row[j, h : h + 1, :] + row[j, h + 8 : h + 9, :]).astype(jnp.int32)
                hots.append(one_hot(lines == place))
            got[pl.ds(r, step), pl.ds(at, ch)] = dot(jnp.concatenate(hots, axis=1), gp[...]).astype(BF)
        return carried

    lax.fori_loop(0, count, gather, 0, unroll=next(u for u in (9, 6, 5, 3, 1) if count % u == 0))
    for copy in later:
        copy.wait()
    for r in range(0, size, step):
        value = dot(got[pl.ds(r, step), :], weights[...], NT)
        total[pl.ds(r, step), :] = value if before_hbm is None else value + total[pl.ds(r, step), :]


def backward_scratch(row, gp, size, count):
    own, ch = gp.shape
    return [
        pltpu.VMEM((count,) + row.shape[1:], F32),
        pltpu.VMEM((own, ch), BF),
        pltpu.VMEM((size, count * ch), BF),
        pltpu.VMEM((ch, count * ch), BF),
        pltpu.VMEM((size, ch), F32),
        pltpu.SemaphoreType.DMA((3 + count,)),
    ]


def faces_kernel(ways, where, start, count, flags, row_hbm, gp_hbm, w_hbm, *rest):
    outs, staged, sems, scratch = rest[: len(ways)], rest[len(ways)], rest[len(ways) + 1], rest[len(ways) + 2 :]
    total = scratch[4]
    face = outs[0].shape[0]
    backward_body(start, 0, count, total.shape[0] // 2, row_hbm, gp_hbm, w_hbm, None, *scratch)
    copies = []
    for j, way in enumerate(ways):
        values = [total[pl.ds(place * face, face), :] for place in where[way[1]]]
        value = towards(flags, way, *values) if len(values) == 2 else values[0]
        staged[j] = value.astype(BF)
        copies.append(pltpu.make_async_copy(staged.at[j], outs[j], sems.at[j]))
        copies[-1].start()
    for copy in copies:
        copy.wait()


def backward_faces(ways, flags, row, gp, weight, face):
    taps = row.shape[0]
    own, ch = gp.shape
    where, faced = slots()
    return pl.pallas_call(
        lambda *refs: faces_kernel(ways, where, own, taps, *refs),
        in_specs=[SMEM, HBM, HBM, HBM],
        out_specs=[HBM] * len(ways),
        out_shape=[pltpu.HBM((face, ch), BF)] * len(ways),
        scratch_shapes=[pltpu.VMEM((len(ways), face, ch), BF), pltpu.SemaphoreType.DMA((len(ways),))]
        + backward_scratch(row, gp, faced * face, taps),
        compiler_params=params(18),
        name="backward_faces",
    )(flags, hold(row), hold(gp), hold(weight))


def own_kernel(first, count, row_hbm, gp_hbm, w_hbm, *rest):
    *before, out_hbm = rest[:-6]
    scratch = rest[-6:]
    backward_body(0, first, count, 384, row_hbm, gp_hbm, w_hbm, before[0] if before else None, *scratch)
    copy = pltpu.make_async_copy(scratch[4], out_hbm, scratch[5].at[2])
    copy.start()
    copy.wait()


def backward_own(row, gp, weight, first, count, before):
    args = [row, gp, weight] + before
    return pl.pallas_call(
        lambda *refs: own_kernel(first, count, *refs),
        in_specs=[HBM] * len(args),
        out_specs=HBM,
        out_shape=pltpu.HBM(gp.shape, F32),
        scratch_shapes=backward_scratch(row, gp, gp.shape[0], count),
        compiler_params=params(14),
        name="backward_own",
    )(*[hold(x) for x in args])


def finish_kernel(ways, first, count, flags, rows_hbm, row_hbm, gp_hbm, w_hbm, before_hbm, *rest):
    faces_hbm, out_ref, rows_ref, faces, sems = rest[: len(ways)], *rest[len(ways) : len(ways) + 4]
    scratch = rest[len(ways) + 4 :]
    copies = [pltpu.make_async_copy(rows_hbm, rows_ref, sems.at[len(ways)])]
    for j in range(len(ways)):
        copies.append(pltpu.make_async_copy(faces_hbm[j], faces.at[j], sems.at[j]))
    for copy in copies:
        copy.start()
    backward_body(0, first, count, 384, row_hbm, gp_hbm, w_hbm, before_hbm, *scratch)
    face = rows_ref.shape[2]
    own = out_ref.shape[0]
    places = lax.broadcasted_iota(jnp.int32, (own, face), 0)
    total = scratch[4][...]
    for copy in copies:
        copy.wait()
    for j, way in enumerate(ways):
        rows = towards(flags, way, rows_ref[2 * way[1]], rows_ref[2 * way[1] + 1])
        total = total + dot(one_hot(places == rows), faces[j])
    out_ref[...] = total.astype(BF)


def finish(ways, flags, rows, row, gp, weight, first, count, before, returned):
    return pl.pallas_call(
        lambda *refs: finish_kernel(ways, first, count, *refs),
        in_specs=[SMEM] + [HBM] * (5 + len(returned)),
        out_specs=VMEM,
        out_shape=jax.ShapeDtypeStruct(gp.shape, BF),
        scratch_shapes=[
            pltpu.VMEM(rows.shape, jnp.int32),
            pltpu.VMEM((len(ways),) + returned[0].shape, BF),
            pltpu.SemaphoreType.DMA((len(ways) + 1,)),
        ]
        + backward_scratch(row, gp, gp.shape[0], count),
        compiler_params=params(16),
        name="finish",
    )(flags, *[hold(x) for x in [rows, row, gp, weight, before] + returned])


def swap(x, axis, bit):
    n = lax.axis_size(axis)
    return lax.ppermute(x, axis, [(j, j ^ (1 << bit)) for j in range(n)])


def side(axis, bit):
    return (lax.axis_index(axis) >> bit) & 1


def place_kernel(size, turns, n, flip, spots, *refs):
    arrays, out, sem = refs[:4], refs[-2], refs[-1]
    half, ch = out.shape[0] // 2, out.shape[1] // 2
    at, odd = spots[2 * turns], spots[2 * turns + 1]
    copies = []
    for a, array in enumerate(arrays):
        i, twin = a % 2, a // 2
        side_of = lambda t, r: jnp.bitwise_xor(spots[i * turns + t], r)
        lane = pl.multiple_of((odd if twin == 0 else 1 - odd) * ch, 128)
        for b in range(array.shape[0] // size):
            s, rest = b % n, b // n
            row = i * half + side_of(0, flip) * (half // 2)
            for t in range(turns - 1, 0, -1):
                row = row + side_of(t, rest % 2) * (half >> (t + 1))
                rest = rest // 2
            row = row + jnp.where(at >= s, at - s, at - s + n) * size
            target = out.at[pl.ds(pl.multiple_of(row, 8), size), pl.ds(lane, ch)]
            copies.append(pltpu.make_async_copy(array.at[pl.ds(b * size, size), :], target, sem.at[len(copies)]))
            copies[-1].start()
    for copy in copies:
        copy.wait()


def place(spots, arrays, size, turns, rows, flip, before):
    blocks = len(arrays) * (arrays[0].shape[0] // size)
    n = lax.axis_size("gy")
    args = list(arrays) + ([] if before is None else [before])
    return pl.pallas_call(
        lambda *refs: place_kernel(size, turns, n, flip, *refs),
        in_specs=[SMEM] + [ANY] * len(arrays) + [HBM] * (len(args) - len(arrays)),
        out_specs=HBM,
        out_shape=jax.ShapeDtypeStruct((rows, 2 * arrays[0].shape[1]), BF),
        scratch_shapes=[pltpu.SemaphoreType.DMA((blocks,))],
        input_output_aliases={} if before is None else {len(args): 0},
        compiler_params=params(4),
        name="place",
    )(spots, *args)


def reduce_all(keep, give, scaling, beside):
    bits = lambda axis, low: [(axis, b) for b in range(low, lax.axis_size(axis).bit_length() - 1)]
    plane = [bits("gx", 0) + bits("gz", 1), bits("gz", 1) + bits("gx", 0)]
    turns = len(plane[0])
    rows, ch = keep.shape
    sides = [[side(*plane[i][t]) for t in range(turns)] for i in range(2)]
    terms = [[(keep, i * (rows // 2)), (swap(give[i], "gz", 0), 0)] for i in range(2)]

    def total(i, extra, size):
        out = None
        for array, start in terms[i]:
            value = lax.dynamic_slice_in_dim(array, start + extra, size, 0).astype(F32)
            out = value if out is None else out + value
        return out

    size = rows // 2
    for turn in range(turns):
        size = size // 2
        mine = [side(*plane[i][turn]) for i in range(2)]
        out = [total(i, (1 - mine[i]) * size, size).astype(BF) for i in range(2)]
        came = beside(out, [swap(out[i], *plane[i][turn]) for i in range(2)])
        for i in range(2):
            terms[i] = [(a, start + mine[i] * size) for a, start in terms[i]] + [(came[i], 0)]
    n = lax.axis_size("gy")
    at = lax.axis_index("gy")
    size = size // n
    slot = lambda s: jnp.concatenate([total(i, ((at + s) % n) * size, size) for i in range(2)], axis=0)
    turn_by = lambda y, s: lax.ppermute(y, "gy", [(j, (j + s) % n) for j in range(n)])
    out = [slot(s).astype(BF) for s in range(1, n)]
    came = beside(out, [turn_by(y, s + 1) for s, y in enumerate(out)])
    final = slot(0)
    for y in came:
        final = final + y.astype(F32)
    mine = (final * scaling).astype(BF)
    came = beside([mine], [turn_by(mine, s) for s in range(1, n)])
    pieces = [jnp.concatenate([y[i * size : (i + 1) * size] for y in [mine] + came], axis=0) for i in range(2)]
    for turn in range(turns - 1, 0, -1):
        came = beside(pieces, [swap(pieces[i], *plane[i][turn]) for i in range(2)])
        pieces = [jnp.concatenate([pieces[i], came[i]], axis=0) for i in range(2)]
    odd = side("gz", 0)
    cross = lambda arrays: [swap(y, "gz", 0) for y in arrays]
    came = beside(pieces, [swap(pieces[i], *plane[i][0]) for i in range(2)])
    twins = cross(pieces)
    if size % 8 == 0:
        spots = jnp.stack(sides[0] + sides[1] + [at, odd]).astype(jnp.int32)
        half = place(spots, pieces + twins, size, turns, rows, 0, None)
        last = cross(came)
        return place(spots, came + last, size, turns, rows, 1, half)
    last = cross(came)

    def ordered(i, first, second):
        x = jnp.concatenate([first, second], axis=0).reshape((2,) * turns + (n, size, ch))
        for t in range(turns):
            x = jnp.where(sides[i][t] == 1, jnp.flip(x, t), x)
        x = jnp.take(x, (at - jnp.arange(n)) % n, axis=turns)
        return x.reshape(rows // 2, ch)

    mine = jnp.concatenate([ordered(i, pieces[i], came[i]) for i in range(2)], axis=0)
    other = jnp.concatenate([ordered(i, twins[i], last[i]) for i in range(2)], axis=0)
    low, high = jnp.where(odd == 1, other, mine), jnp.where(odd == 1, mine, other)
    return jnp.concatenate([low, high], axis=1)


def shards(features, weight, upstream, send_rows, in_rows, out_rows, tap_pair_exists):
    own_features = features[0, 0, 0]
    own, ch = own_features.shape
    single = lambda x: x[0, 0, 0][:, None, :]
    sends = single(send_rows)
    taps = weight.shape[0]
    block = 128
    ways = routes()
    flags = jnp.stack([side("gz", 0)] + [lax.axis_index(a) & 1 for a in AXES]).astype(jnp.int32)
    faces = exchange(send(ways, flags, sends, own_features), ways)
    col, row = invert(
        flags, single(in_rows), single(out_rows), single(tap_pair_exists), sends.shape[2], block
    )
    activated, gp, keep, *give = forward(ways, flags, col, own_features, faces, weight, upstream[0, 0, 0])
    devices = lax.axis_size("gx") * lax.axis_size("gy") * lax.axis_size("gz")
    split = (0, 3, 15, 18)
    state = {"turn": 0, "returned": {}, "grad": []}
    late = [j for j, way in enumerate(ways) if way in ((0, 0), (1, 2))]
    early = [j for j in range(len(ways)) if j not in late]

    def tied(out, work, came):
        held = lax.optimization_barrier((gp, *out))
        made = work(held[0])
        held = lax.optimization_barrier((*made, *came))
        return held[: len(made)], list(held[len(made) :])

    def beside(out, came):
        turn = state["turn"]
        state["turn"] = turn + 1
        if turn == 0:
            work = lambda g: backward_faces(ways, flags, row, g, weight, sends.shape[2])
            state["back"], came = tied(out, work, came)
        elif turn in (1, 2):
            picks = early if turn == 1 else late
            held = lax.optimization_barrier((*[state["back"][j] for j in picks], *out))
            got = exchange(held[: len(picks)], [ways[j] for j in picks])
            held = lax.optimization_barrier((*got, *came))
            for j, face in zip(picks, held):
                state["returned"][j] = face
            came = list(held[len(picks) :])
        if turn in (2, 3, 4):
            first, after = split[turn - 2 : turn]
            work = lambda g: [backward_own(row, g, weight, first, after - first, state["grad"])]
            made, came = tied(out, work, came)
            state["grad"] = [made[0]]
        if turn == 5:
            faces = [state["returned"][j] for j in range(len(ways))]
            first = split[-1]
            work = lambda g: [finish(ways, flags, sends, row, g, weight, first, taps - first, state["grad"][0], faces)]
            (state["done"],), came = tied(out, work, came)
        return came

    grad_weight = reduce_all(keep, give, float(devices * own) ** -0.5, beside).reshape(weight.shape)
    return activated[None, None, None], state["done"][None, None, None], grad_weight


def solution(mesh):
    part = P("gx", "gy", "gz", None, None)
    return jax.shard_map(
        shards,
        mesh=mesh,
        in_specs=(part, P(), part, part, part, part, part),
        out_specs=(part, part, P()),
        check_vma=False,
    )
```
